128 devices in a mesh: seq: 32 (over z, y, core), head: 4 (over x).
Axes of the slice: x: 4, y: 4, z: 4, core: 2. Of those that a mesh axis runs over, the one named last changes fastest.
Arguments:
- queries: bfloat16 [32768, 2048], P('seq', 'head'), may hold values from -100 to 100
- values: bfloat16 [32768, 2048], P('seq', 'head'), may hold values from -6 to 6
- codes: int32 [32768, 16], P('seq', 'head'), may hold values from 0 to 511
- codebook: bfloat16 [16, 512, 128], P('head'), may hold values from -4 to 4
- out_weight: bfloat16 [2048, 2048], P('head'), may hold values from -0.125 to 0.125
- grad_out: bfloat16 [32768, 2048], P('seq', 'head'), may hold values from -6 to 6
Outputs:
- grad_queries: bfloat16 [32768, 2048], P('seq', 'head')
- grad_values: bfloat16 [32768, 2048], P('seq', 'head')
- grad_codebook: float32 [16, 512, 128], P('head')
The draws below stay inside these ranges and needn't reach their ends.
All inputs are finite; a program needn't handle non-finite values.
Results may differ from the reference program's by a relative error of at most 0.012.
The reference program's roundings to bfloat16 on the way count: a program that leaves them out, or rounds other values in their place, can miss the bound.
Values may be sent and summed in bfloat16 or wider, within the bound.
No kernel may reach another device: no remote copies, remote signals or barrier semaphores. Data moves between devices by JAX's collectives and lax.ppermute only.
A program may use at most 192 MiB of HBM per device.

```python
import math
import jax
import jax.numpy as jnp
import numpy as np
from jax import lax

D = 2048
HEADS = 16
E = 128
S = 512
BLOCK = 512
TOKENS = 32768


def codeword_table(key):
    codewords = jnp.clip(jax.random.normal(jax.random.fold_in(key, 11), (HEADS, S, E), jnp.float32), -4.0, 4.0)
    return codewords


def draw_codebook(key, part):
    return codeword_table(key).astype(jnp.bfloat16)


def draw_queries(key, part):
    queries = jnp.clip(jax.random.normal(jax.random.fold_in(key, 21), (TOKENS, HEADS * E), jnp.float32), -6.0, 6.0)
    return queries.astype(jnp.bfloat16)


def set_ends(values, key, low, high):
    shape = values.shape
    index_at = [jax.random.randint(jax.random.fold_in(key, axis), (), 0, shape[axis]) for axis in range(len(shape))]
    values = values.at[tuple(index_at)].set(low)
    longest = shape.index(max(shape))
    index_at[longest] = (index_at[longest] + 1) % shape[longest]
    return values.at[tuple(index_at)].set(high)


def shard_levels(rng, extent, cuts, least, high):
    level = 1.0
    for axis_at, parts in cuts:
        steps = jax.random.uniform(jax.random.fold_in(jax.random.fold_in(rng, 6), axis_at), (parts,), jnp.float32, least / len(cuts), high / len(cuts))
        level = level * jnp.repeat(jnp.exp(steps), extent[axis_at] // parts).reshape((-1,) + (1,) * (len(extent) - 1 - axis_at))
    return level


def cumulative_ranks(number_of, lean):
    weights = [(1 << 20) // math.isqrt(rank ** lean) + 1 for rank in range(1, number_of + 1)]
    scale = 1 + sum(weights) // (1 << 30)
    return np.cumsum(np.array([max(1, weight // scale) for weight in weights]))


def skewed_ids(key, shape, amount, skew):
    grid = cumulative_ranks(amount, skew)
    ticket = jax.random.randint(jax.random.fold_in(key, 1), shape, 0, int(grid[amount - 1]))
    rank = jnp.searchsorted(jnp.asarray(grid, jnp.int32), ticket, side="right")
    return jax.random.permutation(jax.random.fold_in(key, 2), amount)[rank].astype(jnp.int32)


def scatter_about(key, extent, deviation, most, cuts=(), held_as=jnp.bfloat16):
    result = jax.random.normal(key, extent, jnp.float32) * deviation
    if len(cuts) > 0:
        result = shard_levels(key, extent, cuts, -0.22, 0.18) * result
    return jnp.clip(result, min=-most, max=most).astype(held_as)


def setup_inputs(seed: int = 0) -> dict:
    splits = jax.random.split(jax.random.key(seed), 7)
    queries = draw_queries(jax.random.fold_in(splits[6], 71), 0)
    values = scatter_about(splits[1], (TOKENS, HEADS * E), 1.0, 6.0, ((0, 32), (1, 4)))
    codes = set_ends(skewed_ids(splits[2], (TOKENS, HEADS), S, 2), jax.random.fold_in(splits[2], 3), 0, S - 1).astype(jnp.int32)
    codebook = draw_codebook(jax.random.fold_in(splits[6], 71), 0)
    out_weight = scatter_about(splits[4], (HEADS * E, D), D ** -0.5, 0.125, ((0, 4),))
    grad_out = scatter_about(splits[5], (TOKENS, D), 1.0, 6.0, ((0, 32), (1, 4)))
    return dict(queries=queries, values=values, codes=codes, codebook=codebook, out_weight=out_weight, grad_out=grad_out)


def lowered(array):
    return lax.optimization_barrier(array.astype(jnp.bfloat16)).astype(jnp.float32)


def product(form, left, right):
    return jnp.einsum(form, left.astype(jnp.float32), right.astype(jnp.float32))


def block_terms(query, value, block_codes, dout, codebook, prefix_values, prefix_counts):
    block_rows, heads_all, head_width = query.shape
    entries = codebook.shape[1]
    scale = head_width ** -0.5
    onehot = (block_codes[:, :, None] == jnp.arange(entries, dtype=jnp.int32)[None, None, :]).astype(jnp.float32)
    keys = lowered(product("ths,hse->the", onehot, codebook))
    scores = product("the,uhe->htu", query, keys) * scale
    positions = jnp.arange(block_rows, dtype=jnp.int32)
    causal = positions[:, None] >= positions[None, :]
    cache_scores = product("the,hce->htc", query, codebook) * scale
    counts_row = prefix_counts[:, None, :]
    present = counts_row > 0.0
    highest = jnp.maximum(jnp.max(jnp.where(causal, scores, -jnp.inf), axis=-1, keepdims=True),
                          jnp.max(jnp.where(present, cache_scores, -jnp.inf), axis=-1, keepdims=True))
    local_exp = jnp.where(causal, jnp.exp(jnp.where(causal, scores - highest, 0.0)), 0.0)
    cache_exp = jnp.where(present, jnp.exp(jnp.where(present, cache_scores - highest, 0.0)), 0.0)
    total = jnp.sum(local_exp, axis=-1, keepdims=True) + jnp.sum(cache_exp * counts_row, axis=-1, keepdims=True)
    local_prob = local_exp / total
    cache_prob = cache_exp / total
    local_low = lowered(local_prob)
    cache_low = lowered(cache_prob)
    cache_values = lowered(prefix_values)
    attended = product("htu,uhe->hte", local_low, value) + product("htc,hce->hte", cache_low, cache_values)
    delta = jnp.sum(jnp.transpose(dout.astype(jnp.float32), (1, 0, 2)) * attended, axis=-1)[..., None]
    local_grad = product("the,uhe->htu", dout, value)
    local_score_grad = lowered(local_prob * (local_grad - delta) * scale)
    cache_grad = product("the,hce->htc", dout, cache_values)
    cache_score_grad = lowered(cache_prob * (cache_grad - delta * counts_row) * scale)
    grad_query = (product("htu,uhe->the", local_score_grad, keys)
                  + product("htc,hce->the", cache_score_grad, codebook)).astype(jnp.bfloat16)
    key_grad = lowered(product("htu,the->uhe", local_score_grad, query))
    grad_code = product("ths,the->hse", onehot, key_grad) + product("htc,the->hce", cache_score_grad, query)
    value_part = product("htc,the->hce", cache_low, dout)
    local_values = product("htu,the->uhe", local_low, dout)
    own_values = product("ths,the->hse", onehot, value)
    own_counts = jnp.sum(onehot, axis=0)
    return grad_query, local_values, grad_code, value_part, own_values, own_counts


def reference(queries, values, codes, codebook, out_weight, grad_out):
    heads_all, entries, head_width = codebook.shape
    grad_heads = jnp.dot(grad_out, out_weight.T, preferred_element_type=jnp.float32).astype(jnp.bfloat16)
    nblocks = queries.shape[0] // BLOCK

    def stacked(array):
        return array.reshape(nblocks, BLOCK, heads_all, head_width)

    items = (stacked(queries), stacked(values), codes.reshape(nblocks, BLOCK, heads_all), stacked(grad_heads))

    def forward(carry, item):
        prefix_values, prefix_counts, code_sum = carry
        query, value, block_codes, dout = item
        grad_query, local_values, grad_code, value_part, own_values, own_counts = block_terms(
            query, value, block_codes, dout, codebook, prefix_values, prefix_counts)
        return (prefix_values + own_values, prefix_counts + own_counts, code_sum + grad_code), (grad_query, local_values, value_part)

    start_values = jnp.zeros((heads_all, entries, head_width), jnp.float32)
    start_counts = jnp.zeros((heads_all, entries), jnp.float32)
    (ignored_values, ignored_counts, grad_codebook), (grad_query, local_values, value_parts) = lax.scan(
        forward, (start_values, start_counts, start_values), items)

    def backward(later, item):
        block_codes, local_part, value_part = item
        onehot = (block_codes[:, :, None] == jnp.arange(entries, dtype=jnp.int32)[None, None, :]).astype(jnp.float32)
        lookup = jnp.einsum("ths,hse->the", onehot, lowered(later))
        return later + value_part, (local_part + lookup).astype(jnp.bfloat16)

    ignored_later, grad_value = lax.scan(backward, start_values,
                                         (codes.reshape(nblocks, BLOCK, heads_all), local_values, value_parts), reverse=True)
    return (grad_query.reshape(-1, heads_all * head_width), grad_value.reshape(-1, heads_all * head_width), grad_codebook)
```

```python
import functools
import math

import jax
import jax.numpy as jnp
from jax import lax
from jax.experimental import pallas as pl
from jax.experimental.pallas import tpu as pltpu
from jax.sharding import PartitionSpec as P

BLOCK = 512
TILE = 128
HALF = 64
ROWS = 80
F32 = jnp.float32
BF16 = jnp.bfloat16
VMEM_LIMIT = 56 << 20


def dot(left, right):
    return lax.dot_general(left, right, (((1,), (0,)), ((), ())), preferred_element_type=F32)


def dot_nt(left, right):
    return lax.dot_general(left, right, (((1,), (1,)), ((), ())), preferred_element_type=F32)


def params(count=1):
    return pltpu.CompilerParams(
        dimension_semantics=("arbitrary",) * count, vmem_limit_bytes=VMEM_LIMIT
    )


def onehot_rows(codes_row, start):
    shape = (TILE, codes_row.shape[1])
    entry = lax.broadcasted_iota(jnp.int32, shape, 0) + start
    return jnp.where(entry == codes_row, 1.0, 0.0).astype(BF16)


def own_kernel(codes_ref, value_ref, send_ref, first_ref):
    entries = first_ref.shape[1]
    ones = jnp.ones((BLOCK, TILE), BF16)
    count_rows = []
    for i in range(entries // TILE):
        total = None
        row_total = None
        for b in range(codes_ref.shape[2] // BLOCK):
            span = slice(b * BLOCK, (b + 1) * BLOCK)
            hot = onehot_rows(codes_ref[0, :, span], i * TILE)
            part = dot(hot, value_ref[span, :])
            if b == 0:
                first_ref[0, i * TILE : (i + 1) * TILE, :TILE] = part
                first_ref[0, i * TILE : (i + 1) * TILE, TILE:] = dot(hot, ones)
            row = dot_nt(jnp.ones((16, BLOCK), BF16), hot)
            total = part if total is None else total + part
            row_total = row if row_total is None else row_total + row
        high = jnp.floor(row_total * (1.0 / 256.0))
        low = row_total - high * 256.0
        place = lax.broadcasted_iota(jnp.int32, (16, TILE), 0)
        extra = jnp.where(place == 0, high, jnp.where(place == 1, low, 0.0)).astype(BF16)
        for k in range(2):
            send_ref[2 * i + k, :HALF, :] = total[k * HALF : (k + 1) * HALF].astype(BF16)
            send_ref[2 * i + k, HALF:, :] = extra


def own_sums(codes_rows, values, heads, entries):
    tokens = values.shape[0]
    slices = entries // HALF
    return pl.pallas_call(
        own_kernel,
        grid=(heads,),
        in_specs=[
            pl.BlockSpec((1, 1, tokens), lambda h: (h, 0, 0)),
            pl.BlockSpec((tokens, TILE), lambda h: (0, h)),
        ],
        out_specs=[
            pl.BlockSpec((slices, ROWS, TILE), lambda h: (h, 0, 0)),
            pl.BlockSpec((1, entries, 2 * TILE), lambda h: (h, 0, 0)),
        ],
        out_shape=[
            jax.ShapeDtypeStruct((heads * slices, ROWS, TILE), BF16),
            jax.ShapeDtypeStruct((heads, entries, 2 * TILE), F32),
        ],
        compiler_params=params(),
        name="own_sums",
    )(codes_rows, values)


def prefix_kernel(in_ref, out_ref):
    count = in_ref.shape[0]
    running = jnp.zeros((HALF, TILE), F32)
    number = jnp.zeros((1, TILE), F32)
    place = lax.broadcasted_iota(jnp.int32, (16, TILE), 0)
    for d in range(count):
        out_ref[d, :HALF, :] = running.astype(BF16)
        high = jnp.floor(number * (1.0 / 256.0))
        low = number - high * 256.0
        extra = jnp.where(place == 0, high, jnp.where(place == 1, low, 0.0))
        out_ref[d, HALF:, :] = extra.astype(BF16)
        running = running + in_ref[d, :HALF, :].astype(F32)
        rows = in_ref[d, HALF:, :].astype(F32)
        number = number + rows[0:1] * 256.0 + rows[1:2]


def prefix_scan(pieces):
    return pl.pallas_call(
        prefix_kernel,
        out_shape=jax.ShapeDtypeStruct(pieces.shape, BF16),
        compiler_params=pltpu.CompilerParams(vmem_limit_bytes=VMEM_LIMIT),
        name="prefix_scan",
    )(pieces)


def suffix_kernel(in_ref, out_ref):
    count = in_ref.shape[0]
    running = jnp.zeros((HALF, TILE), F32)
    total = jnp.zeros((HALF, TILE), F32)
    for d in reversed(range(count)):
        out_ref[d, :HALF, :] = running.astype(BF16)
        running = running + in_ref[d, :HALF, :].astype(F32)
        total = total + in_ref[d, HALF:, :].astype(F32)
    low = total.astype(BF16)
    for d in range(count):
        out_ref[d, HALF:, :] = low


def suffix_scan(pieces):
    return pl.pallas_call(
        suffix_kernel,
        out_shape=jax.ShapeDtypeStruct(pieces.shape, BF16),
        compiler_params=pltpu.CompilerParams(vmem_limit_bytes=VMEM_LIMIT),
        name="suffix_scan",
    )(pieces)


def fold(array):
    rows, lanes = array.shape
    return jnp.sum(array.reshape(rows // 8, 8, lanes), axis=0)


def fold_max(array):
    rows, lanes = array.shape
    return jnp.max(array.reshape(rows // 8, 8, lanes), axis=0)


def attend_kernel(block, refs):
    if block == 0:
        (codes_ref, query_ref, value_ref, cotangent_ref, weight_ref, book_ref, book_t_ref,
         prefix_ref, grad_query_ref, local_ref, part_ref, code_ref,
         hot, dout, rows_k, rows_v, counts, scores, grads, score_grad, key_grad) = refs
    else:
        (codes_ref, query_ref, value_ref, cotangent_ref, weight_ref, book_ref, book_t_ref,
         prefix_ref, first_ref, part0_ref, code0_ref, _, _,
         grad_query_ref, local_ref, part_ref, send_ref,
         hot, dout, rows_k, rows_v, counts, scores, grads, score_grad, key_grad) = refs
    head = pl.program_id(0)
    entries, width = book_ref.shape[1:]
    tiles = BLOCK // TILE
    entry_tiles = entries // TILE
    scale = width ** -0.5
    factor = scale * math.log2(math.e)

    @pl.when(head == 0)
    def _():
        score_grad[...] = jnp.zeros_like(score_grad)
        for part in range(2):
            rows = slice(part * 256, (part + 1) * 256)
            total = None
            for k in range(cotangent_ref.shape[0]):
                columns = slice(k * BLOCK, (k + 1) * BLOCK)
                term = dot_nt(cotangent_ref[k, rows, :], weight_ref[:, columns])
                total = term if total is None else total + term
            for h in range(dout.shape[0]):
                dout[h, rows, :] = total[:, h * TILE : (h + 1) * TILE].astype(BF16)

    codes_row = codes_ref[0]
    for i in range(entry_tiles):
        hot[i * TILE : (i + 1) * TILE, :] = onehot_rows(codes_row, i * TILE)
    keys_t = dot(book_t_ref[0], hot[...])
    rows_k[:BLOCK, :] = keys_t.T.astype(BF16)
    keys_t = keys_t.astype(BF16)
    rows_k[BLOCK:, :] = book_ref[0]
    rows_v[:BLOCK, :] = value_ref[...]
    diagonal = lax.broadcasted_iota(jnp.int32, (TILE, TILE), 0) == lax.broadcasted_iota(
        jnp.int32, (TILE, TILE), 1
    )
    ones = jnp.ones((TILE, TILE), BF16)
    for i in range(entry_tiles):
        rows = slice(i * TILE, (i + 1) * TILE)
        line = prefix_ref[2 * i, HALF:, :].astype(F32)
        high = jnp.where(diagonal, line[0:1] * 256.0, 0.0).astype(BF16)
        low = jnp.where(diagonal, line[1:2], 0.0).astype(BF16)
        number = dot(high, ones) + dot(low, ones)
        for k in range(2):
            at = i * TILE + k * HALF
            sums = prefix_ref[2 * i + k, :HALF, :]
            if block > 0:
                sums = (sums.astype(F32) + first_ref[0, at : at + HALF, :TILE]).astype(BF16)
            rows_v[BLOCK + at : BLOCK + at + HALF, :] = sums
        if block > 0:
            number = number + first_ref[0, rows, TILE:]
        counts[rows, :] = number

    causal = lax.broadcasted_iota(jnp.int32, (TILE, TILE), 1) >= lax.broadcasted_iota(
        jnp.int32, (TILE, TILE), 0
    )
    top = [jnp.full((8, TILE), -jnp.inf, F32) for _ in range(tiles)]
    for i in range(tiles + entry_tiles):
        local = i < tiles
        start = i if local else 0
        rows = slice(i * TILE, (i + 1) * TILE)
        score = dot_nt(rows_k[rows, :], query_ref[start * TILE :, :])
        if not local:
            present = counts[(i - tiles) * TILE : (i - tiles + 1) * TILE, :] > 0.0
        for j in range(start, tiles):
            piece = score[:, (j - start) * TILE : (j - start + 1) * TILE]
            if local:
                if j == i:
                    piece = jnp.where(causal, piece, -jnp.inf)
            else:
                piece = jnp.where(present, piece, -jnp.inf)
            top[j] = jnp.maximum(top[j], fold_max(piece))
            scores[rows, j * TILE : (j + 1) * TILE] = piece
    top = [jnp.max(t, axis=0, keepdims=True) for t in top]
    total = [jnp.zeros((8, TILE), F32) for _ in range(tiles)]
    for i in range(tiles + entry_tiles):
        local = i < tiles
        rows = slice(i * TILE, (i + 1) * TILE)
        for j in range(i if local else 0, tiles):
            columns = slice(j * TILE, (j + 1) * TILE)
            piece = jnp.exp2((scores[rows, columns] - top[j]) * factor)
            scores[rows, columns] = piece
            if not local:
                piece = piece * counts[(i - tiles) * TILE : (i - tiles + 1) * TILE, :]
            total[j] = total[j] + fold(piece)
    inverse = [1.0 / jnp.sum(t, axis=0, keepdims=True) for t in total]
    mine = dout[head]
    delta = [jnp.zeros((8, TILE), F32) for _ in range(tiles)]
    for i in range(tiles + entry_tiles):
        local = i < tiles
        start = i if local else 0
        rows = slice(i * TILE, (i + 1) * TILE)
        grad = dot_nt(rows_v[rows, :], mine[start * TILE :, :])
        pieces = []
        for j in range(start, tiles):
            columns = slice(j * TILE, (j + 1) * TILE)
            low = (scores[rows, columns] * inverse[j]).astype(BF16)
            pieces.append(low)
            piece = grad[:, (j - start) * TILE : (j - start + 1) * TILE]
            grads[rows, columns] = piece
            delta[j] = delta[j] + fold(low.astype(F32) * piece)
        low = pieces[0] if len(pieces) == 1 else jnp.concatenate(pieces, axis=1)
        result = dot(low, mine[start * TILE :, :])
        if local:
            local_ref[rows, :] = result
        else:
            part_ref[0, (i - tiles) * TILE : (i - tiles + 1) * TILE, :] = result
    delta = [jnp.sum(t, axis=0, keepdims=True) for t in delta]
    inverse = [t * scale for t in inverse]
    code = []
    for i in range(tiles + entry_tiles):
        local = i < tiles
        start = i if local else 0
        rows = slice(i * TILE, (i + 1) * TILE)
        pieces = []
        for j in range(start, tiles):
            columns = slice(j * TILE, (j + 1) * TILE)
            shift = delta[j]
            if not local:
                shift = shift * counts[(i - tiles) * TILE : (i - tiles + 1) * TILE, :]
            piece = scores[rows, columns] * ((grads[rows, columns] - shift) * inverse[j])
            piece = piece.astype(BF16)
            pieces.append(piece)
            score_grad[rows, columns] = piece
        low = pieces[0] if len(pieces) == 1 else jnp.concatenate(pieces, axis=1)
        result = dot(low, query_ref[start * TILE :, :])
        if local:
            key_grad[rows, :] = result.astype(BF16)
        else:
            code.append(result)
    grad_t = dot(keys_t, score_grad[:BLOCK, :]) + dot(book_t_ref[0], score_grad[BLOCK:, :])
    grad_query_ref[...] = grad_t.T.astype(BF16)
    for i in range(entry_tiles):
        rows = slice(i * TILE, (i + 1) * TILE)
        result = code[i] + dot(hot[rows, :], key_grad[...])
        if block == 0:
            code_ref[0, rows, :] = result
        else:
            result = result + code0_ref[0, rows, :]
            parts = part_ref[0, rows, :] + part0_ref[0, rows, :]
            for k in range(2):
                half = slice(k * HALF, (k + 1) * HALF)
                send_ref[2 * i + k, :HALF, :] = parts[half].astype(BF16)
                send_ref[2 * i + k, HALF:, :] = result[half].astype(BF16)


def attend(block, codes_rows, queries, values, cotangent, weight, book, book_t, prefix, extra=None):
    heads, entries, width = book.shape
    tokens = queries.shape[0]
    slices = entries // HALF
    rows_of = lambda h: (block, h)
    whole3 = lambda h: (0, 0, 0)
    by_head = lambda h: (h, 0, 0)
    in_specs = [
        pl.BlockSpec((1, 1, BLOCK), lambda h: (h, 0, block)),
        pl.BlockSpec((BLOCK, width), rows_of),
        pl.BlockSpec((BLOCK, width), rows_of),
        pl.BlockSpec(cotangent.shape, whole3),
        pl.BlockSpec(weight.shape, lambda h: (0, 0)),
        pl.BlockSpec((1, entries, width), by_head),
        pl.BlockSpec((1, width, entries), by_head),
        pl.BlockSpec((slices, ROWS, TILE), by_head),
    ]
    args = [codes_rows, queries, values, cotangent, weight, book, book_t, prefix]
    per_head = pl.BlockSpec((1, entries, width), by_head)
    out_specs = [pl.BlockSpec((BLOCK, width), rows_of), pl.BlockSpec((BLOCK, width), rows_of), per_head]
    out_shape = [
        jax.ShapeDtypeStruct((tokens, heads * width), BF16),
        jax.ShapeDtypeStruct((tokens, heads * width), F32),
        jax.ShapeDtypeStruct(book.shape, F32),
    ]
    aliases = {}
    if block == 0:
        out_specs.append(per_head)
        out_shape.append(jax.ShapeDtypeStruct(book.shape, F32))
    else:
        first, part0, code0, grad_query, local = extra
        args += [first, part0, code0, grad_query, local]
        in_specs += [
            pl.BlockSpec((1, entries, 2 * width), by_head),
            per_head,
            per_head,
            pl.BlockSpec(memory_space=pl.ANY),
            pl.BlockSpec(memory_space=pl.ANY),
        ]
        aliases = {11: 0, 12: 1}
        out_specs.append(pl.BlockSpec((slices, 2 * HALF, TILE), by_head))
        out_shape.append(jax.ShapeDtypeStruct((heads * slices, 2 * HALF, TILE), BF16))
    both = BLOCK + entries
    return pl.pallas_call(
        lambda *refs: attend_kernel(block, refs),
        grid=(heads,),
        in_specs=in_specs,
        out_specs=out_specs,
        out_shape=out_shape,
        scratch_shapes=[
            pltpu.VMEM((entries, BLOCK), BF16),
            pltpu.VMEM((heads, BLOCK, width), BF16),
            pltpu.VMEM((both, width), BF16),
            pltpu.VMEM((both, width), BF16),
            pltpu.VMEM((entries, TILE), F32),
            pltpu.VMEM((both, BLOCK), F32),
            pltpu.VMEM((both, BLOCK), F32),
            pltpu.VMEM((both, BLOCK), BF16),
            pltpu.VMEM((BLOCK, width), BF16),
        ],
        input_output_aliases=aliases,
        compiler_params=params(),
        name=f"attend_block_{block}",
    )(*args)


def finish_kernel(codes_ref, local_ref, later_ref, part_ref, out_ref, book_ref):
    heads, entries, width = part_ref.shape
    slices = entries // HALF
    first = pl.program_id(0) == 0
    levels = lax.broadcasted_iota(jnp.int32, (BLOCK, entries), 1)
    for h in range(heads):
        pieces = later_ref[h * slices : (h + 1) * slices]
        later = pieces[:, :HALF, :].reshape(entries, width)
        total = (later.astype(F32) + jnp.where(first, part_ref[h], 0.0)).astype(BF16)
        hot = jnp.where(levels == codes_ref[:, h : h + 1], 1.0, 0.0).astype(BF16)
        columns = slice(h * width, (h + 1) * width)
        out_ref[:, columns] = (local_ref[:, columns] + dot(hot, total)).astype(BF16)
        book_ref[h] = pieces[:, HALF:, :].reshape(entries, width).astype(F32)


def finish(codes, local, later, part):
    heads, entries, width = part.shape
    tokens = local.shape[0]
    return pl.pallas_call(
        finish_kernel,
        grid=(tokens // BLOCK,),
        in_specs=[
            pl.BlockSpec((BLOCK, heads), lambda b: (b, 0)),
            pl.BlockSpec((BLOCK, heads * width), lambda b: (b, 0)),
            pl.BlockSpec(later.shape, lambda b: (0, 0, 0)),
            pl.BlockSpec(part.shape, lambda b: (0, 0, 0)),
        ],
        out_specs=[
            pl.BlockSpec((BLOCK, heads * width), lambda b: (b, 0)),
            pl.BlockSpec(part.shape, lambda b: (0, 0, 0)),
        ],
        out_shape=[
            jax.ShapeDtypeStruct(local.shape, BF16),
            jax.ShapeDtypeStruct(part.shape, F32),
        ],
        compiler_params=params(),
        name="finish_values",
    )(codes, local, later, part)


def per_device(queries, values, codes, codebook, out_weight, grad_out):
    heads, entries, width = codebook.shape
    exchange = functools.partial(
        lax.all_to_all, axis_name="seq", split_axis=0, concat_axis=0, tiled=True
    )
    gathered = [
        lax.all_gather(grad_out[b * BLOCK : (b + 1) * BLOCK], "head") for b in range(2)
    ]
    codes_rows = codes.T.reshape(heads, 1, -1)
    book_t = jnp.swapaxes(codebook, 1, 2)
    send, first = own_sums(codes_rows, values, heads, entries)
    prefix = exchange(prefix_scan(exchange(send)))
    common = (codes_rows, queries, values)
    grad_query, local, part0, code0 = attend(
        0, *common, gathered[0], out_weight, codebook, book_t, prefix
    )
    grad_query, local, part1, send = attend(
        1, *common, gathered[1], out_weight, codebook, book_t, prefix,
        (first, part0, code0, grad_query, local),
    )
    later = exchange(suffix_scan(exchange(send)))
    grad_values, grad_book = finish(codes, local, later, part1)
    return grad_query, grad_values, grad_book


def solution(mesh):
    rows = P("seq", "head")
    return jax.shard_map(
        per_device,
        mesh=mesh,
        in_specs=(rows, rows, rows, P("head", None, None), P("head", None), rows),
        out_specs=(rows, rows, P("head", None, None)),
        check_vma=False,
    )
```

```python
import functools
import math

import jax
import jax.numpy as jnp
from jax import lax
from jax.experimental import pallas as pl
from jax.experimental.pallas import tpu as pltpu
from jax.sharding import PartitionSpec as P

BLOCK = 512
PART = 256
TILE = 128
HALF = 64
F32 = jnp.float32
BF16 = jnp.bfloat16
VMEM_LIMIT = 48 << 20
ANY = pl.BlockSpec(memory_space=pl.ANY)


def dot(left, right):
    return lax.dot_general(left, right, (((1,), (0,)), ((), ())), preferred_element_type=F32)


def dot_nt(left, right):
    return lax.dot_general(left, right, (((1,), (1,)), ((), ())), preferred_element_type=F32)


def call(kernel, name, grid, in_specs, outs, scratch=(), aliases=None, prefetch=0, flops=0, size=0):
    return pl.pallas_call(
        kernel,
        grid_spec=pltpu.PrefetchScalarGridSpec(
            num_scalar_prefetch=prefetch,
            grid=grid,
            in_specs=in_specs,
            out_specs=[spec for _, _, spec in outs],
            scratch_shapes=list(scratch),
        ),
        out_shape=[jax.ShapeDtypeStruct(shape, dtype) for shape, dtype, _ in outs],
        input_output_aliases=aliases or {},
        compiler_params=pltpu.CompilerParams(
            dimension_semantics=("arbitrary",) * len(grid), vmem_limit_bytes=VMEM_LIMIT
        ),
        cost_estimate=pl.CostEstimate(flops=flops, bytes_accessed=size, transcendentals=0),
        name=name,
    )


def onehot_rows(codes_row, entries):
    entry = lax.broadcasted_iota(jnp.int32, (entries, codes_row.shape[1]), 0)
    return jnp.where(entry == codes_row, 1.0, 0.0).astype(BF16)


def fold(array):
    rows, lanes = array.shape
    return jnp.sum(array.reshape(rows // 8, 8, lanes), axis=0)


def fold_max(array):
    rows, lanes = array.shape
    return jnp.max(array.reshape(rows // 8, 8, lanes), axis=0)


def count_kernel(codes_ref, total_ref, first_ref):
    heads, entries = total_ref.shape[0], total_ref.shape[2]
    levels = lax.broadcasted_iota(jnp.int32, (BLOCK, entries), 1)
    for h in range(heads):
        total = None
        for b in range(codes_ref.shape[0] // BLOCK):
            column = codes_ref[b * BLOCK : (b + 1) * BLOCK, h : h + 1]
            part = jnp.sum(fold(jnp.where(levels == column, 1.0, 0.0)), axis=0, keepdims=True)
            if b == 0:
                first_ref[h] = part
            total = part if total is None else total + part
        total_ref[h] = total


def own_counts(codes, entries):
    tokens, heads = codes.shape
    shape = (heads, 1, entries)
    spec = pl.BlockSpec(shape, lambda i: (0, 0, 0))
    return call(
        count_kernel, "own_counts", (1,),
        [pl.BlockSpec(codes.shape, lambda i: (0, 0))],
        [(shape, F32, spec), (shape, F32, spec)],
        size=1 << 20,
    )(codes)


def sum_kernel(codes_ref, value_ref, send_ref, first_ref):
    entries = first_ref.shape[1]
    total = None
    for b in range(codes_ref.shape[2] // BLOCK):
        span = slice(b * BLOCK, (b + 1) * BLOCK)
        part = dot(onehot_rows(codes_ref[0, :, span], entries), value_ref[span, :])
        if b == 0:
            first_ref[0] = part
        total = part if total is None else total + part
    for k in range(entries // HALF):
        send_ref[k] = total[k * HALF : (k + 1) * HALF].astype(BF16)


def own_sums(codes_rows, values, heads, entries):
    tokens = values.shape[0]
    slices = entries // HALF
    by_head = lambda h: (h, 0, 0)
    return call(
        sum_kernel, "own_sums", (heads,),
        [
            pl.BlockSpec((1, 1, tokens), by_head),
            pl.BlockSpec((tokens, TILE), lambda h: (0, h)),
        ],
        [
            ((heads * slices, HALF, TILE), BF16, pl.BlockSpec((slices, HALF, TILE), by_head)),
            ((heads, entries, TILE), F32, pl.BlockSpec((1, entries, TILE), by_head)),
        ],
        flops=1 << 30, size=4 << 20,
    )(codes_rows, values)


def prefix_kernel(in_ref, out_ref):
    running = jnp.zeros(in_ref.shape[1:], F32)
    for d in range(in_ref.shape[0]):
        out_ref[d] = running.astype(BF16)
        running = running + in_ref[d].astype(F32)


def suffix_kernel(in_ref, out_ref):
    running = jnp.zeros(in_ref.shape[1:], F32)
    for d in reversed(range(in_ref.shape[0])):
        out_ref[d] = running.astype(BF16)
        running = running + in_ref[d].astype(F32)


def total_kernel(in_ref, out_ref):
    running = jnp.zeros(in_ref.shape[1:], F32)
    for d in range(in_ref.shape[0]):
        running = running + in_ref[d].astype(F32)
    low = running.astype(BF16)
    for d in range(in_ref.shape[0]):
        out_ref[d] = low


def scanned(kernel, name, pieces):
    spec = pl.BlockSpec(pieces.shape, lambda i: (0, 0, 0))
    return call(
        kernel, name, (1,), [spec], [(pieces.shape, BF16, spec)], size=1 << 20
    )(pieces)[0]


def forward_kernel(block, me_ref, codes_ref, query_ref, book_ref, book_t_ref, all_ref, first_ref,
                   low_ref, keys_ref, rows_k, counts, scores):
    entries, width = book_ref.shape[1:]
    entry_tiles = entries // TILE
    factor = width ** -0.5 * math.log2(math.e)
    keys_t = dot(book_t_ref[0], onehot_rows(codes_ref[0], entries))
    keys_ref[0] = keys_t.astype(BF16)
    rows_k[:entries, :] = book_ref[0]
    rows_k[entries:, :] = keys_t.T.astype(BF16)
    number = jnp.zeros((1, entries), F32)
    for d in range(all_ref.shape[0]):
        number = number + jnp.where(d < me_ref[0], all_ref[d, 0], 0.0)
    if block > 0:
        number = number + first_ref[0]
    for i in range(entry_tiles):
        rows = slice(i * TILE, (i + 1) * TILE)
        counts[rows, :] = jnp.broadcast_to(number[:, rows], (TILE, TILE)).T
    causal = lax.broadcasted_iota(jnp.int32, (TILE, TILE), 1) >= lax.broadcasted_iota(
        jnp.int32, (TILE, TILE), 0
    )
    for n in range(BLOCK // PART):
        used = entries + PART * (n + 1)
        span = slice(n * PART, (n + 1) * PART)
        scores[n, :used, :] = dot_nt(rows_k[:used, :], query_ref[span, :])
    for n in range(BLOCK // PART):
        used = entries + PART * (n + 1)
        for j in range(PART // TILE):
            columns = slice(j * TILE, (j + 1) * TILE)
            target = slice(n * PART + j * TILE, n * PART + (j + 1) * TILE)
            pieces = range(entry_tiles + 2 * n + j + 1)
            top = jnp.full((8, TILE), -jnp.inf, F32)
            for i in pieces:
                rows = slice(i * TILE, (i + 1) * TILE)
                piece = scores[n, rows, columns]
                if i < entry_tiles:
                    piece = jnp.where(counts[rows, :] > 0.0, piece, -jnp.inf)
                    scores[n, rows, columns] = piece
                elif i == pieces[-1]:
                    piece = jnp.where(causal, piece, -jnp.inf)
                    scores[n, rows, columns] = piece
                top = jnp.maximum(top, fold_max(piece))
            top = jnp.max(top, axis=0, keepdims=True)
            total = jnp.zeros((8, TILE), F32)
            for i in pieces:
                rows = slice(i * TILE, (i + 1) * TILE)
                piece = jnp.exp2((scores[n, rows, columns] - top) * factor)
                scores[n, rows, columns] = piece
                if i < entry_tiles:
                    piece = piece * counts[rows, :]
                total = total + fold(piece)
            inverse = 1.0 / jnp.sum(total, axis=0, keepdims=True)
            for i in pieces:
                rows = slice(i * TILE, (i + 1) * TILE)
                low_ref[0, rows, target] = (scores[n, rows, columns] * inverse).astype(BF16)
            if j == 0:
                low_ref[0, used - TILE : used, target] = jnp.zeros((TILE, TILE), BF16)


def forward(block, me, codes_rows, queries, book, book_t, every, first):
    heads, entries, width = book.shape
    both = entries + BLOCK
    by_head = lambda h, *_: (h, 0, 0)
    row = pl.BlockSpec((1, 1, entries), by_head)
    return call(
        functools.partial(forward_kernel, block), f"forward_{block}", (heads,),
        [
            pl.BlockSpec((1, 1, BLOCK), lambda h, *_: (h, 0, block)),
            pl.BlockSpec((BLOCK, width), lambda h, *_: (block, h)),
            pl.BlockSpec((1, entries, width), by_head),
            pl.BlockSpec((1, width, entries), by_head),
            pl.BlockSpec((every.shape[0], 1, 1, entries), lambda h, *_: (0, h, 0, 0)),
            row,
        ],
        [
            ((heads, both, BLOCK), BF16, pl.BlockSpec((1, both, BLOCK), by_head)),
            ((heads, width, BLOCK), BF16, pl.BlockSpec((1, width, BLOCK), by_head)),
        ],
        [
            pltpu.VMEM((both, width), BF16),
            pltpu.VMEM((entries, TILE), F32),
            pltpu.VMEM((2, both, PART), F32),
        ],
        prefetch=1, flops=3 << 30, size=8 << 20,
    )(me, codes_rows, queries, book, book_t, every, first)


def values_kernel(block, *refs):
    (_, own_ref, left_ref, right_ref, low_half_ref, high_half_ref,
     own_w, left_w, right_w, far_w, probs_ref) = refs[:11]
    if block == 0:
        dout_ref, local_ref, part_ref, dout = refs[11:]
    else:
        part0_ref, _, dout_ref, local_ref, part_ref, send_ref, dout = refs[11:]
    head = pl.program_id(0)
    entries, width = part_ref.shape[1:]

    @pl.when(head == 0)
    def _():
        for n in range(BLOCK // PART):
            span = slice(n * PART, (n + 1) * PART)
            far = low_half_ref[...] if n == 0 else high_half_ref[...]
            total = dot_nt(own_ref[span, :], own_w[...]) + dot_nt(left_ref[span, :], left_w[...])
            total = total + dot_nt(right_ref[span, :], right_w[...]) + dot_nt(far, far_w[...])
            for h in range(dout.shape[0]):
                dout[h, span, :] = total[:, h * width : (h + 1) * width].astype(BF16)

    mine = dout[head]
    dout_ref[0] = mine
    used = entries + PART
    low = dot(probs_ref[0, :used, :PART], mine[:PART])
    high = dot(probs_ref[0, :, PART:], mine[PART:])
    local_ref[:PART, :] = low[entries:] + high[entries:used]
    local_ref[PART:, :] = high[used:]
    part = low[:entries] + high[:entries]
    part_ref[0] = part
    if block > 0:
        part = part + part0_ref[0]
        for k in range(entries // HALF):
            send_ref[k] = part[k * HALF : (k + 1) * HALF].astype(BF16)


def value_grads(block, me, pieces, weight, probs, extra=()):
    heads, both, _ = probs.shape
    entries = both - BLOCK
    width = weight.shape[0] // heads
    columns = weight.shape[1] // 4
    tokens = 2 * BLOCK
    slices = entries // HALF
    by_head = lambda h, *_: (h, 0, 0)
    per_head = pl.BlockSpec((1, entries, width), by_head)
    full = lambda h, *_: (0, 0)

    def chunk(offset):
        return pl.BlockSpec(
            (weight.shape[0], columns), lambda h, me: (0, lax.rem(me[0] + offset, 4))
        )

    in_specs = [pl.BlockSpec((BLOCK, columns), lambda h, *_: (block, 0))]
    in_specs += [pl.BlockSpec(piece.shape, full) for piece in pieces[1:]]
    in_specs += [chunk(0), chunk(3), chunk(1), chunk(2), pl.BlockSpec((1, both, BLOCK), by_head)]
    outs = [
        ((heads, BLOCK, width), BF16, pl.BlockSpec((1, BLOCK, width), by_head)),
        ((tokens, heads * width), F32, pl.BlockSpec((BLOCK, width), lambda h, *_: (block, h))),
        ((heads, entries, width), F32, per_head),
    ]
    aliases = {}
    if block > 0:
        in_specs += [per_head, ANY]
        aliases = {12: 1}
        outs.append(
            ((heads * slices, HALF, width), BF16, pl.BlockSpec((slices, HALF, width), by_head))
        )
    return call(
        functools.partial(values_kernel, block), f"value_grads_{block}", (heads,), in_specs, outs,
        [pltpu.VMEM((heads, BLOCK, width), BF16)],
        aliases=aliases, prefetch=1, flops=3 << 30, size=12 << 20,
    )(me, *pieces, *[weight] * 4, probs, *extra)


def scores_kernel(block, me_ref, *refs):
    (codes_ref, query_ref, value_ref, dout_ref, probs_ref, keys_ref, book_t_ref, prefix_ref,
     all_ref) = refs[:9]
    if block == 0:
        (grad_query_ref, code_ref, hot, rows_v, counts, grads, score_grad, key_grad,
         wide_t) = refs[9:]
    else:
        (first_ref, first_count_ref, code0_ref, _, grad_query_ref, send_ref,
         hot, rows_v, counts, grads, score_grad, key_grad, wide_t) = refs[9:]
    width, entries = book_t_ref.shape[1:]
    entry_tiles = entries // TILE
    scale = width ** -0.5
    hot[...] = onehot_rows(codes_ref[0], entries)
    wide_t[:, :entries] = book_t_ref[0]
    wide_t[:, entries:] = keys_ref[0]
    sums = prefix_ref[...].reshape(entries, width)
    if block > 0:
        sums = (sums.astype(F32) + first_ref[0]).astype(BF16)
    rows_v[:entries, :] = sums
    rows_v[entries:, :] = value_ref[...]
    number = jnp.zeros((1, entries), F32)
    for d in range(all_ref.shape[0]):
        number = number + jnp.where(d < me_ref[0], all_ref[d, 0], 0.0)
    if block > 0:
        number = number + first_count_ref[0]
    for i in range(entry_tiles):
        rows = slice(i * TILE, (i + 1) * TILE)
        counts[rows, :] = jnp.broadcast_to(number[:, rows], (TILE, TILE)).T
    for n in range(BLOCK // PART):
        used = entries + PART * (n + 1)
        span = slice(n * PART, (n + 1) * PART)
        grads[n, :used, :] = dot_nt(rows_v[:used, :], dout_ref[0, span, :])
    sums_k = None
    for n in range(BLOCK // PART):
        used = entries + PART * (n + 1)
        span = slice(n * PART, (n + 1) * PART)
        for j in range(PART // TILE):
            columns = slice(j * TILE, (j + 1) * TILE)
            source = slice(n * PART + j * TILE, n * PART + (j + 1) * TILE)
            pieces = range(entry_tiles + 2 * n + j + 1)
            delta = jnp.zeros((8, TILE), F32)
            for i in pieces:
                rows = slice(i * TILE, (i + 1) * TILE)
                delta = delta + fold(
                    probs_ref[0, rows, source].astype(F32) * grads[n, rows, columns]
                )
            delta = jnp.sum(delta, axis=0, keepdims=True) * scale
            for i in pieces:
                rows = slice(i * TILE, (i + 1) * TILE)
                shift = delta
                if i < entry_tiles:
                    shift = delta * counts[rows, :]
                piece = grads[n, rows, columns] * scale - shift
                piece = probs_ref[0, rows, source].astype(F32) * piece
                score_grad[n, rows, columns] = piece.astype(BF16)
            if j == 0:
                score_grad[n, used - TILE : used, columns] = jnp.zeros((TILE, TILE), BF16)
        result = dot(score_grad[n, :used, :], query_ref[span, :])
        grad_t = dot(wide_t[:, :used], score_grad[n, :used, :])
        grad_query_ref[span, :] = grad_t.T.astype(BF16)
        if n == 0:
            sums_k = result
        else:
            middle = entries + PART
            key_grad[:PART, :] = (sums_k[entries:] + result[entries:middle]).astype(BF16)
            key_grad[PART:, :] = result[middle:].astype(BF16)
            code = sums_k[:entries] + result[:entries]
    code = code + dot(hot[...], key_grad[...])
    if block == 0:
        code_ref[0] = code
    else:
        code = code + code0_ref[0]
        for k in range(entries // HALF):
            send_ref[k] = code[k * HALF : (k + 1) * HALF].astype(BF16)


def score_grads(block, me, codes_rows, queries, values, dout, probs, keys_t, book_t, prefix, every,
                extra=()):
    heads, width, entries = book_t.shape
    both = entries + BLOCK
    slices = entries // HALF
    by_head = lambda h, *_: (h, 0, 0)
    rows_of = lambda h, *_: (block, h)
    row = pl.BlockSpec((1, 1, entries), by_head)
    per_head = pl.BlockSpec((1, entries, width), by_head)
    in_specs = [
        pl.BlockSpec((1, 1, BLOCK), lambda h, *_: (h, 0, block)),
        pl.BlockSpec((BLOCK, width), rows_of),
        pl.BlockSpec((BLOCK, width), rows_of),
        pl.BlockSpec((1, BLOCK, width), by_head),
        pl.BlockSpec((1, both, BLOCK), by_head),
        pl.BlockSpec((1, width, BLOCK), by_head),
        pl.BlockSpec((1, width, entries), by_head),
        pl.BlockSpec((slices, HALF, width), by_head),
        pl.BlockSpec((every.shape[0], 1, 1, entries), lambda h, *_: (0, h, 0, 0)),
    ]
    outs = [(queries.shape, BF16, pl.BlockSpec((BLOCK, width), rows_of))]
    aliases = {}
    if block == 0:
        outs.append(((heads, entries, width), F32, per_head))
    else:
        in_specs += [per_head, row, per_head, ANY]
        aliases = {13: 0}
        outs.append(
            ((heads * slices, HALF, width), BF16, pl.BlockSpec((slices, HALF, width), by_head))
        )
    return call(
        functools.partial(scores_kernel, block), f"score_grads_{block}", (heads,), in_specs, outs,
        [
            pltpu.VMEM((entries, BLOCK), BF16),
            pltpu.VMEM((both, width), BF16),
            pltpu.VMEM((entries, TILE), F32),
            pltpu.VMEM((2, both, PART), F32),
            pltpu.VMEM((2, both, PART), BF16),
            pltpu.VMEM((BLOCK, width), BF16),
            pltpu.VMEM((width, both), BF16),
        ],
        aliases=aliases, prefetch=1, flops=5 << 30, size=12 << 20,
    )(me, codes_rows, queries, values, dout, probs, keys_t, book_t, prefix, every, *extra)


def finish_kernel(codes_ref, local_ref, later_ref, part_ref, out_ref):
    heads, entries, width = part_ref.shape
    slices = entries // HALF
    first = pl.program_id(0) == 0
    levels = lax.broadcasted_iota(jnp.int32, (BLOCK, entries), 1)
    for h in range(heads):
        later = later_ref[h * slices : (h + 1) * slices].reshape(entries, width)
        total = (later.astype(F32) + jnp.where(first, part_ref[h], 0.0)).astype(BF16)
        hot = jnp.where(levels == codes_ref[:, h : h + 1], 1.0, 0.0).astype(BF16)
        columns = slice(h * width, (h + 1) * width)
        out_ref[:, columns] = (local_ref[:, columns] + dot(hot, total)).astype(BF16)


def finish(codes, local, later, part):
    heads, entries, width = part.shape
    whole = lambda b: (0, 0, 0)
    rows = pl.BlockSpec((BLOCK, heads * width), lambda b: (b, 0))
    return call(
        finish_kernel, "finish_values", (local.shape[0] // BLOCK,),
        [
            pl.BlockSpec((BLOCK, heads), lambda b: (b, 0)),
            rows,
            pl.BlockSpec(later.shape, whole),
            pl.BlockSpec(part.shape, whole),
        ],
        [(local.shape, BF16, rows)],
        flops=1 << 30, size=4 << 20,
    )(codes, local, later, part)[0]


def ring_pieces(array):
    count = lax.axis_size("head")
    up = [(i, (i + 1) % count) for i in range(count)]
    down = [(i, (i - 1) % count) for i in range(count)]
    left = lax.ppermute(array, "head", up)
    right = lax.ppermute(array, "head", down)
    half = array.shape[0] // 2
    return left, right, lax.ppermute(left[:half], "head", up), lax.ppermute(right[half:], "head", down)


def per_device(queries, values, codes, codebook, out_weight, grad_out):
    heads, entries, width = codebook.shape
    exchange = functools.partial(
        lax.all_to_all, axis_name="seq", split_axis=0, concat_axis=0, tiled=True
    )
    me_seq = lax.axis_index("seq").astype(jnp.int32).reshape(1)
    me_head = lax.axis_index("head").astype(jnp.int32).reshape(1)
    pieces = [
        (grad_out, *ring_pieces(grad_out[b * BLOCK : (b + 1) * BLOCK])) for b in range(2)
    ]
    total, first_count = own_counts(codes, entries)
    every = exchange(jnp.broadcast_to(total[None], (lax.axis_size("seq"), *total.shape)))
    codes_rows = codes.T.reshape(heads, 1, -1)
    book_t = jnp.swapaxes(codebook, 1, 2)
    send, first = own_sums(codes_rows, values, heads, entries)
    prefix = exchange(scanned(prefix_kernel, "prefix_scan", exchange(send)))
    probs, keys = zip(*[
        forward(b, me_seq, codes_rows, queries, codebook, book_t, every, first_count)
        for b in range(2)
    ])
    dout0, local, part0 = value_grads(0, me_head, pieces[0], out_weight, probs[0])
    dout1, local, part1, send = value_grads(
        1, me_head, pieces[1], out_weight, probs[1], (part0, local)
    )
    later = exchange(scanned(suffix_kernel, "suffix_scan", exchange(send)))
    grad_query, code0 = score_grads(
        0, me_seq, codes_rows, queries, values, dout0, probs[0], keys[0], book_t, prefix, every
    )
    grad_query, send = score_grads(
        1, me_seq, codes_rows, queries, values, dout1, probs[1], keys[1], book_t, prefix, every,
        (first, first_count, code0, grad_query),
    )
    grad_book = exchange(scanned(total_kernel, "total_scan", exchange(send)))
    grad_values = finish(codes, local, later, part1)
    return grad_query, grad_values, grad_book.reshape(codebook.shape).astype(F32)


def solution(mesh):
    rows = P("seq", "head")
    return jax.shard_map(
        per_device,
        mesh=mesh,
        in_specs=(rows, rows, rows, P("head", None, None), P("head", None), rows),
        out_specs=(rows, rows, P("head", None, None)),
        check_vma=False,
    )
```

```python
import functools
import math

import jax
import jax.numpy as jnp
from jax import lax
from jax.experimental import pallas as pl
from jax.experimental.pallas import tpu as pltpu
from jax.sharding import PartitionSpec as P

BLOCK = 512
PART = 256
TILE = 128
HALF = 64
ROWS = 96
F32 = jnp.float32
BF16 = jnp.bfloat16
VMEM_LIMIT = 60 << 20


def dot(left, right):
    return lax.dot_general(left, right, (((1,), (0,)), ((), ())), preferred_element_type=F32)


def dot_nt(left, right):
    return lax.dot_general(left, right, (((1,), (1,)), ((), ())), preferred_element_type=F32)


def call(kernel, name, grid, in_specs, outs, scratch=(), aliases=None, prefetch=0, flops=0, size=0):
    return pl.pallas_call(
        kernel,
        grid_spec=pltpu.PrefetchScalarGridSpec(
            num_scalar_prefetch=prefetch,
            grid=grid,
            in_specs=in_specs,
            out_specs=[spec for _, _, spec in outs],
            scratch_shapes=list(scratch),
        ),
        out_shape=[jax.ShapeDtypeStruct(shape, dtype) for shape, dtype, _ in outs],
        input_output_aliases=aliases or {},
        compiler_params=pltpu.CompilerParams(
            dimension_semantics=("arbitrary",) * len(grid), vmem_limit_bytes=VMEM_LIMIT
        ),
        cost_estimate=pl.CostEstimate(flops=flops, bytes_accessed=size, transcendentals=0),
        name=name,
    )


def onehot_rows(codes_row, entries):
    entry = lax.broadcasted_iota(jnp.int32, (entries, codes_row.shape[1]), 0)
    return jnp.where(entry == codes_row, 1.0, 0.0).astype(BF16)


def fold(array):
    rows, lanes = array.shape
    return jnp.sum(array.reshape(rows // 8, 8, lanes), axis=0)


def fold_max(array):
    rows, lanes = array.shape
    return jnp.max(array.reshape(rows // 8, 8, lanes), axis=0)


def sum_kernel(codes_ref, columns_ref, value_ref, send_ref, first_ref, first_count_ref):
    heads, entries, width = first_ref.shape
    slices = entries // HALF
    blocks = value_ref.shape[0] // BLOCK
    levels = lax.broadcasted_iota(jnp.int32, (BLOCK, entries), 1)
    lines = []
    for h in range(heads):
        total = None
        number = None
        for b in range(blocks):
            span = slice(b * BLOCK, (b + 1) * BLOCK)
            hot = onehot_rows(codes_ref[h, :, span], entries)
            part = dot(hot, value_ref[span, h * width : (h + 1) * width])
            same = jnp.where(levels == columns_ref[span, h : h + 1], 1.0, 0.0)
            amount = jnp.sum(fold(same), axis=0, keepdims=True)
            if b == 0:
                first_ref[h] = part
                first_count_ref[h] = amount
            total = part if b == 0 else total + part
            number = amount if b == 0 else number + amount
        for k in range(slices):
            send_ref[h * slices + k, :HALF, :] = total[k * HALF : (k + 1) * HALF].astype(BF16)
        lines += [number[:, i * TILE : (i + 1) * TILE] for i in range(entries // TILE)]
    lines = jnp.concatenate(lines, axis=0)
    high = jnp.floor(lines * (1.0 / 256.0))
    digits = jnp.concatenate([high, lines - high * 256.0], axis=0).astype(BF16)
    for k in range(heads * slices):
        send_ref[k, HALF:, :] = digits


def own_sums(codes_rows, codes, values, heads, entries):
    tokens = values.shape[0]
    width = values.shape[1] // heads
    slices = entries // HALF
    whole = lambda i: (0, 0, 0)
    return call(
        sum_kernel, "own_sums", (1,),
        [
            pl.BlockSpec(codes_rows.shape, whole),
            pl.BlockSpec(codes.shape, lambda i: (0, 0)),
            pl.BlockSpec(values.shape, lambda i: (0, 0)),
        ],
        [
            ((heads * slices, ROWS, TILE), BF16, pl.BlockSpec((heads * slices, ROWS, TILE), whole)),
            ((heads, entries, width), F32, pl.BlockSpec((heads, entries, width), whole)),
            ((heads, 1, entries), F32, pl.BlockSpec((heads, 1, entries), whole)),
        ],
        flops=1 << 30, size=4 << 20,
    )(codes_rows, codes, values)


def prefix_kernel(me_ref, in_ref, first_ref, out_ref, count_ref):
    running = jnp.zeros(out_ref.shape[1:], F32)
    lines = (ROWS - HALF) // 2
    number = jnp.zeros((lines, TILE), F32)
    for d in range(in_ref.shape[0]):
        out_ref[d] = running.astype(BF16)
        running = running + in_ref[d, :HALF, :].astype(F32)
        digits = in_ref[d, HALF:, :].astype(F32)
        digits = digits[:lines] * 256.0 + digits[lines:]
        number = number + jnp.where(d < me_ref[0], digits, 0.0)
    heads = first_ref.shape[0]
    per = lines // heads
    for h in range(heads):
        for i in range(per):
            line = number[h * per + i : h * per + i + 1]
            columns = slice(i * TILE, (i + 1) * TILE)
            count_ref[0, h, :, columns] = line
            count_ref[1, h, :, columns] = line + first_ref[h, :, columns]


def prefix_scan(me, pieces, first):
    count = pieces.shape[0]
    heads, _, entries = first.shape
    whole = lambda i, *_: (0, 0, 0)
    shape = (2, heads, 1, entries)
    return call(
        prefix_kernel, "prefix_scan", (1,),
        [pl.BlockSpec(pieces.shape, whole), pl.BlockSpec(first.shape, whole)],
        [
            ((count, HALF, TILE), BF16, pl.BlockSpec((count, HALF, TILE), whole)),
            (shape, F32, pl.BlockSpec(shape, lambda i, *_: (0, 0, 0, 0))),
        ],
        prefetch=1, size=1 << 20,
    )(me, pieces, first)


def suffix_kernel(in_ref, out_ref):
    running = jnp.zeros((HALF, TILE), F32)
    total = jnp.zeros((HALF, TILE), F32)
    for d in reversed(range(in_ref.shape[0])):
        out_ref[d, :HALF, :] = running.astype(BF16)
        running = running + in_ref[d, :HALF, :].astype(F32)
        total = total + in_ref[d, HALF:, :].astype(F32)
    low = total.astype(BF16)
    for d in range(in_ref.shape[0]):
        out_ref[d, HALF:, :] = low


def suffix_scan(pieces):
    spec = pl.BlockSpec(pieces.shape, lambda i: (0, 0, 0))
    return call(
        suffix_kernel, "suffix_scan", (1,), [spec], [(pieces.shape, BF16, spec)], size=2 << 20
    )(pieces)[0]


def count_columns(number):
    tiles = [
        jnp.broadcast_to(number[:, i * TILE : (i + 1) * TILE], (TILE, TILE)).T
        for i in range(number.shape[1] // TILE)
    ]
    return jnp.concatenate(tiles, axis=0)


def forward_kernel(codes_ref, query_ref, book_ref, book_t_ref, count_ref,
                   low_ref, keys_ref, rows_k, counts, scores):
    entries, width = book_ref.shape[1:]
    entry_tiles = entries // TILE
    factor = width ** -0.5 * math.log2(math.e)
    causal = lax.broadcasted_iota(jnp.int32, (TILE, TILE), 1) >= lax.broadcasted_iota(
        jnp.int32, (TILE, TILE), 0
    )
    parts = BLOCK // PART
    blocks = low_ref.shape[0]

    def prepare(b):
        keys_t = dot(
            book_t_ref[0], onehot_rows(codes_ref[0, :, b * BLOCK : (b + 1) * BLOCK], entries)
        )
        keys_ref[b, 0] = keys_t.astype(BF16)
        rows_k[b, :entries, :] = book_ref[0]
        rows_k[b, entries:, :] = keys_t.T.astype(BF16)
        counts[b] = count_columns(count_ref[b, 0])

    def multiply(b, n):
        used = entries + PART * (n + 1)
        at = b * BLOCK + n * PART
        scores[b, n, :used, :] = dot_nt(rows_k[b, :used, :], query_ref[at : at + PART, :])

    def soften(b, n):
        used = entries + PART * (n + 1)
        for j in range(PART // TILE):
            columns = slice(j * TILE, (j + 1) * TILE)
            target = slice(n * PART + j * TILE, n * PART + (j + 1) * TILE)
            pieces = range(entry_tiles + 2 * n + j + 1)
            top = jnp.full((8, TILE), -jnp.inf, F32)
            for i in pieces:
                rows = slice(i * TILE, (i + 1) * TILE)
                piece = scores[b, n, rows, columns]
                if i < entry_tiles:
                    piece = jnp.where(counts[b, rows, :] > 0.0, piece, -jnp.inf)
                    scores[b, n, rows, columns] = piece
                elif i == pieces[-1]:
                    piece = jnp.where(causal, piece, -jnp.inf)
                    scores[b, n, rows, columns] = piece
                top = jnp.maximum(top, fold_max(piece))
            top = jnp.max(top, axis=0, keepdims=True)
            total = jnp.zeros((8, TILE), F32)
            for i in pieces:
                rows = slice(i * TILE, (i + 1) * TILE)
                piece = jnp.exp2((scores[b, n, rows, columns] - top) * factor)
                scores[b, n, rows, columns] = piece
                if i < entry_tiles:
                    piece = piece * counts[b, rows, :]
                total = total + fold(piece)
            inverse = 1.0 / jnp.sum(total, axis=0, keepdims=True)
            for i in pieces:
                rows = slice(i * TILE, (i + 1) * TILE)
                low_ref[b, 0, rows, target] = (scores[b, n, rows, columns] * inverse).astype(BF16)
            if j == 0:
                low_ref[b, 0, used - TILE : used, target] = jnp.zeros((TILE, TILE), BF16)

    order = [(b, n) for b in range(blocks) for n in range(parts)]
    for b in range(blocks):
        prepare(b)
    multiply(*order[0])
    for k, item in enumerate(order):
        if k + 1 < len(order):
            multiply(*order[k + 1])
        soften(*item)


def forward(codes_rows, queries, book, book_t, counts):
    heads, entries, width = book.shape
    tokens = queries.shape[0]
    blocks = tokens // BLOCK
    both = entries + BLOCK
    by_head = lambda h: (h, 0, 0)
    in_blocks = lambda h: (0, h, 0, 0)
    return call(
        forward_kernel, "forward", (heads,),
        [
            pl.BlockSpec((1, 1, tokens), by_head),
            pl.BlockSpec((tokens, width), lambda h: (0, h)),
            pl.BlockSpec((1, entries, width), by_head),
            pl.BlockSpec((1, width, entries), by_head),
            pl.BlockSpec((blocks, 1, 1, entries), in_blocks),
        ],
        [
            ((blocks, heads, both, BLOCK), BF16, pl.BlockSpec((blocks, 1, both, BLOCK), in_blocks)),
            ((blocks, heads, width, BLOCK), BF16, pl.BlockSpec((blocks, 1, width, BLOCK), in_blocks)),
        ],
        [
            pltpu.VMEM((blocks, both, width), BF16),
            pltpu.VMEM((blocks, entries, TILE), F32),
            pltpu.VMEM((blocks, 2, both, PART), F32),
        ],
        flops=6 << 30, size=12 << 20,
    )(codes_rows, queries, book, book_t, counts)


def backward_kernel(_, own_ref, left_ref, right_ref, far0_ref, far1_ref, own_w, left_w, right_w,
                    far_w, codes_ref, query_ref, value_ref, probs_ref, keys_ref, book_t_ref,
                    prefix_ref, count_ref, first_ref,
                    grad_query_ref, local_ref, part_ref, send_ref,
                    dout, hot, rows_v, counts, grads, score_grad, key_grad, wide_t):
    width, entries = book_t_ref.shape[1:]
    entry_tiles = entries // TILE
    parts = BLOCK // PART
    blocks = probs_ref.shape[0]
    scale = width ** -0.5
    head = pl.program_id(0)

    @pl.when(head == 0)
    def _():
        count = own_ref.shape[0] // PART
        for n in range(count):
            span = slice(n * PART, (n + 1) * PART)
            total = dot_nt(own_ref[span, :], own_w[...]) + dot_nt(left_ref[span, :], left_w[...])
            total = total + dot_nt(right_ref[span, :], right_w[...])
            if n < count // 2:
                far = far0_ref[span, :]
            else:
                far = far1_ref[(n - count // 2) * PART : (n + 1 - count // 2) * PART, :]
            total = total + dot_nt(far, far_w[...])
            for h in range(dout.shape[0]):
                dout[h, span, :] = total[:, h * width : (h + 1) * width].astype(BF16)

    def prepare(b):
        hot[b] = onehot_rows(codes_ref[0, :, b * BLOCK : (b + 1) * BLOCK], entries)
        wide_t[b, :, :entries] = book_t_ref[0]
        wide_t[b, :, entries:] = keys_ref[b, 0]
        sums = prefix_ref[...].reshape(entries, width)
        if b > 0:
            sums = (sums.astype(F32) + first_ref[0]).astype(BF16)
        rows_v[b, :entries, :] = sums
        rows_v[b, entries:, :] = value_ref[b * BLOCK : (b + 1) * BLOCK, :]
        counts[b] = count_columns(count_ref[b, 0])

    def multiply(b, n):
        used = entries + PART * (n + 1)
        at = b * BLOCK + n * PART
        grads[b, n, :used, :] = dot_nt(rows_v[b, :used, :], dout[head, at : at + PART, :])

    def combine(b, n):
        used = entries + PART * (n + 1)
        for j in range(PART // TILE):
            columns = slice(j * TILE, (j + 1) * TILE)
            source = slice(n * PART + j * TILE, n * PART + (j + 1) * TILE)
            pieces = range(entry_tiles + 2 * n + j + 1)
            delta = jnp.zeros((8, TILE), F32)
            for i in pieces:
                rows = slice(i * TILE, (i + 1) * TILE)
                delta = delta + fold(
                    probs_ref[b, 0, rows, source].astype(F32) * grads[b, n, rows, columns]
                )
            delta = jnp.sum(delta, axis=0, keepdims=True) * scale
            for i in pieces:
                rows = slice(i * TILE, (i + 1) * TILE)
                shift = delta
                if i < entry_tiles:
                    shift = delta * counts[b, rows, :]
                piece = grads[b, n, rows, columns] * scale - shift
                piece = probs_ref[b, 0, rows, source].astype(F32) * piece
                score_grad[b, n, rows, columns] = piece.astype(BF16)
            if j == 0:
                score_grad[b, n, used - TILE : used, columns] = jnp.zeros((TILE, TILE), BF16)

    sums_k = [[None] * parts for _ in range(blocks)]
    sums_v = [[None] * parts for _ in range(blocks)]

    def outputs(b, n):
        used = entries + PART * (n + 1)
        at = b * BLOCK + n * PART
        span = slice(at, at + PART)
        sums_v[b][n] = dot(probs_ref[b, 0, :used, n * PART : (n + 1) * PART], dout[head, span, :])
        sums_k[b][n] = dot(score_grad[b, n, :used, :], query_ref[span, :])
        grad_t = dot(wide_t[b, :, :used], score_grad[b, n, :used, :])
        grad_query_ref[span, :] = grad_t.T.astype(BF16)

    order = [(b, n) for b in range(blocks) for n in range(parts)]
    for b in range(blocks):
        prepare(b)
    multiply(*order[0])
    code = None
    part = None
    middle = entries + PART
    for k, item in enumerate(order):
        if k + 1 < len(order):
            multiply(*order[k + 1])
        combine(*item)
        outputs(*item)
        b, n = item
        if n == parts - 1:
            first, last = sums_v[b]
            at = b * BLOCK
            local_ref[at : at + PART, :] = first[entries:] + last[entries:middle]
            local_ref[at + PART : at + BLOCK, :] = last[middle:]
            mine = first[:entries] + last[:entries]
            if b == blocks - 1:
                part_ref[0] = mine
            part = mine if b == 0 else part + mine
            first, last = sums_k[b]
            key_grad[b, :PART, :] = (first[entries:] + last[entries:middle]).astype(BF16)
            key_grad[b, PART:, :] = last[middle:].astype(BF16)
            mine = first[:entries] + last[:entries] + dot(hot[b], key_grad[b])
            code = mine if b == 0 else code + mine
    for k in range(entries // HALF):
        rows = slice(k * HALF, (k + 1) * HALF)
        send_ref[k, :HALF, :] = part[rows].astype(BF16)
        send_ref[k, HALF:, :] = code[rows].astype(BF16)


def backward(me, pieces, weight, codes_rows, queries, values, probs, keys, book_t, prefix, counts,
             first):
    heads, width, entries = book_t.shape
    tokens = queries.shape[0]
    blocks = tokens // BLOCK
    both = entries + BLOCK
    columns = weight.shape[1] // 4
    slices = entries // HALF
    by_head = lambda h, *_: (h, 0, 0)
    in_blocks = lambda h, *_: (0, h, 0, 0)
    rows_of = pl.BlockSpec((tokens, width), lambda h, *_: (0, h))
    per_head = pl.BlockSpec((1, entries, width), by_head)

    def chunk(offset):
        return pl.BlockSpec(
            (weight.shape[0], columns), lambda h, me: (0, lax.rem(me[0] + offset, 4))
        )

    in_specs = [pl.BlockSpec(piece.shape, lambda h, *_: (0, 0)) for piece in pieces]
    in_specs += [chunk(0), chunk(3), chunk(1), chunk(2)]
    in_specs += [
        pl.BlockSpec((1, 1, tokens), by_head),
        rows_of,
        rows_of,
        pl.BlockSpec((blocks, 1, both, BLOCK), in_blocks),
        pl.BlockSpec((blocks, 1, width, BLOCK), in_blocks),
        pl.BlockSpec((1, width, entries), by_head),
        pl.BlockSpec((slices, HALF, width), by_head),
        pl.BlockSpec((blocks, 1, 1, entries), in_blocks),
        per_head,
    ]
    outs = [
        (queries.shape, BF16, rows_of),
        (queries.shape, F32, rows_of),
        ((heads, entries, width), F32, per_head),
        ((heads * slices, 2 * HALF, width), BF16, pl.BlockSpec((slices, 2 * HALF, width), by_head)),
    ]
    return call(
        backward_kernel, "backward", (heads,), in_specs, outs,
        [
            pltpu.VMEM((heads, tokens, width), BF16),
            pltpu.VMEM((blocks, entries, BLOCK), BF16),
            pltpu.VMEM((blocks, both, width), BF16),
            pltpu.VMEM((blocks, entries, TILE), F32),
            pltpu.VMEM((blocks, 2, both, PART), F32),
            pltpu.VMEM((blocks, 2, both, PART), BF16),
            pltpu.VMEM((blocks, BLOCK, width), BF16),
            pltpu.VMEM((blocks, width, both), BF16),
        ],
        prefetch=1, flops=20 << 30, size=24 << 20,
    )(me, *pieces, *[weight] * 4, codes_rows, queries, values, probs, keys, book_t, prefix, counts,
      first)


def finish_kernel(codes_ref, local_ref, later_ref, part_ref, out_ref, book_ref, tables):
    heads, entries, width = part_ref.shape
    slices = entries // HALF
    step = pl.program_id(0)

    @pl.when(step == 0)
    def _():
        for h in range(heads):
            pieces = later_ref[h * slices : (h + 1) * slices]
            later = pieces[:, :HALF, :].reshape(entries, width)
            tables[1, h] = later
            tables[0, h] = (later.astype(F32) + part_ref[h]).astype(BF16)
            book_ref[h] = pieces[:, HALF:, :].reshape(entries, width).astype(F32)

    block = step // (pl.num_programs(0) // 2)
    levels = lax.broadcasted_iota(jnp.int32, (codes_ref.shape[0], entries), 1)
    for h in range(heads):
        hot = jnp.where(levels == codes_ref[:, h : h + 1], 1.0, 0.0).astype(BF16)
        columns = slice(h * width, (h + 1) * width)
        out_ref[:, columns] = (local_ref[:, columns] + dot(hot, tables[block, h])).astype(BF16)


def finish(codes, local, later, part):
    heads, entries, width = part.shape
    whole = lambda b: (0, 0, 0)
    rows = pl.BlockSpec((PART, heads * width), lambda b: (b, 0))
    return call(
        finish_kernel, "finish_values", (local.shape[0] // PART,),
        [
            pl.BlockSpec((PART, heads), lambda b: (b, 0)),
            rows,
            pl.BlockSpec(later.shape, whole),
            pl.BlockSpec(part.shape, whole),
        ],
        [(local.shape, BF16, rows), (part.shape, F32, pl.BlockSpec(part.shape, whole))],
        [pltpu.VMEM((2, heads, entries, width), BF16)],
        flops=1 << 30, size=4 << 20,
    )(codes, local, later, part)


def ring_pieces(array):
    count = lax.axis_size("head")
    up = [(i, (i + 1) % count) for i in range(count)]
    down = [(i, (i - 1) % count) for i in range(count)]
    left = lax.ppermute(array, "head", up)
    right = lax.ppermute(array, "head", down)
    half = array.shape[0] // 2
    far = lax.ppermute(left[:half], "head", up), lax.ppermute(right[half:], "head", down)
    return array, left, right, *far


def per_device(queries, values, codes, codebook, out_weight, grad_out):
    heads, entries, width = codebook.shape
    exchange = functools.partial(
        lax.all_to_all, axis_name="seq", split_axis=0, concat_axis=0, tiled=True
    )
    me_seq = lax.axis_index("seq").astype(jnp.int32).reshape(1)
    me_head = lax.axis_index("head").astype(jnp.int32).reshape(1)
    pieces = ring_pieces(grad_out)
    codes_rows = codes.T.reshape(heads, 1, -1)
    book_t = jnp.swapaxes(codebook, 1, 2)
    send, first, first_count = own_sums(codes_rows, codes, values, heads, entries)
    prefix, counts = prefix_scan(me_seq, exchange(send), first_count)
    prefix = exchange(prefix)
    probs, keys = forward(codes_rows, queries, codebook, book_t, counts)
    grad_query, local, part, send = backward(
        me_head, pieces, out_weight, codes_rows, queries, values, probs, keys, book_t, prefix,
        counts, first,
    )
    later = exchange(suffix_scan(exchange(send)))
    grad_values, grad_book = finish(codes, local, later, part)
    return grad_query, grad_values, grad_book


def solution(mesh):
    rows = P("seq", "head")
    return jax.shard_map(
        per_device,
        mesh=mesh,
        in_specs=(rows, rows, rows, P("head", None, None), P("head", None), rows),
        out_specs=(rows, rows, P("head", None, None)),
        check_vma=False,
    )
```

```python
import functools
import math

import jax
import jax.numpy as jnp
from jax import lax
from jax.experimental import pallas as pl
from jax.experimental.pallas import tpu as pltpu
from jax.sharding import PartitionSpec as P

BLOCK = 512
PART = 256
TILE = 128
HALF = 64
ROWS = 96
F32 = jnp.float32
BF16 = jnp.bfloat16
VMEM_LIMIT = 60 << 20


def dot(left, right):
    return lax.dot_general(left, right, (((1,), (0,)), ((), ())), preferred_element_type=F32)


def dot_nt(left, right):
    return lax.dot_general(left, right, (((1,), (1,)), ((), ())), preferred_element_type=F32)


def call(kernel, name, grid, in_specs, outs, scratch=(), aliases=None, prefetch=0, flops=0, size=0,
         limit=VMEM_LIMIT):
    return pl.pallas_call(
        kernel,
        grid_spec=pltpu.PrefetchScalarGridSpec(
            num_scalar_prefetch=prefetch,
            grid=grid,
            in_specs=in_specs,
            out_specs=[spec for _, _, spec in outs],
            scratch_shapes=list(scratch),
        ),
        out_shape=[jax.ShapeDtypeStruct(shape, dtype) for shape, dtype, _ in outs],
        input_output_aliases=aliases or {},
        compiler_params=pltpu.CompilerParams(
            dimension_semantics=("arbitrary",) * len(grid), vmem_limit_bytes=limit
        ),
        cost_estimate=pl.CostEstimate(flops=flops, bytes_accessed=size, transcendentals=0),
        name=name,
    )


def onehot_rows(codes_row, entries):
    entry = lax.broadcasted_iota(jnp.int32, (entries, codes_row.shape[1]), 0)
    return jnp.where(entry == codes_row, 1.0, 0.0).astype(BF16)


def row_at(ref, index):
    place = lax.broadcasted_iota(jnp.int32, ref.shape, 0)
    return jnp.sum(jnp.where(place == index, ref[...], 0), axis=0, keepdims=True)


def fold(array):
    rows, lanes = array.shape
    return jnp.sum(array.reshape(rows // 8, 8, lanes), axis=0)


def fold_max(array):
    rows, lanes = array.shape
    return jnp.max(array.reshape(rows // 8, 8, lanes), axis=0)


def sum_kernel(codes_ref, value_ref, send_ref, first_ref, first_count_ref):
    heads, entries, width = first_ref.shape
    slices = entries // HALF
    blocks = value_ref.shape[0] // BLOCK
    ones = jnp.ones((BLOCK, TILE), BF16)
    lines = []
    for h in range(heads):
        total = None
        for b in range(blocks):
            span = slice(b * BLOCK, (b + 1) * BLOCK)
            hot = onehot_rows(codes_ref[h : h + 1, span], entries)
            columns = value_ref[span, h * width : (h + 1) * width]
            part = dot(hot, jnp.concatenate([columns, ones], axis=1))
            if b == 0:
                first_ref[h] = part[:, :width]
                for i in range(entries // TILE):
                    rows = slice(i * TILE, (i + 1) * TILE)
                    first_count_ref[h, :, rows] = part[rows, width:].T[:1]
            total = part if b == 0 else total + part
        for k in range(slices):
            rows = slice(k * HALF, (k + 1) * HALF)
            send_ref[h * slices + k, :HALF, :] = total[rows, :width].astype(BF16)
        for i in range(entries // TILE):
            lines.append(total[i * TILE : (i + 1) * TILE, width:].T[:1])
    lines = jnp.concatenate(lines, axis=0)
    high = jnp.floor(lines * (1.0 / 256.0))
    digits = jnp.concatenate([high, lines - high * 256.0], axis=0).astype(BF16)
    for k in range(heads * slices):
        send_ref[k, HALF:, :] = digits


def own_sums(codes, values, heads, entries):
    width = values.shape[1] // heads
    slices = entries // HALF
    whole = lambda i: (0, 0, 0)
    return call(
        sum_kernel, "own_sums", (1,),
        [
            pl.BlockSpec(codes.shape, lambda i: (0, 0)),
            pl.BlockSpec(values.shape, lambda i: (0, 0)),
        ],
        [
            ((heads * slices, ROWS, TILE), BF16, pl.BlockSpec((heads * slices, ROWS, TILE), whole)),
            ((heads, entries, width), F32, pl.BlockSpec((heads, entries, width), whole)),
            ((heads, 1, entries), F32, pl.BlockSpec((heads, 1, entries), whole)),
        ],

    )(codes, values)


def prefix_kernel(me_ref, in_ref, first_ref, out_ref, count_ref):
    running = jnp.zeros(out_ref.shape[1:], F32)
    lines = (ROWS - HALF) // 2
    number = jnp.zeros((lines, TILE), F32)
    for d in range(in_ref.shape[0]):
        out_ref[d] = running.astype(BF16)
        running = running + in_ref[d, :HALF, :].astype(F32)
        digits = in_ref[d, HALF:, :].astype(F32)
        digits = digits[:lines] * 256.0 + digits[lines:]
        number = number + jnp.where(d < me_ref[0], digits, 0.0)
    heads = first_ref.shape[0]
    per = lines // heads
    for h in range(heads):
        for i in range(per):
            line = number[h * per + i : h * per + i + 1]
            columns = slice(i * TILE, (i + 1) * TILE)
            count_ref[0, h, :, columns] = line
            count_ref[1, h, :, columns] = line + first_ref[h, :, columns]


def prefix_scan(me, pieces, first):
    count = pieces.shape[0]
    heads, _, entries = first.shape
    whole = lambda i, *_: (0, 0, 0)
    shape = (2, heads, 1, entries)
    return call(
        prefix_kernel, "prefix_scan", (1,),
        [pl.BlockSpec(pieces.shape, whole), pl.BlockSpec(first.shape, whole)],
        [
            ((count, HALF, TILE), BF16, pl.BlockSpec((count, HALF, TILE), whole)),
            (shape, F32, pl.BlockSpec(shape, lambda i, *_: (0, 0, 0, 0))),
        ],
        prefetch=1
    )(me, pieces, first)


def suffix_kernel(in_ref, out_ref):
    running = jnp.zeros((HALF, TILE), F32)
    total = jnp.zeros((HALF, TILE), F32)
    for d in reversed(range(in_ref.shape[0])):
        out_ref[d, :HALF, :] = running.astype(BF16)
        running = running + in_ref[d, :HALF, :].astype(F32)
        total = total + in_ref[d, HALF:, :].astype(F32)
    low = total.astype(BF16)
    for d in range(in_ref.shape[0]):
        out_ref[d, HALF:, :] = low


def suffix_scan(pieces):
    spec = pl.BlockSpec(pieces.shape, lambda i: (0, 0, 0))
    return call(
        suffix_kernel, "suffix_scan", (1,), [spec], [(pieces.shape, BF16, spec)], size=2 << 20
    )(pieces)[0]


def count_columns(number):
    tiles = [
        jnp.broadcast_to(number[:, i * TILE : (i + 1) * TILE], (TILE, TILE)).T
        for i in range(number.shape[1] // TILE)
    ]
    return jnp.concatenate(tiles, axis=0)


def forward_kernel(codes_ref, query_ref, book_ref, book_t_ref, count_ref,
                   low_ref, keys_ref, rows_k, counts, scores):
    entries, width = book_ref.shape[1:]
    head = pl.program_id(0)
    entry_tiles = entries // TILE
    factor = width ** -0.5 * math.log2(math.e)
    causal = lax.broadcasted_iota(jnp.int32, (TILE, TILE), 1) >= lax.broadcasted_iota(
        jnp.int32, (TILE, TILE), 0
    )
    parts = BLOCK // PART
    blocks = low_ref.shape[0]

    codes_row = row_at(codes_ref, head)

    def prepare(b):
        keys_t = dot(
            book_t_ref[0], onehot_rows(codes_row[:, b * BLOCK : (b + 1) * BLOCK], entries)
        )
        keys_ref[b, 0] = keys_t.astype(BF16)
        rows_k[b, :entries, :] = book_ref[0]
        rows_k[b, entries:, :] = keys_t.T.astype(BF16)
        counts[b] = count_columns(count_ref[b, 0])

    def multiply(b, n):
        used = entries + PART * (n + 1)
        at = b * BLOCK + n * PART
        scores[b, n, :used, :] = dot_nt(rows_k[b, :used, :], query_ref[at : at + PART, :])

    def soften(b, n):
        used = entries + PART * (n + 1)
        for j in range(PART // TILE):
            columns = slice(j * TILE, (j + 1) * TILE)
            target = slice(n * PART + j * TILE, n * PART + (j + 1) * TILE)
            pieces = range(entry_tiles + 2 * n + j + 1)
            top = jnp.full((8, TILE), -jnp.inf, F32)
            for i in pieces:
                rows = slice(i * TILE, (i + 1) * TILE)
                piece = scores[b, n, rows, columns]
                if i < entry_tiles:
                    piece = jnp.where(counts[b, rows, :] > 0.0, piece, -jnp.inf)
                    scores[b, n, rows, columns] = piece
                elif i == pieces[-1]:
                    piece = jnp.where(causal, piece, -jnp.inf)
                    scores[b, n, rows, columns] = piece
                top = jnp.maximum(top, fold_max(piece))
            top = jnp.max(top, axis=0, keepdims=True)
            total = jnp.zeros((8, TILE), F32)
            for i in pieces:
                rows = slice(i * TILE, (i + 1) * TILE)
                piece = jnp.exp2((scores[b, n, rows, columns] - top) * factor)
                scores[b, n, rows, columns] = piece
                if i < entry_tiles:
                    piece = piece * counts[b, rows, :]
                total = total + fold(piece)
            inverse = 1.0 / jnp.sum(total, axis=0, keepdims=True)
            for i in pieces:
                rows = slice(i * TILE, (i + 1) * TILE)
                low_ref[b, 0, rows, target] = (scores[b, n, rows, columns] * inverse).astype(BF16)
            if j == 0:
                low_ref[b, 0, used - TILE : used, target] = jnp.zeros((TILE, TILE), BF16)

    order = [(b, n) for b in range(blocks) for n in range(parts)]
    for b in range(blocks):
        prepare(b)
    multiply(*order[0])
    for k, item in enumerate(order):
        if k + 1 < len(order):
            multiply(*order[k + 1])
        soften(*item)


def forward(codes, queries, book, book_t, counts):
    heads, entries, width = book.shape
    tokens = queries.shape[0]
    blocks = tokens // BLOCK
    both = entries + BLOCK
    by_head = lambda h: (h, 0, 0)
    in_blocks = lambda h: (0, h, 0, 0)
    return call(
        forward_kernel, "forward", (heads,),
        [
            pl.BlockSpec(codes.shape, lambda h: (0, 0)),
            pl.BlockSpec((tokens, width), lambda h: (0, h)),
            pl.BlockSpec((1, entries, width), by_head),
            pl.BlockSpec((1, width, entries), by_head),
            pl.BlockSpec((blocks, 1, 1, entries), in_blocks),
        ],
        [
            ((blocks, heads, both, BLOCK), BF16, pl.BlockSpec((blocks, 1, both, BLOCK), in_blocks)),
            ((blocks, heads, width, BLOCK), BF16, pl.BlockSpec((blocks, 1, width, BLOCK), in_blocks)),
        ],
        [
            pltpu.VMEM((blocks, both, width), BF16),
            pltpu.VMEM((blocks, entries, TILE), F32),
            pltpu.VMEM((blocks, 2, both, PART), F32),
        ],

    )(codes, queries, book, book_t, counts)


def cotangent_kernel(_, own_ref, left_ref, right_ref, far_ref, own_w, left_w, right_w, far_w,
                     out_ref):
    heads, rows, width = out_ref.shape
    total = dot_nt(own_ref[...], own_w[...]) + dot_nt(left_ref[...], left_w[...])
    total = total + dot_nt(right_ref[...], right_w[...]) + dot_nt(far_ref[...], far_w[...])
    for h in range(heads):
        out_ref[h] = total[:, h * width : (h + 1) * width].astype(BF16)


def cotangent(me, block, pieces, weight, heads):
    width = weight.shape[0] // heads
    columns = weight.shape[1] // 4

    def chunk(offset):
        return pl.BlockSpec(
            (weight.shape[0], columns), lambda n, me: (0, lax.rem(me[0] + offset, 4))
        )

    rows = pl.BlockSpec((PART, columns), lambda n, *_: (2 * block + n, 0))
    return call(
        cotangent_kernel, f"cotangent_{block}", (2,),
        [
            rows, rows, rows, pl.BlockSpec((PART, columns), lambda n, *_: (n, 0)), chunk(0), chunk(3), chunk(1), chunk(2),
        ],
        [((heads, BLOCK, width), BF16, pl.BlockSpec((heads, PART, width), lambda n, *_: (0, n, 0)))],
        prefetch=1, flops=1 << 30, size=5 << 20,
    )(me, *pieces, *[weight] * 4)[0]


def backward_kernel(block, refs):
    (codes_ref, query_ref, value_ref, dout_ref, probs_ref, keys_ref, book_t_ref, prefix_ref,
     count_ref) = refs[:9]
    if block == 0:
        grad_query_ref, local_ref, part_ref, code_ref = refs[9:13]
    else:
        first_ref, part0_ref, code0_ref = refs[9:12]
        grad_query_ref, local_ref, part_ref, send_ref = refs[14:18]
    hot, rows_v, counts, grads, score_grad, key_grad, wide_t = refs[-7:]
    width, entries = book_t_ref.shape[1:]
    entry_tiles = entries // TILE
    parts = BLOCK // PART
    scale = width ** -0.5
    codes_row = row_at(codes_ref, pl.program_id(0))
    hot[...] = onehot_rows(codes_row[:, block * BLOCK : (block + 1) * BLOCK], entries)
    wide_t[:, :entries] = book_t_ref[0]
    wide_t[:, entries:] = keys_ref[0, 0]
    sums = prefix_ref[...].reshape(entries, width)
    if block > 0:
        sums = (sums.astype(F32) + first_ref[0]).astype(BF16)
    rows_v[:entries, :] = sums
    rows_v[entries:, :] = value_ref[...]
    counts[...] = count_columns(count_ref[0, 0])

    def multiply(n):
        used = entries + PART * (n + 1)
        grads[n, :used, :] = dot_nt(rows_v[:used, :], dout_ref[0, n * PART : (n + 1) * PART, :])

    def combine(n):
        used = entries + PART * (n + 1)
        for j in range(PART // TILE):
            columns = slice(j * TILE, (j + 1) * TILE)
            source = slice(n * PART + j * TILE, n * PART + (j + 1) * TILE)
            pieces = range(entry_tiles + 2 * n + j + 1)
            delta = jnp.zeros((8, TILE), F32)
            for i in pieces:
                rows = slice(i * TILE, (i + 1) * TILE)
                delta = delta + fold(
                    probs_ref[0, 0, rows, source].astype(F32) * grads[n, rows, columns]
                )
            delta = jnp.sum(delta, axis=0, keepdims=True) * scale
            for i in pieces:
                rows = slice(i * TILE, (i + 1) * TILE)
                shift = delta
                if i < entry_tiles:
                    shift = delta * counts[rows, :]
                piece = grads[n, rows, columns] * scale - shift
                piece = probs_ref[0, 0, rows, source].astype(F32) * piece
                score_grad[n, rows, columns] = piece.astype(BF16)
            if j == 0:
                score_grad[n, used - TILE : used, columns] = jnp.zeros((TILE, TILE), BF16)

    sums_k = []
    sums_v = []

    def outputs(n):
        used = entries + PART * (n + 1)
        span = slice(n * PART, (n + 1) * PART)
        sums_k.append(dot(score_grad[n, :used, :], query_ref[span, :]))
        grad_t = dot(wide_t[:, :used], score_grad[n, :used, :])
        grad_query_ref[span, :] = grad_t.T.astype(BF16)

    def shares(n):
        used = entries + PART * (n + 1)
        span = slice(n * PART, (n + 1) * PART)
        sums_v.append(dot(probs_ref[0, 0, :used, span], dout_ref[0, span, :]))

    middle = entries + PART
    multiply(0)
    multiply(1)
    combine(0)
    shares(0)
    shares(1)
    outputs(0)
    combine(1)
    outputs(1)
    first, last = sums_v
    local_ref[:PART, :] = first[entries:] + last[entries:middle]
    local_ref[PART:, :] = last[middle:]
    part = first[:entries] + last[:entries]
    part_ref[0] = part
    first, last = sums_k
    key_grad[:PART, :] = (first[entries:] + last[entries:middle]).astype(BF16)
    key_grad[PART:, :] = last[middle:].astype(BF16)
    code = first[:entries] + last[:entries] + dot(hot[...], key_grad[...])
    if block == 0:
        code_ref[0] = code
    else:
        part = part + part0_ref[0]
        code = code + code0_ref[0]
        for k in range(entries // HALF):
            rows = slice(k * HALF, (k + 1) * HALF)
            send_ref[k, :HALF, :] = part[rows].astype(BF16)
            send_ref[k, HALF:, :] = code[rows].astype(BF16)


def backward(block, codes, queries, values, dout, probs, keys, book_t, prefix, counts, extra=()):
    heads, width, entries = book_t.shape
    tokens = queries.shape[0]
    both = entries + BLOCK
    slices = entries // HALF
    by_head = lambda h: (h, 0, 0)
    in_blocks = lambda h: (block, h, 0, 0)
    rows_of = pl.BlockSpec((BLOCK, width), lambda h: (block, h))
    per_head = pl.BlockSpec((1, entries, width), by_head)
    in_specs = [
        pl.BlockSpec(codes.shape, lambda h: (0, 0)),
        rows_of,
        rows_of,
        pl.BlockSpec((1, BLOCK, width), by_head),
        pl.BlockSpec((1, 1, both, BLOCK), in_blocks),
        pl.BlockSpec((1, 1, width, BLOCK), in_blocks),
        pl.BlockSpec((1, width, entries), by_head),
        pl.BlockSpec((slices, HALF, width), by_head),
        pl.BlockSpec((1, 1, 1, entries), in_blocks),
    ]
    outs = [
        (queries.shape, BF16, rows_of),
        (queries.shape, F32, rows_of),
        ((heads, entries, width), F32, per_head),
    ]
    aliases = None
    if block == 0:
        outs.append(((heads, entries, width), F32, per_head))
    else:
        in_specs += [per_head] * 3 + [pl.BlockSpec(memory_space=pl.ANY)] * 2
        aliases = {12: 0, 13: 1}
        outs.append(
            ((heads * slices, 2 * HALF, width), BF16,
             pl.BlockSpec((slices, 2 * HALF, width), by_head))
        )
    return call(
        lambda *refs: backward_kernel(block, refs), f"backward_{block}", (heads,), in_specs, outs,
        [
            pltpu.VMEM((entries, BLOCK), BF16),
            pltpu.VMEM((both, width), BF16),
            pltpu.VMEM((entries, TILE), F32),
            pltpu.VMEM((2, both, PART), F32),
            pltpu.VMEM((2, both, PART), BF16),
            pltpu.VMEM((BLOCK, width), BF16),
            pltpu.VMEM((width, both), BF16),
        ],
        aliases=aliases, flops=10 << 30, size=12 << 20,
    )(codes, queries, values, dout, probs, keys, book_t, prefix, counts, *extra)


def finish_kernel(codes_ref, local_ref, later_ref, part_ref, out_ref, book_ref):
    entries, width = part_ref.shape[1:]
    head = pl.program_id(0)
    codes_row = row_at(codes_ref, head)
    pieces = later_ref[...]
    later = pieces[:, :HALF, :].reshape(entries, width)
    book_ref[0] = pieces[:, HALF:, :].reshape(entries, width).astype(F32)
    tokens = local_ref.shape[0]
    tables = [later] * (tokens // BLOCK)
    tables[0] = (later.astype(F32) + part_ref[0]).astype(BF16)
    levels = lax.broadcasted_iota(jnp.int32, (TILE, TILE), 1)
    for i in range(tokens // TILE):
        rows = slice(i * TILE, (i + 1) * TILE)
        column = jnp.broadcast_to(codes_row[:, rows], (TILE, TILE)).T
        hot = jnp.concatenate(
            [
                jnp.where(levels + k * TILE == column, 1.0, 0.0).astype(BF16)
                for k in range(entries // TILE)
            ],
            axis=1,
        )
        out_ref[rows, :] = (local_ref[rows, :] + dot(hot, tables[i * TILE // BLOCK])).astype(BF16)


def finish(codes, local, later, part):
    heads, entries, width = part.shape
    tokens = local.shape[0]
    by_head = lambda h: (h, 0, 0)
    rows_of = pl.BlockSpec((tokens, width), lambda h: (0, h))
    per_head = pl.BlockSpec((1, entries, width), by_head)
    return call(
        finish_kernel, "finish_values", (heads,),
        [
            pl.BlockSpec(codes.shape, lambda h: (0, 0)),
            rows_of,
            pl.BlockSpec((entries // HALF, 2 * HALF, width), by_head),
            per_head,
        ],
        [(local.shape, BF16, rows_of), (part.shape, F32, per_head)],
        flops=1 << 30, size=8 << 20,
    )(codes, local, later, part)


def moved(array, step):
    count = lax.axis_size("head")
    return lax.ppermute(array, "head", [(i, (i + step) % count) for i in range(count)])


def per_device(queries, values, codes, codebook, out_weight, grad_out):
    heads, entries, width = codebook.shape
    exchange = functools.partial(
        lax.all_to_all, axis_name="seq", split_axis=0, concat_axis=0, tiled=True
    )
    me_seq = lax.axis_index("seq").astype(jnp.int32).reshape(1)
    me_head = lax.axis_index("head").astype(jnp.int32).reshape(1)
    left, right = moved(grad_out, 1), moved(grad_out, -1)
    far = [moved(grad_out[b * BLOCK : (b + 1) * BLOCK], 2) for b in range(2)]
    codes = codes.T
    book_t = jnp.swapaxes(codebook, 1, 2)
    send, first, first_count = own_sums(codes, values, heads, entries)
    prefix, counts = prefix_scan(me_seq, exchange(send), first_count)
    prefix, left, right = lax.optimization_barrier((prefix, left, right))
    prefix = exchange(prefix)
    probs, keys = forward(codes, queries, codebook, book_t, counts)
    extra = ()
    for b in range(2):
        if extra:
            far[b], part = lax.optimization_barrier((far[b], part))
            extra = (first, part, *extra[2:])
        dout = cotangent(me_head, b, (grad_out, left, right, far[b]), out_weight, heads)
        grad_query, local, part, last = backward(
            b, codes, queries, values, dout, probs, keys, book_t, prefix, counts, extra
        )
        extra = (first, part, last, grad_query, local)
    later = exchange(suffix_scan(exchange(last)))
    grad_values, grad_book = finish(codes, local, later, part)
    return grad_query, grad_values, grad_book


def solution(mesh):
    rows = P("seq", "head")
    return jax.shard_map(
        per_device,
        mesh=mesh,
        in_specs=(rows, rows, rows, P("head", None, None), P("head", None), rows),
        out_specs=(rows, rows, P("head", None, None)),
        check_vma=False,
    )
```

```python
import functools
import math

import jax
import jax.numpy as jnp
from jax import lax
from jax.experimental import pallas as pl
from jax.experimental.pallas import tpu as pltpu
from jax.sharding import PartitionSpec as P

BLOCK = 512
PART = 256
TILE = 128
HALF = 64
ROWS = 96
F32 = jnp.float32
BF16 = jnp.bfloat16
VMEM_LIMIT = 60 << 20


def dot(left, right):
    return lax.dot_general(left, right, (((1,), (0,)), ((), ())), preferred_element_type=F32)


def dot_nt(left, right):
    return lax.dot_general(left, right, (((1,), (1,)), ((), ())), preferred_element_type=F32)


def call(kernel, name, grid, in_specs, outs, scratch=(), aliases=None, prefetch=0, flops=0, size=0,
         limit=VMEM_LIMIT):
    return pl.pallas_call(
        kernel,
        grid_spec=pltpu.PrefetchScalarGridSpec(
            num_scalar_prefetch=prefetch,
            grid=grid,
            in_specs=in_specs,
            out_specs=[spec for _, _, spec in outs],
            scratch_shapes=list(scratch),
        ),
        out_shape=[jax.ShapeDtypeStruct(shape, dtype) for shape, dtype, _ in outs],
        input_output_aliases=aliases or {},
        compiler_params=pltpu.CompilerParams(
            dimension_semantics=("arbitrary",) * len(grid), vmem_limit_bytes=limit
        ),
        cost_estimate=pl.CostEstimate(flops=flops, bytes_accessed=size, transcendentals=0),
        name=name,
    )


def onehot_rows(codes_row, entries):
    entry = lax.broadcasted_iota(jnp.int32, (entries, codes_row.shape[1]), 0)
    return jnp.where(entry == codes_row, 1.0, 0.0).astype(BF16)


def row_at(ref, index):
    place = lax.broadcasted_iota(jnp.int32, ref.shape, 0)
    return jnp.sum(jnp.where(place == index, ref[...], 0), axis=0, keepdims=True)


def fold(array):
    rows, lanes = array.shape
    return jnp.sum(array.reshape(rows // 8, 8, lanes), axis=0)


def fold_max(array):
    rows, lanes = array.shape
    return jnp.max(array.reshape(rows // 8, 8, lanes), axis=0)


def sum_kernel(codes_ref, value_ref, send_ref, first_ref, first_count_ref):
    heads, entries, width = first_ref.shape
    slices = entries // HALF
    blocks = value_ref.shape[0] // BLOCK
    ones = jnp.ones((BLOCK, TILE), BF16)
    lines = []
    for h in range(heads):
        total = None
        for b in range(blocks):
            span = slice(b * BLOCK, (b + 1) * BLOCK)
            hot = onehot_rows(codes_ref[h : h + 1, span], entries)
            columns = value_ref[span, h * width : (h + 1) * width]
            part = dot(hot, jnp.concatenate([columns, ones], axis=1))
            if b == 0:
                first_ref[h] = part[:, :width]
                for i in range(entries // TILE):
                    rows = slice(i * TILE, (i + 1) * TILE)
                    first_count_ref[h, :, rows] = part[rows, width:].T[:1]
            total = part if b == 0 else total + part
        for k in range(slices):
            rows = slice(k * HALF, (k + 1) * HALF)
            send_ref[h * slices + k, :HALF, :] = total[rows, :width].astype(BF16)
        for i in range(entries // TILE):
            lines.append(total[i * TILE : (i + 1) * TILE, width:].T[:1])
    lines = jnp.concatenate(lines, axis=0)
    high = jnp.floor(lines * (1.0 / 256.0))
    digits = jnp.concatenate([high, lines - high * 256.0], axis=0).astype(BF16)
    for k in range(heads * slices):
        send_ref[k, HALF:, :] = digits


def own_sums(codes, values, heads, entries):
    width = values.shape[1] // heads
    slices = entries // HALF
    whole = lambda i: (0, 0, 0)
    return call(
        sum_kernel, "own_sums", (1,),
        [
            pl.BlockSpec(codes.shape, lambda i: (0, 0)),
            pl.BlockSpec(values.shape, lambda i: (0, 0)),
        ],
        [
            ((heads * slices, ROWS, TILE), BF16, pl.BlockSpec((heads * slices, ROWS, TILE), whole)),
            ((heads, entries, width), F32, pl.BlockSpec((heads, entries, width), whole)),
            ((heads, 1, entries), F32, pl.BlockSpec((heads, 1, entries), whole)),
        ],

    )(codes, values)


def prefix_kernel(me_ref, in_ref, first_ref, out_ref, count_ref):
    running = jnp.zeros(out_ref.shape[1:], F32)
    lines = (ROWS - HALF) // 2
    number = jnp.zeros((lines, TILE), F32)
    for d in range(in_ref.shape[0]):
        out_ref[d] = running.astype(BF16)
        running = running + in_ref[d, :HALF, :].astype(F32)
        digits = in_ref[d, HALF:, :].astype(F32)
        digits = digits[:lines] * 256.0 + digits[lines:]
        number = number + jnp.where(d < me_ref[0], digits, 0.0)
    heads = first_ref.shape[0]
    per = lines // heads
    for h in range(heads):
        for i in range(per):
            line = number[h * per + i : h * per + i + 1]
            columns = slice(i * TILE, (i + 1) * TILE)
            count_ref[0, h, :, columns] = line
            count_ref[1, h, :, columns] = line + first_ref[h, :, columns]


def prefix_scan(me, pieces, first):
    count = pieces.shape[0]
    heads, _, entries = first.shape
    whole = lambda i, *_: (0, 0, 0)
    shape = (2, heads, 1, entries)
    return call(
        prefix_kernel, "prefix_scan", (1,),
        [pl.BlockSpec(pieces.shape, whole), pl.BlockSpec(first.shape, whole)],
        [
            ((count, HALF, TILE), BF16, pl.BlockSpec((count, HALF, TILE), whole)),
            (shape, F32, pl.BlockSpec(shape, lambda i, *_: (0, 0, 0, 0))),
        ],
        prefetch=1
    )(me, pieces, first)


def suffix_kernel(in_ref, out_ref):
    running = jnp.zeros((HALF, TILE), F32)
    total = jnp.zeros((HALF, TILE), F32)
    for d in reversed(range(in_ref.shape[0])):
        out_ref[d, :HALF, :] = running.astype(BF16)
        running = running + in_ref[d, :HALF, :].astype(F32)
        total = total + in_ref[d, HALF:, :].astype(F32)
    low = total.astype(BF16)
    for d in range(in_ref.shape[0]):
        out_ref[d, HALF:, :] = low


def suffix_scan(pieces):
    spec = pl.BlockSpec(pieces.shape, lambda i: (0, 0, 0))
    return call(
        suffix_kernel, "suffix_scan", (1,), [spec], [(pieces.shape, BF16, spec)], size=2 << 20
    )(pieces)[0]


def count_columns(number):
    tiles = [
        jnp.broadcast_to(number[:, i * TILE : (i + 1) * TILE], (TILE, TILE)).T
        for i in range(number.shape[1] // TILE)
    ]
    return jnp.concatenate(tiles, axis=0)


def forward_kernel(codes_ref, query_ref, book_ref, book_t_ref, count_ref,
                   low_ref, keys_ref, rows_k, counts, scores):
    entries, width = book_ref.shape[1:]
    head = pl.program_id(0)
    entry_tiles = entries // TILE
    factor = width ** -0.5 * math.log2(math.e)
    causal = lax.broadcasted_iota(jnp.int32, (TILE, TILE), 1) >= lax.broadcasted_iota(
        jnp.int32, (TILE, TILE), 0
    )
    parts = BLOCK // PART
    blocks = low_ref.shape[0]

    codes_row = row_at(codes_ref, head)

    def prepare(b):
        keys_t = dot(
            book_t_ref[0], onehot_rows(codes_row[:, b * BLOCK : (b + 1) * BLOCK], entries)
        )
        keys_ref[b, 0] = keys_t.astype(BF16)
        rows_k[b, :entries, :] = book_ref[0]
        rows_k[b, entries:, :] = keys_t.T.astype(BF16)
        counts[b] = count_columns(count_ref[b, 0])

    def multiply(b, n):
        used = entries + PART * (n + 1)
        at = b * BLOCK + n * PART
        scores[b, n, :used, :] = dot_nt(rows_k[b, :used, :], query_ref[at : at + PART, :])

    def soften(b, n):
        used = entries + PART * (n + 1)
        for j in range(PART // TILE):
            columns = slice(j * TILE, (j + 1) * TILE)
            target = slice(n * PART + j * TILE, n * PART + (j + 1) * TILE)
            pieces = range(entry_tiles + 2 * n + j + 1)
            top = jnp.full((8, TILE), -jnp.inf, F32)
            for i in pieces:
                rows = slice(i * TILE, (i + 1) * TILE)
                piece = scores[b, n, rows, columns]
                if i < entry_tiles:
                    piece = jnp.where(counts[b, rows, :] > 0.0, piece, -jnp.inf)
                    scores[b, n, rows, columns] = piece
                elif i == pieces[-1]:
                    piece = jnp.where(causal, piece, -jnp.inf)
                    scores[b, n, rows, columns] = piece
                top = jnp.maximum(top, fold_max(piece))
            top = jnp.max(top, axis=0, keepdims=True)
            total = jnp.zeros((8, TILE), F32)
            for i in pieces:
                rows = slice(i * TILE, (i + 1) * TILE)
                piece = jnp.exp2((scores[b, n, rows, columns] - top) * factor)
                scores[b, n, rows, columns] = piece
                if i < entry_tiles:
                    piece = piece * counts[b, rows, :]
                total = total + fold(piece)
            inverse = 1.0 / jnp.sum(total, axis=0, keepdims=True)
            for i in pieces:
                rows = slice(i * TILE, (i + 1) * TILE)
                low_ref[b, 0, rows, target] = (scores[b, n, rows, columns] * inverse).astype(BF16)
            if j == 0:
                low_ref[b, 0, used - TILE : used, target] = jnp.zeros((TILE, TILE), BF16)

    order = [(b, n) for b in range(blocks) for n in range(parts)]
    for b in range(blocks):
        prepare(b)
    multiply(*order[0])
    for k, item in enumerate(order):
        if k + 1 < len(order):
            multiply(*order[k + 1])
        soften(*item)


def forward(codes, queries, book, book_t, counts):
    heads, entries, width = book.shape
    tokens = queries.shape[0]
    blocks = tokens // BLOCK
    both = entries + BLOCK
    by_head = lambda h: (h, 0, 0)
    in_blocks = lambda h: (0, h, 0, 0)
    return call(
        forward_kernel, "forward", (heads,),
        [
            pl.BlockSpec(codes.shape, lambda h: (0, 0)),
            pl.BlockSpec((tokens, width), lambda h: (0, h)),
            pl.BlockSpec((1, entries, width), by_head),
            pl.BlockSpec((1, width, entries), by_head),
            pl.BlockSpec((blocks, 1, 1, entries), in_blocks),
        ],
        [
            ((blocks, heads, both, BLOCK), BF16, pl.BlockSpec((blocks, 1, both, BLOCK), in_blocks)),
            ((blocks, heads, width, BLOCK), BF16, pl.BlockSpec((blocks, 1, width, BLOCK), in_blocks)),
        ],
        [
            pltpu.VMEM((blocks, both, width), BF16),
            pltpu.VMEM((blocks, entries, TILE), F32),
            pltpu.VMEM((blocks, 2, both, PART), F32),
        ],

    )(codes, queries, book, book_t, counts)


def backward_kernel(_, own_ref, left_ref, right_ref, far0_ref, far1_ref, own_w, left_w, right_w,
                    far_w, codes_ref, query_ref, value_ref, probs_ref, keys_ref, book_t_ref,
                    prefix_ref, count_ref, first_ref,
                    grad_query_ref, local_ref, part_ref, send_ref,
                    dout, hot, rows_v, counts, grads, score_grad, key_grad, wide_t):
    width, entries = book_t_ref.shape[1:]
    entry_tiles = entries // TILE
    parts = BLOCK // PART
    blocks = probs_ref.shape[0]
    scale = width ** -0.5
    head = pl.program_id(0)

    @pl.when(head == 0)
    def _():
        count = own_ref.shape[0] // PART
        for n in range(count):
            span = slice(n * PART, (n + 1) * PART)
            total = dot_nt(own_ref[span, :], own_w[...]) + dot_nt(left_ref[span, :], left_w[...])
            total = total + dot_nt(right_ref[span, :], right_w[...])
            if n < count // 2:
                far = far0_ref[span, :]
            else:
                far = far1_ref[(n - count // 2) * PART : (n + 1 - count // 2) * PART, :]
            total = total + dot_nt(far, far_w[...])
            for h in range(dout.shape[0]):
                dout[h, span, :] = total[:, h * width : (h + 1) * width].astype(BF16)

    codes_row = row_at(codes_ref, head)

    def prepare(b):
        hot[b] = onehot_rows(codes_row[:, b * BLOCK : (b + 1) * BLOCK], entries)
        wide_t[b, :, :entries] = book_t_ref[0]
        wide_t[b, :, entries:] = keys_ref[b, 0]
        sums = prefix_ref[...].reshape(entries, width)
        if b > 0:
            sums = (sums.astype(F32) + first_ref[0]).astype(BF16)
        rows_v[b, :entries, :] = sums
        rows_v[b, entries:, :] = value_ref[b * BLOCK : (b + 1) * BLOCK, :]
        counts[b] = count_columns(count_ref[b, 0])

    def multiply(b, n):
        used = entries + PART * (n + 1)
        at = b * BLOCK + n * PART
        grads[b, n, :used, :] = dot_nt(rows_v[b, :used, :], dout[head, at : at + PART, :])

    def combine(b, n):
        used = entries + PART * (n + 1)
        for j in range(PART // TILE):
            columns = slice(j * TILE, (j + 1) * TILE)
            source = slice(n * PART + j * TILE, n * PART + (j + 1) * TILE)
            pieces = range(entry_tiles + 2 * n + j + 1)
            delta = jnp.zeros((8, TILE), F32)
            for i in pieces:
                rows = slice(i * TILE, (i + 1) * TILE)
                delta = delta + fold(
                    probs_ref[b, 0, rows, source].astype(F32) * grads[b, n, rows, columns]
                )
            delta = jnp.sum(delta, axis=0, keepdims=True) * scale
            for i in pieces:
                rows = slice(i * TILE, (i + 1) * TILE)
                shift = delta
                if i < entry_tiles:
                    shift = delta * counts[b, rows, :]
                piece = grads[b, n, rows, columns] * scale - shift
                piece = probs_ref[b, 0, rows, source].astype(F32) * piece
                score_grad[b, n, rows, columns] = piece.astype(BF16)
            if j == 0:
                score_grad[b, n, used - TILE : used, columns] = jnp.zeros((TILE, TILE), BF16)

    sums_k = [[None] * parts for _ in range(blocks)]
    sums_v = [[None] * parts for _ in range(blocks)]

    def outputs(b, n):
        used = entries + PART * (n + 1)
        at = b * BLOCK + n * PART
        span = slice(at, at + PART)
        sums_v[b][n] = dot(probs_ref[b, 0, :used, n * PART : (n + 1) * PART], dout[head, span, :])
        sums_k[b][n] = dot(score_grad[b, n, :used, :], query_ref[span, :])
        grad_t = dot(wide_t[b, :, :used], score_grad[b, n, :used, :])
        grad_query_ref[span, :] = grad_t.T.astype(BF16)

    order = [(b, n) for b in range(blocks) for n in range(parts)]
    for b in range(blocks):
        prepare(b)
    multiply(*order[0])
    code = None
    part = None
    middle = entries + PART
    for k, item in enumerate(order):
        if k + 1 < len(order):
            multiply(*order[k + 1])
        combine(*item)
        outputs(*item)
        b, n = item
        if n == parts - 1:
            first, last = sums_v[b]
            at = b * BLOCK
            local_ref[at : at + PART, :] = first[entries:] + last[entries:middle]
            local_ref[at + PART : at + BLOCK, :] = last[middle:]
            mine = first[:entries] + last[:entries]
            if b == blocks - 1:
                part_ref[0] = mine
            part = mine if b == 0 else part + mine
            first, last = sums_k[b]
            key_grad[b, :PART, :] = (first[entries:] + last[entries:middle]).astype(BF16)
            key_grad[b, PART:, :] = last[middle:].astype(BF16)
            mine = first[:entries] + last[:entries] + dot(hot[b], key_grad[b])
            code = mine if b == 0 else code + mine
    for k in range(entries // HALF):
        rows = slice(k * HALF, (k + 1) * HALF)
        send_ref[k, :HALF, :] = part[rows].astype(BF16)
        send_ref[k, HALF:, :] = code[rows].astype(BF16)


def backward(me, pieces, weight, codes, queries, values, probs, keys, book_t, prefix, counts,
             first):
    heads, width, entries = book_t.shape
    tokens = queries.shape[0]
    blocks = tokens // BLOCK
    both = entries + BLOCK
    columns = weight.shape[1] // 4
    slices = entries // HALF
    by_head = lambda h, *_: (h, 0, 0)
    in_blocks = lambda h, *_: (0, h, 0, 0)
    rows_of = pl.BlockSpec((tokens, width), lambda h, *_: (0, h))
    per_head = pl.BlockSpec((1, entries, width), by_head)

    def chunk(offset):
        return pl.BlockSpec(
            (weight.shape[0], columns), lambda h, me: (0, lax.rem(me[0] + offset, 4))
        )

    in_specs = [pl.BlockSpec(piece.shape, lambda h, *_: (0, 0)) for piece in pieces]
    in_specs += [chunk(0), chunk(3), chunk(1), chunk(2)]
    in_specs += [
        pl.BlockSpec(codes.shape, lambda h, *_: (0, 0)),
        rows_of,
        rows_of,
        pl.BlockSpec((blocks, 1, both, BLOCK), in_blocks),
        pl.BlockSpec((blocks, 1, width, BLOCK), in_blocks),
        pl.BlockSpec((1, width, entries), by_head),
        pl.BlockSpec((slices, HALF, width), by_head),
        pl.BlockSpec((blocks, 1, 1, entries), in_blocks),
        per_head,
    ]
    outs = [
        (queries.shape, BF16, rows_of),
        (queries.shape, F32, rows_of),
        ((heads, entries, width), F32, per_head),
        ((heads * slices, 2 * HALF, width), BF16, pl.BlockSpec((slices, 2 * HALF, width), by_head)),
    ]
    return call(
        backward_kernel, "backward", (heads,), in_specs, outs,
        [
            pltpu.VMEM((heads, tokens, width), BF16),
            pltpu.VMEM((blocks, entries, BLOCK), BF16),
            pltpu.VMEM((blocks, both, width), BF16),
            pltpu.VMEM((blocks, entries, TILE), F32),
            pltpu.VMEM((blocks, 2, both, PART), F32),
            pltpu.VMEM((blocks, 2, both, PART), BF16),
            pltpu.VMEM((blocks, BLOCK, width), BF16),
            pltpu.VMEM((blocks, width, both), BF16),
        ],
        prefetch=1, flops=20 << 30, size=24 << 20,
    )(me, *pieces, *[weight] * 4, codes, queries, values, probs, keys, book_t, prefix, counts,
      first)


def finish_kernel(codes_ref, local_ref, later_ref, part_ref, out_ref, book_ref):
    entries, width = part_ref.shape[1:]
    head = pl.program_id(0)
    codes_row = row_at(codes_ref, head)
    pieces = later_ref[...]
    later = pieces[:, :HALF, :].reshape(entries, width)
    book_ref[0] = pieces[:, HALF:, :].reshape(entries, width).astype(F32)
    tokens = local_ref.shape[0]
    tables = [later] * (tokens // BLOCK)
    tables[0] = (later.astype(F32) + part_ref[0]).astype(BF16)
    levels = lax.broadcasted_iota(jnp.int32, (TILE, TILE), 1)
    for i in range(tokens // TILE):
        rows = slice(i * TILE, (i + 1) * TILE)
        column = jnp.broadcast_to(codes_row[:, rows], (TILE, TILE)).T
        hot = jnp.concatenate(
            [
                jnp.where(levels + k * TILE == column, 1.0, 0.0).astype(BF16)
                for k in range(entries // TILE)
            ],
            axis=1,
        )
        out_ref[rows, :] = (local_ref[rows, :] + dot(hot, tables[i * TILE // BLOCK])).astype(BF16)


def finish(codes, local, later, part):
    heads, entries, width = part.shape
    tokens = local.shape[0]
    by_head = lambda h: (h, 0, 0)
    rows_of = pl.BlockSpec((tokens, width), lambda h: (0, h))
    per_head = pl.BlockSpec((1, entries, width), by_head)
    return call(
        finish_kernel, "finish_values", (heads,),
        [
            pl.BlockSpec(codes.shape, lambda h: (0, 0)),
            rows_of,
            pl.BlockSpec((entries // HALF, 2 * HALF, width), by_head),
            per_head,
        ],
        [(local.shape, BF16, rows_of), (part.shape, F32, per_head)],
        flops=1 << 30, size=8 << 20,
    )(codes, local, later, part)


def ring_pieces(array):
    count = lax.axis_size("head")
    up = [(i, (i + 1) % count) for i in range(count)]
    down = [(i, (i - 1) % count) for i in range(count)]
    left = lax.ppermute(array, "head", up)
    right = lax.ppermute(array, "head", down)
    half = array.shape[0] // 2
    far = lax.ppermute(left[:half], "head", up), lax.ppermute(right[half:], "head", down)
    return array, left, right, *far


def per_device(queries, values, codes, codebook, out_weight, grad_out):
    heads, entries, width = codebook.shape
    exchange = functools.partial(
        lax.all_to_all, axis_name="seq", split_axis=0, concat_axis=0, tiled=True
    )
    me_seq = lax.axis_index("seq").astype(jnp.int32).reshape(1)
    me_head = lax.axis_index("head").astype(jnp.int32).reshape(1)
    pieces = ring_pieces(grad_out)
    codes = codes.T
    book_t = jnp.swapaxes(codebook, 1, 2)
    send, first, first_count = own_sums(codes, values, heads, entries)
    prefix, counts = prefix_scan(me_seq, exchange(send), first_count)
    prefix = exchange(prefix)
    probs, keys = forward(codes, queries, codebook, book_t, counts)
    grad_query, local, part, last = backward(
        me_head, pieces, out_weight, codes, queries, values, probs, keys, book_t, prefix, counts,
        first,
    )
    later = exchange(suffix_scan(exchange(last)))
    grad_values, grad_book = finish(codes, local, later, part)
    return grad_query, grad_values, grad_book


def solution(mesh):
    rows = P("seq", "head")
    return jax.shard_map(
        per_device,
        mesh=mesh,
        in_specs=(rows, rows, rows, P("head", None, None), P("head", None), rows),
        out_specs=(rows, rows, P("head", None, None)),
        check_vma=False,
    )
```

```python
import functools
import math

import jax
import jax.numpy as jnp
from jax import lax
from jax.experimental import pallas as pl
from jax.experimental.pallas import tpu as pltpu
from jax.sharding import Mesh
from jax.sharding import PartitionSpec as P

BLOCK = 512
PART = 256
TILE = 128
HALF = 64
ROWS = 96
F32 = jnp.float32
BF16 = jnp.bfloat16
VMEM_LIMIT = 60 << 20


def dot(left, right):
    return lax.dot_general(left, right, (((1,), (0,)), ((), ())), preferred_element_type=F32)


def dot_nt(left, right):
    return lax.dot_general(left, right, (((1,), (1,)), ((), ())), preferred_element_type=F32)


def call(kernel, name, grid, in_specs, outs, scratch=(), aliases=None, prefetch=0, flops=0, size=0,
         limit=VMEM_LIMIT):
    return pl.pallas_call(
        kernel,
        grid_spec=pltpu.PrefetchScalarGridSpec(
            num_scalar_prefetch=prefetch,
            grid=grid,
            in_specs=in_specs,
            out_specs=[spec for _, _, spec in outs],
            scratch_shapes=list(scratch),
        ),
        out_shape=[jax.ShapeDtypeStruct(shape, dtype) for shape, dtype, _ in outs],
        input_output_aliases=aliases or {},
        compiler_params=pltpu.CompilerParams(
            dimension_semantics=("arbitrary",) * len(grid), vmem_limit_bytes=limit
        ),
        cost_estimate=pl.CostEstimate(flops=flops, bytes_accessed=size, transcendentals=0),
        name=name,
    )


def onehot_rows(codes_row, entries):
    entry = lax.broadcasted_iota(jnp.int32, (entries, codes_row.shape[1]), 0)
    return jnp.where(entry == codes_row, 1.0, 0.0).astype(BF16)


def row_at(ref, index):
    place = lax.broadcasted_iota(jnp.int32, ref.shape, 0)
    return jnp.sum(jnp.where(place == index, ref[...], 0), axis=0, keepdims=True)


def fold(array):
    rows, lanes = array.shape
    return jnp.sum(array.reshape(rows // 8, 8, lanes), axis=0)


def fold_max(array):
    rows, lanes = array.shape
    return jnp.max(array.reshape(rows // 8, 8, lanes), axis=0)


def sum_kernel(codes_ref, value_ref, send_ref, first_ref, first_count_ref):
    heads, entries, width = first_ref.shape
    slices = entries // HALF
    blocks = value_ref.shape[0] // BLOCK
    ones = jnp.ones((BLOCK, TILE), BF16)
    lines = []
    for h in range(heads):
        total = None
        for b in range(blocks):
            span = slice(b * BLOCK, (b + 1) * BLOCK)
            hot = onehot_rows(codes_ref[h : h + 1, span], entries)
            columns = value_ref[span, h * width : (h + 1) * width]
            part = dot(hot, jnp.concatenate([columns, ones], axis=1))
            if b == 0:
                first_ref[h] = part[:, :width]
                for i in range(entries // TILE):
                    rows = slice(i * TILE, (i + 1) * TILE)
                    first_count_ref[h, :, rows] = part[rows, width:].T[:1]
            total = part if b == 0 else total + part
        for k in range(slices):
            rows = slice(k * HALF, (k + 1) * HALF)
            send_ref[h * slices + k, :HALF, :] = total[rows, :width].astype(BF16)
        for i in range(entries // TILE):
            lines.append(total[i * TILE : (i + 1) * TILE, width:].T[:1])
    lines = jnp.concatenate(lines, axis=0)
    high = jnp.floor(lines * (1.0 / 256.0))
    digits = jnp.concatenate([high, lines - high * 256.0], axis=0).astype(BF16)
    for k in range(heads * slices):
        send_ref[k, HALF:, :] = digits


def own_sums(codes, values, heads, entries):
    width = values.shape[1] // heads
    slices = entries // HALF
    whole = lambda i: (0, 0, 0)
    return call(
        sum_kernel, "own_sums", (1,),
        [
            pl.BlockSpec(codes.shape, lambda i: (0, 0)),
            pl.BlockSpec(values.shape, lambda i: (0, 0)),
        ],
        [
            ((heads * slices, ROWS, TILE), BF16, pl.BlockSpec((heads * slices, ROWS, TILE), whole)),
            ((heads, entries, width), F32, pl.BlockSpec((heads, entries, width), whole)),
            ((heads, 1, entries), F32, pl.BlockSpec((heads, 1, entries), whole)),
        ],

    )(codes, values)


def prefix_kernel(me_ref, in_ref, first_ref, out_ref, count_ref):
    running = jnp.zeros(out_ref.shape[1:], F32)
    lines = (ROWS - HALF) // 2
    number = jnp.zeros((lines, TILE), F32)
    for d in range(in_ref.shape[0]):
        out_ref[d] = running.astype(BF16)
        running = running + in_ref[d, :HALF, :].astype(F32)
        digits = in_ref[d, HALF:, :].astype(F32)
        digits = digits[:lines] * 256.0 + digits[lines:]
        number = number + jnp.where(d < me_ref[0], digits, 0.0)
    heads = first_ref.shape[0]
    per = lines // heads
    for h in range(heads):
        for i in range(per):
            line = number[h * per + i : h * per + i + 1]
            columns = slice(i * TILE, (i + 1) * TILE)
            count_ref[0, h, :, columns] = line
            count_ref[1, h, :, columns] = line + first_ref[h, :, columns]


def prefix_scan(me, pieces, first):
    count = pieces.shape[0]
    heads, _, entries = first.shape
    whole = lambda i, *_: (0, 0, 0)
    shape = (2, heads, 1, entries)
    return call(
        prefix_kernel, "prefix_scan", (1,),
        [pl.BlockSpec(pieces.shape, whole), pl.BlockSpec(first.shape, whole)],
        [
            ((count, HALF, TILE), BF16, pl.BlockSpec((count, HALF, TILE), whole)),
            (shape, F32, pl.BlockSpec(shape, lambda i, *_: (0, 0, 0, 0))),
        ],
        prefetch=1
    )(me, pieces, first)


def suffix_kernel(in_ref, out_ref):
    running = jnp.zeros((HALF, TILE), F32)
    total = jnp.zeros((HALF, TILE), F32)
    for d in reversed(range(in_ref.shape[0])):
        out_ref[d, :HALF, :] = running.astype(BF16)
        running = running + in_ref[d, :HALF, :].astype(F32)
        total = total + in_ref[d, HALF:, :].astype(F32)
    low = total.astype(BF16)
    for d in range(in_ref.shape[0]):
        out_ref[d, HALF:, :] = low


def suffix_scan(pieces):
    spec = pl.BlockSpec(pieces.shape, lambda i: (0, 0, 0))
    return call(
        suffix_kernel, "suffix_scan", (1,), [spec], [(pieces.shape, BF16, spec)], size=2 << 20
    )(pieces)[0]


def count_columns(number):
    tiles = [
        jnp.broadcast_to(number[:, i * TILE : (i + 1) * TILE], (TILE, TILE)).T
        for i in range(number.shape[1] // TILE)
    ]
    return jnp.concatenate(tiles, axis=0)


def forward_kernel(codes_ref, query_ref, book_ref, book_t_ref, count_ref,
                   low_ref, keys_ref, rows_k, counts, scores):
    entries, width = book_ref.shape[1:]
    head = pl.program_id(0)
    entry_tiles = entries // TILE
    factor = width ** -0.5 * math.log2(math.e)
    causal = lax.broadcasted_iota(jnp.int32, (TILE, TILE), 1) >= lax.broadcasted_iota(
        jnp.int32, (TILE, TILE), 0
    )
    parts = BLOCK // PART
    blocks = low_ref.shape[0]

    codes_row = row_at(codes_ref, head)

    def prepare(b):
        keys_t = dot(
            book_t_ref[0], onehot_rows(codes_row[:, b * BLOCK : (b + 1) * BLOCK], entries)
        )
        keys_ref[b, 0] = keys_t.astype(BF16)
        rows_k[b, :entries, :] = book_ref[0]
        rows_k[b, entries:, :] = keys_t.T.astype(BF16)
        counts[b] = count_columns(count_ref[b, 0])

    def multiply(b, n):
        used = entries + PART * (n + 1)
        at = b * BLOCK + n * PART
        scores[b, n, :used, :] = dot_nt(rows_k[b, :used, :], query_ref[at : at + PART, :])

    def soften(b, n):
        used = entries + PART * (n + 1)
        for j in range(PART // TILE):
            columns = slice(j * TILE, (j + 1) * TILE)
            target = slice(n * PART + j * TILE, n * PART + (j + 1) * TILE)
            pieces = range(entry_tiles + 2 * n + j + 1)
            top = jnp.full((8, TILE), -jnp.inf, F32)
            for i in pieces:
                rows = slice(i * TILE, (i + 1) * TILE)
                piece = scores[b, n, rows, columns]
                if i < entry_tiles:
                    piece = jnp.where(counts[b, rows, :] > 0.0, piece, -jnp.inf)
                    scores[b, n, rows, columns] = piece
                elif i == pieces[-1]:
                    piece = jnp.where(causal, piece, -jnp.inf)
                    scores[b, n, rows, columns] = piece
                top = jnp.maximum(top, fold_max(piece))
            top = jnp.max(top, axis=0, keepdims=True)
            total = jnp.zeros((8, TILE), F32)
            for i in pieces:
                rows = slice(i * TILE, (i + 1) * TILE)
                piece = jnp.exp2((scores[b, n, rows, columns] - top) * factor)
                scores[b, n, rows, columns] = piece
                if i < entry_tiles:
                    piece = piece * counts[b, rows, :]
                total = total + fold(piece)
            inverse = 1.0 / jnp.sum(total, axis=0, keepdims=True)
            for i in pieces:
                rows = slice(i * TILE, (i + 1) * TILE)
                low_ref[b, 0, rows, target] = (scores[b, n, rows, columns] * inverse).astype(BF16)
            if j == 0:
                low_ref[b, 0, used - TILE : used, target] = jnp.zeros((TILE, TILE), BF16)

    order = [(b, n) for b in range(blocks) for n in range(parts)]
    for b in range(blocks):
        prepare(b)
    multiply(*order[0])
    for k, item in enumerate(order):
        if k + 1 < len(order):
            multiply(*order[k + 1])
        soften(*item)


def forward(codes, queries, book, book_t, counts):
    heads, entries, width = book.shape
    tokens = queries.shape[0]
    blocks = tokens // BLOCK
    both = entries + BLOCK
    by_head = lambda h: (h, 0, 0)
    in_blocks = lambda h: (0, h, 0, 0)
    return call(
        forward_kernel, "forward", (heads,),
        [
            pl.BlockSpec(codes.shape, lambda h: (0, 0)),
            pl.BlockSpec((tokens, width), lambda h: (0, h)),
            pl.BlockSpec((1, entries, width), by_head),
            pl.BlockSpec((1, width, entries), by_head),
            pl.BlockSpec((blocks, 1, 1, entries), in_blocks),
        ],
        [
            ((blocks, heads, both, BLOCK), BF16, pl.BlockSpec((blocks, 1, both, BLOCK), in_blocks)),
            ((blocks, heads, width, BLOCK), BF16, pl.BlockSpec((blocks, 1, width, BLOCK), in_blocks)),
        ],
        [
            pltpu.VMEM((blocks, both, width), BF16),
            pltpu.VMEM((blocks, entries, TILE), F32),
            pltpu.VMEM((blocks, 2, both, PART), F32),
        ],

    )(codes, queries, book, book_t, counts)


def backward_kernel(me_ref, own_ref, left_ref, right_ref, far0_ref, far1_ref, own_w, left_w, right_w,
                    far_w, codes_ref, query_ref, value_ref, probs_ref, keys_ref, book_t_ref,
                    prefix_ref, count_ref, first_ref,
                    grad_query_ref, local_ref, part_ref, give_ref, keep_ref,
                    dout, hot, rows_v, counts, grads, score_grad, key_grad, wide_t):
    width, entries = book_t_ref.shape[1:]
    entry_tiles = entries // TILE
    parts = BLOCK // PART
    blocks = probs_ref.shape[0]
    scale = width ** -0.5
    step = pl.program_id(0)
    head = lax.rem(step + 2 - 2 * me_ref[1], 4)

    @pl.when(step == 0)
    def _():
        count = own_ref.shape[0] // PART
        for n in range(count):
            span = slice(n * PART, (n + 1) * PART)
            total = dot_nt(own_ref[span, :], own_w[...]) + dot_nt(left_ref[span, :], left_w[...])
            total = total + dot_nt(right_ref[span, :], right_w[...])
            if n < count // 2:
                far = far0_ref[span, :]
            else:
                far = far1_ref[(n - count // 2) * PART : (n + 1 - count // 2) * PART, :]
            total = total + dot_nt(far, far_w[...])
            for h in range(dout.shape[0]):
                dout[h, span, :] = total[:, h * width : (h + 1) * width].astype(BF16)

    codes_row = row_at(codes_ref, head)

    def prepare(b):
        hot[b] = onehot_rows(codes_row[:, b * BLOCK : (b + 1) * BLOCK], entries)
        wide_t[b, :, :entries] = book_t_ref[0]
        wide_t[b, :, entries:] = keys_ref[b, 0]
        sums = prefix_ref[...].reshape(entries, width)
        if b > 0:
            sums = (sums.astype(F32) + first_ref[0]).astype(BF16)
        rows_v[b, :entries, :] = sums
        rows_v[b, entries:, :] = value_ref[b * BLOCK : (b + 1) * BLOCK, :]
        counts[b] = count_columns(count_ref[b, 0])

    def multiply(b, n):
        used = entries + PART * (n + 1)
        at = b * BLOCK + n * PART
        grads[b, n, :used, :] = dot_nt(rows_v[b, :used, :], dout[head, at : at + PART, :])

    def combine(b, n):
        used = entries + PART * (n + 1)
        for j in range(PART // TILE):
            columns = slice(j * TILE, (j + 1) * TILE)
            source = slice(n * PART + j * TILE, n * PART + (j + 1) * TILE)
            pieces = range(entry_tiles + 2 * n + j + 1)
            delta = jnp.zeros((8, TILE), F32)
            for i in pieces:
                rows = slice(i * TILE, (i + 1) * TILE)
                delta = delta + fold(
                    probs_ref[b, 0, rows, source].astype(F32) * grads[b, n, rows, columns]
                )
            delta = jnp.sum(delta, axis=0, keepdims=True) * scale
            for i in pieces:
                rows = slice(i * TILE, (i + 1) * TILE)
                shift = delta
                if i < entry_tiles:
                    shift = delta * counts[b, rows, :]
                piece = grads[b, n, rows, columns] * scale - shift
                piece = probs_ref[b, 0, rows, source].astype(F32) * piece
                score_grad[b, n, rows, columns] = piece.astype(BF16)
            if j == 0:
                score_grad[b, n, used - TILE : used, columns] = jnp.zeros((TILE, TILE), BF16)

    sums_k = [[None] * parts for _ in range(blocks)]
    sums_v = [[None] * parts for _ in range(blocks)]

    def outputs(b, n):
        used = entries + PART * (n + 1)
        at = b * BLOCK + n * PART
        span = slice(at, at + PART)
        sums_v[b][n] = dot(probs_ref[b, 0, :used, n * PART : (n + 1) * PART], dout[head, span, :])
        sums_k[b][n] = dot(score_grad[b, n, :used, :], query_ref[span, :])
        grad_t = dot(wide_t[b, :, :used], score_grad[b, n, :used, :])
        grad_query_ref[span, :] = grad_t.T.astype(BF16)

    order = [(b, n) for b in range(blocks) for n in range(parts)]
    for b in range(blocks):
        prepare(b)
    multiply(*order[0])
    code = None
    part = None
    middle = entries + PART
    for k, item in enumerate(order):
        if k + 1 < len(order):
            multiply(*order[k + 1])
        combine(*item)
        outputs(*item)
        b, n = item
        if n == parts - 1:
            first, last = sums_v[b]
            at = b * BLOCK
            local_ref[at : at + PART, :] = first[entries:] + last[entries:middle]
            local_ref[at + PART : at + BLOCK, :] = last[middle:]
            mine = first[:entries] + last[:entries]
            if b == blocks - 1:
                part_ref[0] = mine
            part = mine if b == 0 else part + mine
            first, last = sums_k[b]
            key_grad[b, :PART, :] = (first[entries:] + last[entries:middle]).astype(BF16)
            key_grad[b, PART:, :] = last[middle:].astype(BF16)
            mine = first[:entries] + last[:entries] + dot(hot[b], key_grad[b])
            code = mine if b == 0 else code + mine

    def write(ref):
        for k in range(entries // HALF):
            rows = slice(k * HALF, (k + 1) * HALF)
            ref[k, :HALF, :] = part[rows].astype(BF16)
            ref[k, HALF:, :] = code[rows].astype(BF16)

    @pl.when(step < 2)
    def _():
        write(give_ref)

    @pl.when(step >= 2)
    def _():
        write(keep_ref)


def backward(me, pieces, weight, codes, queries, values, probs, keys, book_t, prefix, counts,
             first):
    heads, width, entries = book_t.shape
    tokens = queries.shape[0]
    blocks = tokens // BLOCK
    both = entries + BLOCK
    columns = weight.shape[1] // 4
    slices = entries // HALF
    at = lambda s, me: lax.rem(s + 2 - 2 * me[1], 4)
    by_head = lambda s, me: (at(s, me), 0, 0)
    in_blocks = lambda s, me: (0, at(s, me), 0, 0)
    rows_of = pl.BlockSpec((tokens, width), lambda s, me: (0, at(s, me)))
    shape = (slices, 2 * HALF, width)
    both_heads = (2 * slices, 2 * HALF, width)
    per_head = pl.BlockSpec((1, entries, width), by_head)

    def chunk(offset):
        return pl.BlockSpec(
            (weight.shape[0], columns), lambda h, me: (0, lax.rem(me[0] + offset, 4))
        )

    in_specs = [pl.BlockSpec(piece.shape, lambda h, *_: (0, 0)) for piece in pieces]
    in_specs += [chunk(0), chunk(3), chunk(1), chunk(2)]
    in_specs += [
        pl.BlockSpec(codes.shape, lambda h, *_: (0, 0)),
        rows_of,
        rows_of,
        pl.BlockSpec((blocks, 1, both, BLOCK), in_blocks),
        pl.BlockSpec((blocks, 1, width, BLOCK), in_blocks),
        pl.BlockSpec((1, width, entries), by_head),
        pl.BlockSpec((slices, HALF, width), by_head),
        pl.BlockSpec((blocks, 1, 1, entries), in_blocks),
        per_head,
    ]
    outs = [
        (queries.shape, BF16, rows_of),
        (queries.shape, F32, rows_of),
        ((heads, entries, width), F32, per_head),
        (both_heads, BF16, pl.BlockSpec(shape, lambda s, *_: (jnp.minimum(s, 1), 0, 0))),
        (both_heads, BF16, pl.BlockSpec(shape, lambda s, *_: (jnp.maximum(s - 2, 0), 0, 0))),
    ]
    return call(
        backward_kernel, "backward", (heads,), in_specs, outs,
        [
            pltpu.VMEM((heads, tokens, width), BF16),
            pltpu.VMEM((blocks, entries, BLOCK), BF16),
            pltpu.VMEM((blocks, both, width), BF16),
            pltpu.VMEM((blocks, entries, TILE), F32),
            pltpu.VMEM((blocks, 2, both, PART), F32),
            pltpu.VMEM((blocks, 2, both, PART), BF16),
            pltpu.VMEM((blocks, BLOCK, width), BF16),
            pltpu.VMEM((blocks, width, both), BF16),
        ],
        prefetch=1, flops=20 << 30, size=24 << 20,
    )(me, *pieces, *[weight] * 4, codes, queries, values, probs, keys, book_t, prefix, counts,
      first)


def finish_kernel(own, refs):
    me_ref, codes_ref, local_ref, later_ref = refs[:4]
    if own:
        kept_ref, part_ref = refs[4:6]
    else:
        part_ref = refs[4]
    out_ref, book_ref = refs[-2:]
    entries, width = part_ref.shape[1:]
    step = pl.program_id(0)
    head = 2 * me_ref[0] + step if own else 2 - 2 * me_ref[0] + step
    codes_row = row_at(codes_ref, head)
    later = later_ref[:, :HALF, :].astype(F32)
    if own:
        later = later + jnp.where(me_ref[0] == 0, kept_ref[:, :HALF, :].astype(F32), 0.0)
    later = later.reshape(entries, width)
    book_ref[0] = later_ref[:, HALF:, :].reshape(entries, width).astype(F32)
    tokens = local_ref.shape[0]
    tables = [later.astype(BF16)] * (tokens // BLOCK)
    tables[0] = (later + part_ref[0]).astype(BF16)
    levels = lax.broadcasted_iota(jnp.int32, (TILE, TILE), 1)
    for i in range(tokens // TILE):
        rows = slice(i * TILE, (i + 1) * TILE)
        column = jnp.broadcast_to(codes_row[:, rows], (TILE, TILE)).T
        hot = jnp.concatenate(
            [
                jnp.where(levels + k * TILE == column, 1.0, 0.0).astype(BF16)
                for k in range(entries // TILE)
            ],
            axis=1,
        )
        out_ref[rows, :] = (local_ref[rows, :] + dot(hot, tables[i * TILE // BLOCK])).astype(BF16)


def finish(own, core, codes, local, later, part, extra):
    heads, entries, width = part.shape
    tokens = local.shape[0]
    at = lambda s, core: (2 * core[0] if own else 2 - 2 * core[0]) + s
    by_head = lambda s, core: (at(s, core), 0, 0)
    rows_of = pl.BlockSpec((tokens, width), lambda s, core: (0, at(s, core)))
    pieces = pl.BlockSpec((entries // HALF, 2 * HALF, width), lambda s, *_: (s, 0, 0))
    per_head = pl.BlockSpec((1, entries, width), by_head)
    in_specs = [pl.BlockSpec(codes.shape, lambda s, *_: (0, 0)), rows_of, pieces]
    if own:
        in_specs += [pieces, per_head]
        args = (*extra, part)
    else:
        in_specs += [per_head] + [pl.BlockSpec(memory_space=pl.ANY)] * 2
        args = (part, *extra)
    return call(
        lambda *refs: finish_kernel(own, refs), "finish_own" if own else "finish_other", (2,),
        in_specs,
        [(local.shape, BF16, rows_of), (part.shape, F32, per_head)],
        aliases=None if own else {5: 0, 6: 1}, prefetch=1, flops=1 << 30, size=8 << 20,
    )(core, codes, local, later, *args)


def ring_pieces(array):
    count = lax.axis_size("head")
    up = [(i, (i + 1) % count) for i in range(count)]
    down = [(i, (i - 1) % count) for i in range(count)]
    left = lax.ppermute(array, "head", up)
    right = lax.ppermute(array, "head", down)
    half = array.shape[0] // 2
    far = lax.ppermute(left[:half], "head", up), lax.ppermute(right[half:], "head", down)
    return array, left, right, *far


def per_device(queries, values, codes, codebook, out_weight, grad_out):
    heads, entries, width = codebook.shape
    exchange = functools.partial(
        lax.all_to_all, axis_name=("chip", "core"), split_axis=0, concat_axis=0, tiled=True
    )
    between_chips = functools.partial(
        lax.all_to_all, axis_name="chip", split_axis=0, concat_axis=0, tiled=True
    )
    other_core = functools.partial(lax.ppermute, axis_name="core", perm=[(0, 1), (1, 0)])
    core = lax.axis_index("core").astype(jnp.int32)
    me_seq = lax.axis_index(("chip", "core")).astype(jnp.int32).reshape(1)
    me = jnp.stack([lax.axis_index("head").astype(jnp.int32), core])
    pieces = ring_pieces(grad_out)
    codes = codes.T
    book_t = jnp.swapaxes(codebook, 1, 2)
    send, first, first_count = own_sums(codes, values, heads, entries)
    prefix, counts = prefix_scan(me_seq, exchange(send), first_count)
    prefix = exchange(prefix)
    probs, keys = forward(codes, queries, codebook, book_t, counts)
    grad_query, local, part, give, keep = backward(
        me, pieces, out_weight, codes, queries, values, probs, keys, book_t, prefix, counts, first
    )
    got = other_core(give)
    chip = (keep.astype(F32) + got.astype(F32)).astype(BF16)
    later = between_chips(suffix_scan(between_chips(chip)))
    is_value = lax.broadcasted_iota(jnp.int32, later.shape, 1) < HALF
    mine = jnp.where(is_value & (core == 1), keep.astype(F32), 0.0)
    theirs = other_core((later.astype(F32) + mine).astype(BF16))
    core = core.reshape(1)
    results = finish(True, core, codes, local, later, part, (got,))
    grad_values, grad_book = finish(False, core, codes, local, theirs, part, results)
    return grad_query, grad_values, grad_book


def solution(mesh):
    finer = Mesh(mesh.devices.reshape(-1, 2, mesh.shape["head"]), ("chip", "core", "head"))
    rows = P(("chip", "core"), "head")
    return jax.shard_map(
        per_device,
        mesh=finer,
        in_specs=(rows, rows, rows, P("head", None, None), P("head", None), rows),
        out_specs=(rows, rows, P("head", None, None)),
        check_vma=False,
    )
```

```python
import functools
import math

import jax
import jax.numpy as jnp
from jax import lax
from jax.experimental import pallas as pl
from jax.experimental.pallas import tpu as pltpu
from jax.sharding import Mesh
from jax.sharding import PartitionSpec as P

BLOCK = 512
PART = 256
TILE = 128
HALF = 64
ROWS = 96
F32 = jnp.float32
BF16 = jnp.bfloat16
VMEM_LIMIT = 44 << 20
IN_VMEM = pl.BlockSpec(memory_space=pltpu.VMEM)


def dot(left, right):
    return lax.dot_general(left, right, (((1,), (0,)), ((), ())), preferred_element_type=F32)


def dot_nt(left, right):
    return lax.dot_general(left, right, (((1,), (1,)), ((), ())), preferred_element_type=F32)


def call(kernel, name, grid, in_specs, outs, scratch=(), aliases=None, prefetch=0, flops=0, size=0,
         limit=VMEM_LIMIT):
    run = pl.pallas_call(
        kernel,
        grid_spec=pltpu.PrefetchScalarGridSpec(
            num_scalar_prefetch=prefetch,
            grid=grid,
            in_specs=in_specs,
            out_specs=[spec for _, _, spec in outs],
            scratch_shapes=list(scratch),
        ),
        out_shape=[pltpu.HBM(shape, dtype) for shape, dtype, _ in outs],
        input_output_aliases=aliases or {},
        compiler_params=pltpu.CompilerParams(
            dimension_semantics=("arbitrary",) * len(grid), vmem_limit_bytes=limit
        ),
        cost_estimate=pl.CostEstimate(flops=flops, bytes_accessed=size, transcendentals=0),
        name=name,
    )

    def placed(array, spec):
        space = pltpu.VMEM if spec.memory_space == pltpu.VMEM else pltpu.HBM
        return pltpu.with_memory_space_constraint(array, space)

    def with_places(*args):
        arrays = [placed(a, spec) for a, spec in zip(args[prefetch:], in_specs)]
        return run(*args[:prefetch], *arrays)

    return with_places


def onehot_rows(codes_row, entries):
    entry = lax.broadcasted_iota(jnp.int32, (entries, codes_row.shape[1]), 0)
    return jnp.where(entry == codes_row, 1.0, 0.0).astype(BF16)


def row_at(ref, index):
    place = lax.broadcasted_iota(jnp.int32, ref.shape, 0)
    return jnp.sum(jnp.where(place == index, ref[...], 0), axis=0, keepdims=True)


def fold(array):
    rows, lanes = array.shape
    return jnp.sum(array.reshape(rows // 8, 8, lanes), axis=0)


def fold_max(array):
    rows, lanes = array.shape
    return jnp.max(array.reshape(rows // 8, 8, lanes), axis=0)


def sum_kernel(codes_ref, value_ref, send_ref, first_ref, first_count_ref):
    heads, entries, width = first_ref.shape
    slices = entries // HALF
    blocks = value_ref.shape[0] // BLOCK
    ones = jnp.ones((BLOCK, TILE), BF16)
    lines = []
    for h in range(heads):
        total = None
        for b in range(blocks):
            span = slice(b * BLOCK, (b + 1) * BLOCK)
            hot = onehot_rows(codes_ref[h : h + 1, span], entries)
            columns = value_ref[span, h * width : (h + 1) * width]
            part = dot(hot, jnp.concatenate([columns, ones], axis=1))
            if b == 0:
                first_ref[h] = part[:, :width]
                for i in range(entries // TILE):
                    rows = slice(i * TILE, (i + 1) * TILE)
                    first_count_ref[h, :, rows] = part[rows, width:].T[:1]
            total = part if b == 0 else total + part
        for k in range(slices):
            rows = slice(k * HALF, (k + 1) * HALF)
            send_ref[h * slices + k, :HALF, :] = total[rows, :width].astype(BF16)
        for i in range(entries // TILE):
            lines.append(total[i * TILE : (i + 1) * TILE, width:].T[:1])
    lines = jnp.concatenate(lines, axis=0)
    high = jnp.floor(lines * (1.0 / 256.0))
    digits = jnp.concatenate([high, lines - high * 256.0], axis=0).astype(BF16)
    for k in range(heads * slices):
        send_ref[k, HALF:, :] = digits


def own_sums(codes, values, heads, entries):
    width = values.shape[1] // heads
    slices = entries // HALF
    whole = lambda i: (0, 0, 0)
    return call(
        sum_kernel, "own_sums", (1,),
        [
            pl.BlockSpec(codes.shape, lambda i: (0, 0)),
            pl.BlockSpec(values.shape, lambda i: (0, 0)),
        ],
        [
            ((heads * slices, ROWS, TILE), BF16, pl.BlockSpec((heads * slices, ROWS, TILE), whole)),
            ((heads, entries, width), F32, pl.BlockSpec((heads, entries, width), whole)),
            ((heads, 1, entries), F32, pl.BlockSpec((heads, 1, entries), whole)),
        ],

    )(codes, values)


def prefix_kernel(me_ref, in_ref, first_ref, out_ref, count_ref):
    running = jnp.zeros(out_ref.shape[1:], F32)
    lines = (ROWS - HALF) // 2
    number = jnp.zeros((lines, TILE), F32)
    for d in range(in_ref.shape[0]):
        out_ref[d] = running.astype(BF16)
        running = running + in_ref[d, :HALF, :].astype(F32)
        digits = in_ref[d, HALF:, :].astype(F32)
        digits = digits[:lines] * 256.0 + digits[lines:]
        number = number + jnp.where(d < me_ref[0], digits, 0.0)
    heads = first_ref.shape[0]
    per = lines // heads
    for h in range(heads):
        for i in range(per):
            line = number[h * per + i : h * per + i + 1]
            columns = slice(i * TILE, (i + 1) * TILE)
            count_ref[0, h, :, columns] = line
            count_ref[1, h, :, columns] = line + first_ref[h, :, columns]


def prefix_scan(me, pieces, first):
    count = pieces.shape[0]
    heads, _, entries = first.shape
    whole = lambda i, *_: (0, 0, 0)
    shape = (2, heads, 1, entries)
    return call(
        prefix_kernel, "prefix_scan", (1,),
        [IN_VMEM, pl.BlockSpec(first.shape, whole)],
        [
            ((count, HALF, TILE), BF16, pl.BlockSpec((count, HALF, TILE), whole)),
            (shape, F32, pl.BlockSpec(shape, lambda i, *_: (0, 0, 0, 0))),
        ],
        prefetch=1
    )(me, pieces, first)


def suffix_kernel(in_ref, out_ref):
    running = jnp.zeros((HALF, TILE), F32)
    total = jnp.zeros((HALF, TILE), F32)
    for d in reversed(range(in_ref.shape[0])):
        out_ref[d, :HALF, :] = running.astype(BF16)
        running = running + in_ref[d, :HALF, :].astype(F32)
        total = total + in_ref[d, HALF:, :].astype(F32)
    low = total.astype(BF16)
    for d in range(in_ref.shape[0]):
        out_ref[d, HALF:, :] = low


def suffix_scan(pieces):
    spec = pl.BlockSpec(pieces.shape, lambda i: (0, 0, 0))
    return call(
        suffix_kernel, "suffix_scan", (1,), [IN_VMEM], [(pieces.shape, BF16, spec)], size=2 << 20
    )(pieces)[0]


def count_columns(number):
    tiles = [
        jnp.broadcast_to(number[:, i * TILE : (i + 1) * TILE], (TILE, TILE)).T
        for i in range(number.shape[1] // TILE)
    ]
    return jnp.concatenate(tiles, axis=0)


def forward_kernel(codes_ref, query_ref, book_ref, book_t_ref, count_ref,
                   low_ref, keys_ref, rows_k, counts, scores):
    entries, width = book_ref.shape[1:]
    head = pl.program_id(0)
    entry_tiles = entries // TILE
    factor = width ** -0.5 * math.log2(math.e)
    causal = lax.broadcasted_iota(jnp.int32, (TILE, TILE), 1) >= lax.broadcasted_iota(
        jnp.int32, (TILE, TILE), 0
    )
    parts = BLOCK // PART
    blocks = low_ref.shape[0]

    codes_row = row_at(codes_ref, head)

    def prepare(b):
        keys_t = dot(
            book_t_ref[0], onehot_rows(codes_row[:, b * BLOCK : (b + 1) * BLOCK], entries)
        )
        keys_ref[b, 0] = keys_t.astype(BF16)
        rows_k[b, :entries, :] = book_ref[0]
        rows_k[b, entries:, :] = keys_t.T.astype(BF16)
        counts[b] = count_columns(count_ref[b, 0])

    def multiply(b, n):
        used = entries + PART * (n + 1)
        at = b * BLOCK + n * PART
        scores[b, n, :used, :] = dot_nt(rows_k[b, :used, :], query_ref[at : at + PART, :])

    def soften(b, n):
        used = entries + PART * (n + 1)
        for j in range(PART // TILE):
            columns = slice(j * TILE, (j + 1) * TILE)
            target = slice(n * PART + j * TILE, n * PART + (j + 1) * TILE)
            pieces = range(entry_tiles + 2 * n + j + 1)
            top = jnp.full((8, TILE), -jnp.inf, F32)
            for i in pieces:
                rows = slice(i * TILE, (i + 1) * TILE)
                piece = scores[b, n, rows, columns]
                if i < entry_tiles:
                    piece = jnp.where(counts[b, rows, :] > 0.0, piece, -jnp.inf)
                    scores[b, n, rows, columns] = piece
                elif i == pieces[-1]:
                    piece = jnp.where(causal, piece, -jnp.inf)
                    scores[b, n, rows, columns] = piece
                top = jnp.maximum(top, fold_max(piece))
            top = jnp.max(top, axis=0, keepdims=True)
            total = jnp.zeros((8, TILE), F32)
            for i in pieces:
                rows = slice(i * TILE, (i + 1) * TILE)
                piece = jnp.exp2((scores[b, n, rows, columns] - top) * factor)
                scores[b, n, rows, columns] = piece
                if i < entry_tiles:
                    piece = piece * counts[b, rows, :]
                total = total + fold(piece)
            inverse = 1.0 / jnp.sum(total, axis=0, keepdims=True)
            for i in pieces:
                rows = slice(i * TILE, (i + 1) * TILE)
                low_ref[b, 0, rows, target] = (scores[b, n, rows, columns] * inverse).astype(BF16)
            if j == 0:
                low_ref[b, 0, used - TILE : used, target] = jnp.zeros((TILE, TILE), BF16)

    order = [(b, n) for b in range(blocks) for n in range(parts)]
    for b in range(blocks):
        prepare(b)
    multiply(*order[0])
    for k, item in enumerate(order):
        if k + 1 < len(order):
            multiply(*order[k + 1])
        soften(*item)


def forward(codes, queries, book, book_t, counts):
    heads, entries, width = book.shape
    tokens = queries.shape[0]
    blocks = tokens // BLOCK
    both = entries + BLOCK
    by_head = lambda h: (h, 0, 0)
    in_blocks = lambda h: (0, h, 0, 0)
    return call(
        forward_kernel, "forward", (heads,),
        [
            pl.BlockSpec(codes.shape, lambda h: (0, 0)),
            pl.BlockSpec((tokens, width), lambda h: (0, h)),
            pl.BlockSpec((1, entries, width), by_head),
            pl.BlockSpec((1, width, entries), by_head),
            pl.BlockSpec((blocks, 1, 1, entries), in_blocks),
        ],
        [
            ((blocks, heads, both, BLOCK), BF16, pl.BlockSpec((blocks, 1, both, BLOCK), in_blocks)),
            ((blocks, heads, width, BLOCK), BF16, pl.BlockSpec((blocks, 1, width, BLOCK), in_blocks)),
        ],
        [
            pltpu.VMEM((blocks, both, width), BF16),
            pltpu.VMEM((blocks, entries, TILE), F32),
            pltpu.VMEM((blocks, 2, both, PART), F32),
        ],

    )(codes, queries, book, book_t, counts)


def backward_kernel(me_ref, core_ref, own_hbm, left_ref, right_ref, far0_ref, far1_ref, weight_hbm,
                    codes_ref, query_ref, value_ref, probs_ref, keys_ref, book_t_ref,
                    prefix_ref, count_ref, first_ref,
                    grad_query_ref, local_ref, part_ref, give_ref, keep_ref,
                    dout, hot, rows_v, counts, grads, score_grad, key_grad, wide_t, own_ref,
                    weight_ref, sems):
    width, entries = book_t_ref.shape[1:]
    entry_tiles = entries // TILE
    parts = BLOCK // PART
    blocks = probs_ref.shape[0]
    scale = width ** -0.5
    step = pl.program_id(0)
    head = lax.rem(step + 2 - 2 * core_ref[0], 4)

    def chunk(offset):
        columns = own_ref.shape[1]
        at = lax.rem(me_ref[0] + offset, 4) * columns
        return weight_ref[:, pl.ds(pl.multiple_of(at, columns), columns)]

    moves = [
        pltpu.make_async_copy(weight_hbm, weight_ref, sems.at[0]),
        pltpu.make_async_copy(own_hbm, own_ref, sems.at[1]),
    ]

    @pl.when(step == 0)
    def _():
        for move in moves:
            move.start()

    codes_row = row_at(codes_ref, head)

    def prepare(b):
        hot[b] = onehot_rows(codes_row[:, b * BLOCK : (b + 1) * BLOCK], entries)
        wide_t[b, :, :entries] = book_t_ref[0]
        wide_t[b, :, entries:] = keys_ref[b, 0]
        slices = entries // HALF
        sums = prefix_ref[pl.ds(head * slices, slices)].reshape(entries, width)
        if b > 0:
            sums = (sums.astype(F32) + first_ref[0]).astype(BF16)
        rows_v[b, :entries, :] = sums
        rows_v[b, entries:, :] = value_ref[b * BLOCK : (b + 1) * BLOCK, :]
        counts[b] = count_columns(count_ref[b, 0])

    def multiply(b, n):
        used = entries + PART * (n + 1)
        at = b * BLOCK + n * PART
        grads[b, n, :used, :] = dot_nt(rows_v[b, :used, :], dout[head, at : at + PART, :])

    def combine(b, n):
        used = entries + PART * (n + 1)
        for j in range(PART // TILE):
            columns = slice(j * TILE, (j + 1) * TILE)
            source = slice(n * PART + j * TILE, n * PART + (j + 1) * TILE)
            pieces = range(entry_tiles + 2 * n + j + 1)
            delta = jnp.zeros((8, TILE), F32)
            for i in pieces:
                rows = slice(i * TILE, (i + 1) * TILE)
                delta = delta + fold(
                    probs_ref[b, 0, rows, source].astype(F32) * grads[b, n, rows, columns]
                )
            delta = jnp.sum(delta, axis=0, keepdims=True) * scale
            for i in pieces:
                rows = slice(i * TILE, (i + 1) * TILE)
                shift = delta
                if i < entry_tiles:
                    shift = delta * counts[b, rows, :]
                piece = grads[b, n, rows, columns] * scale - shift
                piece = probs_ref[b, 0, rows, source].astype(F32) * piece
                score_grad[b, n, rows, columns] = piece.astype(BF16)
            if j == 0:
                score_grad[b, n, used - TILE : used, columns] = jnp.zeros((TILE, TILE), BF16)

    sums_k = [[None] * parts for _ in range(blocks)]
    sums_v = [[None] * parts for _ in range(blocks)]

    def outputs(b, n):
        used = entries + PART * (n + 1)
        at = b * BLOCK + n * PART
        span = slice(at, at + PART)
        sums_v[b][n] = dot(probs_ref[b, 0, :used, n * PART : (n + 1) * PART], dout[head, span, :])
        sums_k[b][n] = dot(score_grad[b, n, :used, :], query_ref[span, :])
        grad_t = dot(wide_t[b, :, :used], score_grad[b, n, :used, :])
        grad_query_ref[span, :] = grad_t.T.astype(BF16)

    order = [(b, n) for b in range(blocks) for n in range(parts)]
    for b in range(blocks):
        prepare(b)

    @pl.when(step == 0)
    def _():
        for move in moves:
            move.wait()
        count = own_ref.shape[0] // PART
        for n in range(count):
            span = slice(n * PART, (n + 1) * PART)
            total = dot_nt(own_ref[span, :], chunk(0)) + dot_nt(left_ref[span, :], chunk(3))
            total = total + dot_nt(right_ref[span, :], chunk(1))
            if n < count // 2:
                far = far0_ref[span, :]
            else:
                far = far1_ref[(n - count // 2) * PART : (n + 1 - count // 2) * PART, :]
            total = total + dot_nt(far, chunk(2))
            for h in range(dout.shape[0]):
                dout[h, span, :] = total[:, h * width : (h + 1) * width].astype(BF16)

    multiply(*order[0])
    code = None
    part = None
    middle = entries + PART
    for k, item in enumerate(order):
        if k + 1 < len(order):
            multiply(*order[k + 1])
        combine(*item)
        outputs(*item)
        b, n = item
        if n == parts - 1:
            first, last = sums_v[b]
            at = b * BLOCK
            local_ref[at : at + PART, :] = first[entries:] + last[entries:middle]
            local_ref[at + PART : at + BLOCK, :] = last[middle:]
            mine = first[:entries] + last[:entries]
            if b == blocks - 1:
                part_ref[0] = mine
            part = mine if b == 0 else part + mine
            first, last = sums_k[b]
            key_grad[b, :PART, :] = (first[entries:] + last[entries:middle]).astype(BF16)
            key_grad[b, PART:, :] = last[middle:].astype(BF16)
            mine = first[:entries] + last[:entries] + dot(hot[b], key_grad[b])
            code = mine if b == 0 else code + mine

    def write(ref):
        for k in range(entries // HALF):
            rows = slice(k * HALF, (k + 1) * HALF)
            ref[k, :HALF, :] = part[rows].astype(BF16)
            ref[k, HALF:, :] = code[rows].astype(BF16)

    @pl.when(step < 2)
    def _():
        write(give_ref)

    @pl.when(step >= 2)
    def _():
        write(keep_ref)


def backward(me, core, pieces, weight, codes, queries, values, probs, keys, book_t, prefix, counts,
             first):
    heads, width, entries = book_t.shape
    tokens = queries.shape[0]
    blocks = tokens // BLOCK
    both = entries + BLOCK
    slices = entries // HALF
    at = lambda s, core: lax.rem(s + 2 - 2 * core[0], 4)
    by_head = lambda s, _, core: (at(s, core), 0, 0)
    in_blocks = lambda s, _, core: (0, at(s, core), 0, 0)
    rows_of = pl.BlockSpec((tokens, width), lambda s, _, core: (0, at(s, core)))
    shape = (slices, 2 * HALF, width)
    both_heads = (2 * slices, 2 * HALF, width)
    per_head = pl.BlockSpec((1, entries, width), by_head)

    anywhere = pl.BlockSpec(memory_space=pl.ANY)
    in_specs = [anywhere] + [IN_VMEM] * (len(pieces) - 1) + [anywhere]
    in_specs += [
        pl.BlockSpec(codes.shape, lambda h, *_: (0, 0)),
        rows_of,
        rows_of,
        pl.BlockSpec((blocks, 1, both, BLOCK), in_blocks),
        pl.BlockSpec((blocks, 1, width, BLOCK), in_blocks),
        pl.BlockSpec((1, width, entries), by_head),
        IN_VMEM,
        pl.BlockSpec((blocks, 1, 1, entries), in_blocks),
        per_head,
    ]
    outs = [
        (queries.shape, BF16, rows_of),
        (queries.shape, F32, rows_of),
        ((heads, entries, width), F32, per_head),
        (both_heads, BF16, pl.BlockSpec(shape, lambda s, *_: (jnp.minimum(s, 1), 0, 0))),
        (both_heads, BF16, pl.BlockSpec(shape, lambda s, *_: (jnp.maximum(s - 2, 0), 0, 0))),
    ]
    return call(
        backward_kernel, "backward", (heads,), in_specs, outs,
        [
            pltpu.VMEM((heads, tokens, width), BF16),
            pltpu.VMEM((blocks, entries, BLOCK), BF16),
            pltpu.VMEM((blocks, both, width), BF16),
            pltpu.VMEM((blocks, entries, TILE), F32),
            pltpu.VMEM((blocks, 2, both, PART), F32),
            pltpu.VMEM((blocks, 2, both, PART), BF16),
            pltpu.VMEM((blocks, BLOCK, width), BF16),
            pltpu.VMEM((blocks, width, both), BF16),
            pltpu.VMEM(pieces[0].shape, BF16),
            pltpu.VMEM(weight.shape, BF16),
            pltpu.SemaphoreType.DMA((2,)),
        ],
        prefetch=2, flops=20 << 30, size=24 << 20,
    )(me, core, *pieces, weight, codes, queries, values, probs, keys, book_t, prefix, counts,
      first)


def finish_kernel(own, refs):
    me_ref, codes_ref, local_ref, later_ref = refs[:4]
    if own:
        kept_ref, part_ref = refs[4:6]
    else:
        part_ref = refs[4]
    out_ref, book_ref = refs[-2:]
    entries, width = part_ref.shape[1:]
    step = pl.program_id(0)
    head = 2 * me_ref[0] + step if own else 2 - 2 * me_ref[0] + step
    codes_row = row_at(codes_ref, head)
    mine = pl.ds(step * (entries // HALF), entries // HALF)
    later = later_ref[mine, :HALF, :].astype(F32)
    if own:
        later = later + jnp.where(me_ref[0] == 0, kept_ref[mine, :HALF, :].astype(F32), 0.0)
    later = later.reshape(entries, width)
    book_ref[0] = later_ref[mine, HALF:, :].reshape(entries, width).astype(F32)
    tokens = local_ref.shape[0]
    tables = [later.astype(BF16)] * (tokens // BLOCK)
    tables[0] = (later + part_ref[0]).astype(BF16)
    levels = lax.broadcasted_iota(jnp.int32, (TILE, TILE), 1)
    for i in range(tokens // TILE):
        rows = slice(i * TILE, (i + 1) * TILE)
        column = jnp.broadcast_to(codes_row[:, rows], (TILE, TILE)).T
        hot = jnp.concatenate(
            [
                jnp.where(levels + k * TILE == column, 1.0, 0.0).astype(BF16)
                for k in range(entries // TILE)
            ],
            axis=1,
        )
        out_ref[rows, :] = (local_ref[rows, :] + dot(hot, tables[i * TILE // BLOCK])).astype(BF16)


def finish(own, core, codes, local, later, part, extra):
    heads, entries, width = part.shape
    tokens = local.shape[0]
    at = lambda s, core: (2 * core[0] if own else 2 - 2 * core[0]) + s
    by_head = lambda s, core: (at(s, core), 0, 0)
    rows_of = pl.BlockSpec((tokens, width), lambda s, core: (0, at(s, core)))
    per_head = pl.BlockSpec((1, entries, width), by_head)
    in_specs = [pl.BlockSpec(codes.shape, lambda s, *_: (0, 0)), rows_of, IN_VMEM]
    if own:
        in_specs += [IN_VMEM, per_head]
        args = (*extra, part)
    else:
        in_specs += [per_head] + [pl.BlockSpec(memory_space=pl.ANY)] * 2
        args = (part, *extra)
    return call(
        lambda *refs: finish_kernel(own, refs), "finish_own" if own else "finish_other", (2,),
        in_specs,
        [(local.shape, BF16, rows_of), (part.shape, F32, per_head)],
        aliases=None if own else {5: 0, 6: 1}, prefetch=1, flops=1 << 30, size=8 << 20,
    )(core, codes, local, later, *args)


def ring_pieces(array):
    count = lax.axis_size("head")
    up = [(i, (i + 1) % count) for i in range(count)]
    down = [(i, (i - 1) % count) for i in range(count)]
    left = lax.ppermute(array, "head", up)
    right = lax.ppermute(array, "head", down)
    half = array.shape[0] // 2
    far = lax.ppermute(left[:half], "head", up), lax.ppermute(right[half:], "head", down)
    return array, left, right, *far


def per_device(queries, values, codes, codebook, out_weight, grad_out):
    heads, entries, width = codebook.shape
    exchange = functools.partial(
        lax.all_to_all, axis_name=("chip", "core"), split_axis=0, concat_axis=0, tiled=True
    )
    between_chips = functools.partial(
        lax.all_to_all, axis_name="chip", split_axis=0, concat_axis=0, tiled=True
    )
    other_core = functools.partial(lax.ppermute, axis_name="core", perm=[(0, 1), (1, 0)])
    core = lax.axis_index("core").astype(jnp.int32)
    me_seq = lax.axis_index(("chip", "core")).astype(jnp.int32).reshape(1)
    me = lax.axis_index("head").astype(jnp.int32).reshape(1)
    core_at = core.reshape(1)
    pieces = ring_pieces(grad_out)
    codes = codes.T
    book_t = jnp.swapaxes(codebook, 1, 2)
    send, first, first_count = own_sums(codes, values, heads, entries)
    prefix, counts = prefix_scan(me_seq, exchange(send), first_count)
    prefix = exchange(prefix)
    probs, keys = forward(codes, queries, codebook, book_t, counts)
    grad_query, local, part, give, keep = backward(
        me, core_at, pieces, out_weight, codes, queries, values, probs, keys, book_t, prefix, counts, first
    )
    got = other_core(give)
    chip = (keep.astype(F32) + got.astype(F32)).astype(BF16)
    later = between_chips(suffix_scan(between_chips(chip)))
    is_value = lax.broadcasted_iota(jnp.int32, later.shape, 1) < HALF
    mine = jnp.where(is_value & (core == 1), keep.astype(F32), 0.0)
    theirs = other_core((later.astype(F32) + mine).astype(BF16))
    results = finish(True, core_at, codes, local, later, part, (got,))
    grad_values, grad_book = finish(False, core_at, codes, local, theirs, part, results)
    return grad_query, grad_values, grad_book


def solution(mesh):
    finer = Mesh(mesh.devices.reshape(-1, 2, mesh.shape["head"]), ("chip", "core", "head"))
    rows = P(("chip", "core"), "head")
    return jax.shard_map(
        per_device,
        mesh=finer,
        in_specs=(rows, rows, rows, P("head", None, None), P("head", None), rows),
        out_specs=(rows, rows, P("head", None, None)),
        check_vma=False,
    )
```

```python
import functools
import math

import jax
import jax.numpy as jnp
from jax import lax
from jax.experimental import pallas as pl
from jax.experimental.pallas import tpu as pltpu
from jax.sharding import Mesh
from jax.sharding import PartitionSpec as P

BLOCK = 512
PART = 256
TILE = 128
HALF = 64
ROWS = 96
F32 = jnp.float32
BF16 = jnp.bfloat16
VMEM_LIMIT = 44 << 20
IN_VMEM = pl.BlockSpec(memory_space=pltpu.VMEM)


def dot(left, right):
    return lax.dot_general(left, right, (((1,), (0,)), ((), ())), preferred_element_type=F32)


def dot_nt(left, right):
    return lax.dot_general(left, right, (((1,), (1,)), ((), ())), preferred_element_type=F32)


def call(kernel, name, grid, in_specs, outs, scratch=(), aliases=None, prefetch=0, flops=0, size=0,
         limit=VMEM_LIMIT):
    run = pl.pallas_call(
        kernel,
        grid_spec=pltpu.PrefetchScalarGridSpec(
            num_scalar_prefetch=prefetch,
            grid=grid,
            in_specs=in_specs,
            out_specs=[spec for _, _, spec in outs],
            scratch_shapes=list(scratch),
        ),
        out_shape=[pltpu.HBM(shape, dtype) for shape, dtype, _ in outs],
        input_output_aliases=aliases or {},
        compiler_params=pltpu.CompilerParams(
            dimension_semantics=("arbitrary",) * len(grid), vmem_limit_bytes=limit
        ),
        cost_estimate=pl.CostEstimate(flops=flops, bytes_accessed=size, transcendentals=0),
        name=name,
    )

    def placed(array, spec):
        space = pltpu.VMEM if spec.memory_space == pltpu.VMEM else pltpu.HBM
        return pltpu.with_memory_space_constraint(array, space)

    def with_places(*args):
        arrays = [placed(a, spec) for a, spec in zip(args[prefetch:], in_specs)]
        return run(*args[:prefetch], *arrays)

    return with_places


def onehot_rows(codes_row, entries):
    entry = lax.broadcasted_iota(jnp.int32, (entries, codes_row.shape[1]), 0)
    return jnp.where(entry == codes_row, 1.0, 0.0).astype(BF16)


def row_at(ref, index):
    place = lax.broadcasted_iota(jnp.int32, ref.shape, 0)
    return jnp.sum(jnp.where(place == index, ref[...], 0), axis=0, keepdims=True)


def fold(array):
    rows, lanes = array.shape
    return jnp.sum(array.reshape(rows // 8, 8, lanes), axis=0)


def fold_max(array):
    rows, lanes = array.shape
    return jnp.max(array.reshape(rows // 8, 8, lanes), axis=0)


def sum_kernel(codes_ref, value_ref, send_ref, first_ref, first_count_ref):
    heads, entries, width = first_ref.shape
    slices = entries // HALF
    blocks = value_ref.shape[0] // BLOCK
    ones = jnp.ones((BLOCK, TILE), BF16)
    lines = []
    for h in range(heads):
        total = None
        for b in range(blocks):
            span = slice(b * BLOCK, (b + 1) * BLOCK)
            hot = onehot_rows(codes_ref[h : h + 1, span], entries)
            columns = value_ref[span, h * width : (h + 1) * width]
            part = dot(hot, jnp.concatenate([columns, ones], axis=1))
            if b == 0:
                first_ref[h] = part[:, :width]
                for i in range(entries // TILE):
                    rows = slice(i * TILE, (i + 1) * TILE)
                    first_count_ref[h, :, rows] = part[rows, width:].T[:1]
            total = part if b == 0 else total + part
        for k in range(slices):
            rows = slice(k * HALF, (k + 1) * HALF)
            send_ref[h * slices + k, :HALF, :] = total[rows, :width].astype(BF16)
        for i in range(entries // TILE):
            lines.append(total[i * TILE : (i + 1) * TILE, width:].T[:1])
    lines = jnp.concatenate(lines, axis=0)
    high = jnp.floor(lines * (1.0 / 256.0))
    digits = jnp.concatenate([high, lines - high * 256.0], axis=0).astype(BF16)
    for k in range(heads * slices):
        send_ref[k, HALF:, :] = digits


def own_sums(codes, values, heads, entries):
    width = values.shape[1] // heads
    slices = entries // HALF
    whole = lambda i: (0, 0, 0)
    return call(
        sum_kernel, "own_sums", (1,),
        [
            pl.BlockSpec(codes.shape, lambda i: (0, 0)),
            pl.BlockSpec(values.shape, lambda i: (0, 0)),
        ],
        [
            ((heads * slices, ROWS, TILE), BF16, pl.BlockSpec((heads * slices, ROWS, TILE), whole)),
            ((heads, entries, width), F32, pl.BlockSpec((heads, entries, width), whole)),
            ((heads, 1, entries), F32, pl.BlockSpec((heads, 1, entries), whole)),
        ],

    )(codes, values)


def prefix_kernel(me_ref, in_ref, first_ref, out_ref, count_ref):
    running = jnp.zeros(out_ref.shape[1:], F32)
    lines = (ROWS - HALF) // 2
    number = jnp.zeros((lines, TILE), F32)
    for d in range(in_ref.shape[0]):
        out_ref[d] = running.astype(BF16)
        running = running + in_ref[d, :HALF, :].astype(F32)
        digits = in_ref[d, HALF:, :].astype(F32)
        digits = digits[:lines] * 256.0 + digits[lines:]
        number = number + jnp.where(d < me_ref[0], digits, 0.0)
    heads = first_ref.shape[0]
    per = lines // heads
    for h in range(heads):
        for i in range(per):
            line = number[h * per + i : h * per + i + 1]
            columns = slice(i * TILE, (i + 1) * TILE)
            count_ref[0, h, :, columns] = line
            count_ref[1, h, :, columns] = line + first_ref[h, :, columns]


def prefix_scan(me, pieces, first):
    count = pieces.shape[0]
    heads, _, entries = first.shape
    whole = lambda i, *_: (0, 0, 0)
    shape = (2, heads, 1, entries)
    return call(
        prefix_kernel, "prefix_scan", (1,),
        [IN_VMEM, pl.BlockSpec(first.shape, whole)],
        [
            ((count, HALF, TILE), BF16, pl.BlockSpec((count, HALF, TILE), whole)),
            (shape, F32, pl.BlockSpec(shape, lambda i, *_: (0, 0, 0, 0))),
        ],
        prefetch=1
    )(me, pieces, first)


def suffix_kernel(in_ref, out_ref):
    running = jnp.zeros((HALF, TILE), F32)
    total = jnp.zeros((HALF, TILE), F32)
    for d in reversed(range(in_ref.shape[0])):
        out_ref[d, :HALF, :] = running.astype(BF16)
        running = running + in_ref[d, :HALF, :].astype(F32)
        total = total + in_ref[d, HALF:, :].astype(F32)
    low = total.astype(BF16)
    for d in range(in_ref.shape[0]):
        out_ref[d, HALF:, :] = low


def suffix_scan(pieces):
    spec = pl.BlockSpec(pieces.shape, lambda i: (0, 0, 0))
    return call(
        suffix_kernel, "suffix_scan", (1,), [IN_VMEM], [(pieces.shape, BF16, spec)], size=2 << 20
    )(pieces)[0]


def count_columns(number):
    tiles = [
        jnp.broadcast_to(number[:, i * TILE : (i + 1) * TILE], (TILE, TILE)).T
        for i in range(number.shape[1] // TILE)
    ]
    return jnp.concatenate(tiles, axis=0)


def forward_kernel(codes_ref, query_ref, book_ref, count_ref,
                   low_ref, keys_ref, book_t_ref, rows_k, counts, scores):
    entries, width = book_ref.shape[1:]
    head = pl.program_id(0)
    entry_tiles = entries // TILE
    factor = width ** -0.5 * math.log2(math.e)
    causal = lax.broadcasted_iota(jnp.int32, (TILE, TILE), 1) >= lax.broadcasted_iota(
        jnp.int32, (TILE, TILE), 0
    )
    parts = BLOCK // PART
    blocks = low_ref.shape[0]

    codes_row = row_at(codes_ref, head)
    book_t_ref[0] = book_ref[0].astype(F32).T.astype(BF16)

    def prepare(b):
        keys_t = dot(
            book_t_ref[0], onehot_rows(codes_row[:, b * BLOCK : (b + 1) * BLOCK], entries)
        )
        keys_ref[b, 0] = keys_t.astype(BF16)
        rows_k[b, :entries, :] = book_ref[0]
        rows_k[b, entries:, :] = keys_t.T.astype(BF16)
        counts[b] = count_columns(count_ref[b, 0])

    def multiply(b, n):
        used = entries + PART * (n + 1)
        at = b * BLOCK + n * PART
        scores[b, n, :used, :] = dot_nt(rows_k[b, :used, :], query_ref[at : at + PART, :])

    def soften(b, n):
        used = entries + PART * (n + 1)
        for j in range(PART // TILE):
            columns = slice(j * TILE, (j + 1) * TILE)
            target = slice(n * PART + j * TILE, n * PART + (j + 1) * TILE)
            pieces = range(entry_tiles + 2 * n + j + 1)
            top = jnp.full((8, TILE), -jnp.inf, F32)
            for i in pieces:
                rows = slice(i * TILE, (i + 1) * TILE)
                piece = scores[b, n, rows, columns]
                if i < entry_tiles:
                    piece = jnp.where(counts[b, rows, :] > 0.0, piece, -jnp.inf)
                    scores[b, n, rows, columns] = piece
                elif i == pieces[-1]:
                    piece = jnp.where(causal, piece, -jnp.inf)
                    scores[b, n, rows, columns] = piece
                top = jnp.maximum(top, fold_max(piece))
            top = jnp.max(top, axis=0, keepdims=True)
            total = jnp.zeros((8, TILE), F32)
            for i in pieces:
                rows = slice(i * TILE, (i + 1) * TILE)
                piece = jnp.exp2((scores[b, n, rows, columns] - top) * factor)
                scores[b, n, rows, columns] = piece
                if i < entry_tiles:
                    piece = piece * counts[b, rows, :]
                total = total + fold(piece)
            inverse = 1.0 / jnp.sum(total, axis=0, keepdims=True)
            for i in pieces:
                rows = slice(i * TILE, (i + 1) * TILE)
                low_ref[b, 0, rows, target] = (scores[b, n, rows, columns] * inverse).astype(BF16)
            if j == 0:
                low_ref[b, 0, used - TILE : used, target] = jnp.zeros((TILE, TILE), BF16)

    order = [(b, n) for b in range(blocks) for n in range(parts)]
    for b in range(blocks):
        prepare(b)
    multiply(*order[0])
    for k, item in enumerate(order):
        if k + 1 < len(order):
            multiply(*order[k + 1])
        soften(*item)


def forward(codes, queries, book, counts):
    heads, entries, width = book.shape
    tokens = queries.shape[0]
    blocks = tokens // BLOCK
    both = entries + BLOCK
    by_head = lambda h: (h, 0, 0)
    in_blocks = lambda h: (0, h, 0, 0)
    return call(
        forward_kernel, "forward", (heads,),
        [
            pl.BlockSpec(codes.shape, lambda h: (0, 0)),
            pl.BlockSpec((tokens, width), lambda h: (0, h)),
            pl.BlockSpec((1, entries, width), by_head),
            pl.BlockSpec((blocks, 1, 1, entries), in_blocks),
        ],
        [
            ((blocks, heads, both, BLOCK), BF16, pl.BlockSpec((blocks, 1, both, BLOCK), in_blocks)),
            ((blocks, heads, width, BLOCK), BF16, pl.BlockSpec((blocks, 1, width, BLOCK), in_blocks)),
            ((heads, width, entries), BF16, pl.BlockSpec((1, width, entries), by_head)),
        ],
        [
            pltpu.VMEM((blocks, both, width), BF16),
            pltpu.VMEM((blocks, entries, TILE), F32),
            pltpu.VMEM((blocks, 2, both, PART), F32),
        ],

    )(codes, queries, book, counts)


def backward_kernel(me_ref, core_ref, own_ref, left_ref, right_ref, far0_ref, far1_ref, weight_ref,
                    codes_ref, query_ref, value_ref, probs_ref, keys_ref, book_t_ref,
                    prefix_ref, count_ref, first_ref,
                    grad_query_ref, local_ref, part_ref, give_ref, keep_ref,
                    dout, hot, rows_v, counts, grads, score_grad, key_grad, wide_t):
    width, entries = book_t_ref.shape[1:]
    entry_tiles = entries // TILE
    parts = BLOCK // PART
    blocks = probs_ref.shape[0]
    scale = width ** -0.5
    step = pl.program_id(0)
    head = lax.rem(step + 2 - 2 * core_ref[0], 4)

    def chunk(offset):
        columns = own_ref.shape[1]
        at = lax.rem(me_ref[0] + offset, 4) * columns
        return weight_ref[:, pl.ds(pl.multiple_of(at, columns), columns)]

    codes_row = row_at(codes_ref, head)

    def prepare(b):
        hot[b] = onehot_rows(codes_row[:, b * BLOCK : (b + 1) * BLOCK], entries)
        wide_t[b, :, :entries] = book_t_ref[0]
        wide_t[b, :, entries:] = keys_ref[b, 0]
        slices = entries // HALF
        sums = prefix_ref[pl.ds(head * slices, slices)].reshape(entries, width)
        if b > 0:
            sums = (sums.astype(F32) + first_ref[0]).astype(BF16)
        rows_v[b, :entries, :] = sums
        rows_v[b, entries:, :] = value_ref[b * BLOCK : (b + 1) * BLOCK, :]
        counts[b] = count_columns(count_ref[b, 0])

    def multiply(b, n):
        used = entries + PART * (n + 1)
        at = b * BLOCK + n * PART
        grads[b, n, :used, :] = dot_nt(rows_v[b, :used, :], dout[head, at : at + PART, :])

    def combine(b, n):
        used = entries + PART * (n + 1)
        for j in range(PART // TILE):
            columns = slice(j * TILE, (j + 1) * TILE)
            source = slice(n * PART + j * TILE, n * PART + (j + 1) * TILE)
            pieces = range(entry_tiles + 2 * n + j + 1)
            delta = jnp.zeros((8, TILE), F32)
            for i in pieces:
                rows = slice(i * TILE, (i + 1) * TILE)
                delta = delta + fold(
                    probs_ref[b, 0, rows, source].astype(F32) * grads[b, n, rows, columns]
                )
            delta = jnp.sum(delta, axis=0, keepdims=True) * scale
            for i in pieces:
                rows = slice(i * TILE, (i + 1) * TILE)
                shift = delta
                if i < entry_tiles:
                    shift = delta * counts[b, rows, :]
                piece = grads[b, n, rows, columns] * scale - shift
                piece = probs_ref[b, 0, rows, source].astype(F32) * piece
                score_grad[b, n, rows, columns] = piece.astype(BF16)
            if j == 0:
                score_grad[b, n, used - TILE : used, columns] = jnp.zeros((TILE, TILE), BF16)

    sums_k = [[None] * parts for _ in range(blocks)]
    sums_v = [[None] * parts for _ in range(blocks)]

    def outputs(b, n):
        used = entries + PART * (n + 1)
        at = b * BLOCK + n * PART
        span = slice(at, at + PART)
        sums_v[b][n] = dot(probs_ref[b, 0, :used, n * PART : (n + 1) * PART], dout[head, span, :])
        sums_k[b][n] = dot(score_grad[b, n, :used, :], query_ref[span, :])
        grad_t = dot(wide_t[b, :, :used], score_grad[b, n, :used, :])
        grad_query_ref[span, :] = grad_t.T.astype(BF16)

    order = [(b, n) for b in range(blocks) for n in range(parts)]
    for b in range(blocks):
        prepare(b)

    @pl.when(step == 0)
    def _():
        count = own_ref.shape[0] // PART
        for n in range(count):
            span = slice(n * PART, (n + 1) * PART)
            total = dot_nt(own_ref[span, :], chunk(0)) + dot_nt(left_ref[span, :], chunk(3))
            total = total + dot_nt(right_ref[span, :], chunk(1))
            if n < count // 2:
                far = far0_ref[span, :]
            else:
                far = far1_ref[(n - count // 2) * PART : (n + 1 - count // 2) * PART, :]
            total = total + dot_nt(far, chunk(2))
            for h in range(dout.shape[0]):
                dout[h, span, :] = total[:, h * width : (h + 1) * width].astype(BF16)

    multiply(*order[0])
    code = None
    part = None
    middle = entries + PART
    for k, item in enumerate(order):
        if k + 1 < len(order):
            multiply(*order[k + 1])
        combine(*item)
        outputs(*item)
        b, n = item
        if n == parts - 1:
            first, last = sums_v[b]
            at = b * BLOCK
            local_ref[at : at + PART, :] = first[entries:] + last[entries:middle]
            local_ref[at + PART : at + BLOCK, :] = last[middle:]
            mine = first[:entries] + last[:entries]
            if b == blocks - 1:
                part_ref[0] = mine
            part = mine if b == 0 else part + mine
            first, last = sums_k[b]
            key_grad[b, :PART, :] = (first[entries:] + last[entries:middle]).astype(BF16)
            key_grad[b, PART:, :] = last[middle:].astype(BF16)
            mine = first[:entries] + last[:entries] + dot(hot[b], key_grad[b])
            code = mine if b == 0 else code + mine

    def write(ref):
        for k in range(entries // HALF):
            rows = slice(k * HALF, (k + 1) * HALF)
            ref[k, :HALF, :] = part[rows].astype(BF16)
            ref[k, HALF:, :] = code[rows].astype(BF16)

    @pl.when(step < 2)
    def _():
        write(give_ref)

    @pl.when(step >= 2)
    def _():
        write(keep_ref)


def backward(me, core, pieces, weight, codes, queries, values, probs, keys, book_t, prefix, counts,
             first):
    heads, width, entries = book_t.shape
    tokens = queries.shape[0]
    blocks = tokens // BLOCK
    both = entries + BLOCK
    slices = entries // HALF
    at = lambda s, core: lax.rem(s + 2 - 2 * core[0], 4)
    by_head = lambda s, _, core: (at(s, core), 0, 0)
    in_blocks = lambda s, _, core: (0, at(s, core), 0, 0)
    rows_of = pl.BlockSpec((tokens, width), lambda s, _, core: (0, at(s, core)))
    shape = (slices, 2 * HALF, width)
    both_heads = (2 * slices, 2 * HALF, width)
    per_head = pl.BlockSpec((1, entries, width), by_head)

    anywhere = pl.BlockSpec(memory_space=pl.ANY)
    whole = lambda s, *_: (0, 0)
    in_specs = [pl.BlockSpec(pieces[0].shape, whole)] + [IN_VMEM] * (len(pieces) - 1)
    in_specs.append(pl.BlockSpec(weight.shape, whole))
    in_specs += [
        pl.BlockSpec(codes.shape, lambda h, *_: (0, 0)),
        rows_of,
        rows_of,
        pl.BlockSpec((blocks, 1, both, BLOCK), in_blocks),
        pl.BlockSpec((blocks, 1, width, BLOCK), in_blocks),
        pl.BlockSpec((1, width, entries), by_head),
        IN_VMEM,
        pl.BlockSpec((blocks, 1, 1, entries), in_blocks),
        per_head,
    ]
    outs = [
        (queries.shape, BF16, rows_of),
        (queries.shape, F32, rows_of),
        ((heads, entries, width), F32, per_head),
        (both_heads, BF16, pl.BlockSpec(shape, lambda s, *_: (jnp.minimum(s, 1), 0, 0))),
        (both_heads, BF16, pl.BlockSpec(shape, lambda s, *_: (jnp.maximum(s - 2, 0), 0, 0))),
    ]
    return call(
        backward_kernel, "backward", (heads,), in_specs, outs,
        [
            pltpu.VMEM((heads, tokens, width), BF16),
            pltpu.VMEM((blocks, entries, BLOCK), BF16),
            pltpu.VMEM((blocks, both, width), BF16),
            pltpu.VMEM((blocks, entries, TILE), F32),
            pltpu.VMEM((blocks, 2, both, PART), F32),
            pltpu.VMEM((blocks, 2, both, PART), BF16),
            pltpu.VMEM((blocks, BLOCK, width), BF16),
            pltpu.VMEM((blocks, width, both), BF16),
        ],
        prefetch=2, flops=20 << 30, size=24 << 20,
    )(me, core, *pieces, weight, codes, queries, values, probs, keys, book_t, prefix, counts,
      first)


def finish_kernel(own, refs):
    me_ref, codes_ref, local_ref, later_ref = refs[:4]
    if own:
        kept_ref, part_ref = refs[4:6]
    else:
        part_ref = refs[4]
    out_ref, book_ref = refs[-2:]
    entries, width = part_ref.shape[1:]
    step = pl.program_id(0)
    head = 2 * me_ref[0] + step if own else 2 - 2 * me_ref[0] + step
    codes_row = row_at(codes_ref, head)
    mine = pl.ds(step * (entries // HALF), entries // HALF)
    later = later_ref[mine, :HALF, :].astype(F32)
    if own:
        later = later + jnp.where(me_ref[0] == 0, kept_ref[mine, :HALF, :].astype(F32), 0.0)
    later = later.reshape(entries, width)
    book_ref[0] = later_ref[mine, HALF:, :].reshape(entries, width).astype(F32)
    tokens = local_ref.shape[0]
    tables = [later.astype(BF16)] * (tokens // BLOCK)
    tables[0] = (later + part_ref[0]).astype(BF16)
    levels = lax.broadcasted_iota(jnp.int32, (TILE, TILE), 1)
    for i in range(tokens // TILE):
        rows = slice(i * TILE, (i + 1) * TILE)
        column = jnp.broadcast_to(codes_row[:, rows], (TILE, TILE)).T
        hot = jnp.concatenate(
            [
                jnp.where(levels + k * TILE == column, 1.0, 0.0).astype(BF16)
                for k in range(entries // TILE)
            ],
            axis=1,
        )
        out_ref[rows, :] = (local_ref[rows, :] + dot(hot, tables[i * TILE // BLOCK])).astype(BF16)


def finish(own, core, codes, local, later, part, extra):
    heads, entries, width = part.shape
    tokens = local.shape[0]
    at = lambda s, core: (2 * core[0] if own else 2 - 2 * core[0]) + s
    by_head = lambda s, core: (at(s, core), 0, 0)
    rows_of = pl.BlockSpec((tokens, width), lambda s, core: (0, at(s, core)))
    per_head = pl.BlockSpec((1, entries, width), by_head)
    in_specs = [pl.BlockSpec(codes.shape, lambda s, *_: (0, 0)), rows_of, IN_VMEM]
    if own:
        in_specs += [IN_VMEM, per_head]
        args = (*extra, part)
    else:
        in_specs += [per_head] + [pl.BlockSpec(memory_space=pl.ANY)] * 2
        args = (part, *extra)
    return call(
        lambda *refs: finish_kernel(own, refs), "finish_own" if own else "finish_other", (2,),
        in_specs,
        [(local.shape, BF16, rows_of), (part.shape, F32, per_head)],
        aliases=None if own else {5: 0, 6: 1}, prefetch=1, flops=1 << 30, size=8 << 20,
    )(core, codes, local, later, *args)


def ring_pieces(array):
    count = lax.axis_size("head")
    up = [(i, (i + 1) % count) for i in range(count)]
    down = [(i, (i - 1) % count) for i in range(count)]
    left = lax.ppermute(array, "head", up)
    right = lax.ppermute(array, "head", down)
    half = array.shape[0] // 2
    far = lax.ppermute(left[:half], "head", up), lax.ppermute(right[half:], "head", down)
    return array, left, right, *far


def per_device(queries, values, codes, codebook, out_weight, grad_out):
    heads, entries, width = codebook.shape
    exchange = functools.partial(
        lax.all_to_all, axis_name=("chip", "core"), split_axis=0, concat_axis=0, tiled=True
    )
    between_chips = functools.partial(
        lax.all_to_all, axis_name="chip", split_axis=0, concat_axis=0, tiled=True
    )
    other_core = functools.partial(lax.ppermute, axis_name="core", perm=[(0, 1), (1, 0)])
    core = lax.axis_index("core").astype(jnp.int32)
    me_seq = lax.axis_index(("chip", "core")).astype(jnp.int32).reshape(1)
    me = lax.axis_index("head").astype(jnp.int32).reshape(1)
    core_at = core.reshape(1)
    pieces = ring_pieces(grad_out)
    codes = codes.T
    send, first, first_count = own_sums(codes, values, heads, entries)
    prefix, counts = prefix_scan(me_seq, exchange(send), first_count)
    prefix = exchange(prefix)
    probs, keys, book_t = forward(codes, queries, codebook, counts)
    grad_query, local, part, give, keep = backward(
        me, core_at, pieces, out_weight, codes, queries, values, probs, keys, book_t, prefix, counts, first
    )
    got = other_core(give)
    chip = (keep.astype(F32) + got.astype(F32)).astype(BF16)
    later = between_chips(suffix_scan(between_chips(chip)))
    is_value = lax.broadcasted_iota(jnp.int32, later.shape, 1) < HALF
    mine = jnp.where(is_value & (core == 1), keep.astype(F32), 0.0)
    theirs = other_core((later.astype(F32) + mine).astype(BF16))
    results = finish(True, core_at, codes, local, later, part, (got,))
    grad_values, grad_book = finish(False, core_at, codes, local, theirs, part, results)
    return grad_query, grad_values, grad_book


def solution(mesh):
    finer = Mesh(mesh.devices.reshape(-1, 2, mesh.shape["head"]), ("chip", "core", "head"))
    rows = P(("chip", "core"), "head")
    return jax.shard_map(
        per_device,
        mesh=finer,
        in_specs=(rows, rows, rows, P("head", None, None), P("head", None), rows),
        out_specs=(rows, rows, P("head", None, None)),
        check_vma=False,
    )
```

```python
import functools
import math

import jax
import jax.numpy as jnp
from jax import lax
from jax.experimental import pallas as pl
from jax.experimental.pallas import tpu as pltpu
from jax.sharding import Mesh
from jax.sharding import PartitionSpec as P

BLOCK = 512
PART = 256
TILE = 128
HALF = 64
ROWS = 96
F32 = jnp.float32
BF16 = jnp.bfloat16
VMEM_LIMIT = 44 << 20
IN_VMEM = pl.BlockSpec(memory_space=pltpu.VMEM)


def dot(left, right):
    return lax.dot_general(left, right, (((1,), (0,)), ((), ())), preferred_element_type=F32)


def dot_nt(left, right):
    return lax.dot_general(left, right, (((1,), (1,)), ((), ())), preferred_element_type=F32)


def space_of(spec):
    return pltpu.VMEM if spec.memory_space == pltpu.VMEM else pltpu.HBM


def call(kernel, name, grid, in_specs, outs, scratch=(), aliases=None, prefetch=0, flops=0, size=0,
         limit=VMEM_LIMIT):
    run = pl.pallas_call(
        kernel,
        grid_spec=pltpu.PrefetchScalarGridSpec(
            num_scalar_prefetch=prefetch,
            grid=grid,
            in_specs=in_specs,
            out_specs=[spec for _, _, spec in outs],
            scratch_shapes=list(scratch),
        ),
        out_shape=[space_of(spec)(shape, dtype) for shape, dtype, spec in outs],
        input_output_aliases=aliases or {},
        compiler_params=pltpu.CompilerParams(
            dimension_semantics=("arbitrary",) * len(grid), vmem_limit_bytes=limit
        ),
        cost_estimate=pl.CostEstimate(flops=flops, bytes_accessed=size, transcendentals=0),
        name=name,
    )

    def placed(array, spec):
        return pltpu.with_memory_space_constraint(array, space_of(spec))

    def with_places(*args):
        arrays = [placed(a, spec) for a, spec in zip(args[prefetch:], in_specs)]
        return run(*args[:prefetch], *arrays)

    return with_places


def onehot_rows(codes_row, entries):
    entry = lax.broadcasted_iota(jnp.int32, (entries, codes_row.shape[1]), 0)
    return jnp.where(entry == codes_row, 1.0, 0.0).astype(BF16)


def row_at(ref, index):
    place = lax.broadcasted_iota(jnp.int32, ref.shape, 0)
    return jnp.sum(jnp.where(place == index, ref[...], 0), axis=0, keepdims=True)


def fold(array):
    rows, lanes = array.shape
    return jnp.sum(array.reshape(rows // 8, 8, lanes), axis=0)


def fold_max(array):
    rows, lanes = array.shape
    return jnp.max(array.reshape(rows // 8, 8, lanes), axis=0)


def sum_kernel(codes_ref, value_ref, send_ref, first_ref, first_count_ref):
    heads, entries, width = first_ref.shape
    slices = entries // HALF
    blocks = value_ref.shape[0] // BLOCK
    ones = jnp.ones((BLOCK, TILE), BF16)
    lines = []
    for h in range(heads):
        total = None
        for b in range(blocks):
            span = slice(b * BLOCK, (b + 1) * BLOCK)
            hot = onehot_rows(codes_ref[h : h + 1, span], entries)
            columns = value_ref[span, h * width : (h + 1) * width]
            part = dot(hot, jnp.concatenate([columns, ones], axis=1))
            if b == 0:
                first_ref[h] = part[:, :width]
                for i in range(entries // TILE):
                    rows = slice(i * TILE, (i + 1) * TILE)
                    first_count_ref[h, :, rows] = part[rows, width:].T[:1]
            total = part if b == 0 else total + part
        for k in range(slices):
            rows = slice(k * HALF, (k + 1) * HALF)
            send_ref[h * slices + k, :HALF, :] = total[rows, :width].astype(BF16)
        for i in range(entries // TILE):
            lines.append(total[i * TILE : (i + 1) * TILE, width:].T[:1])
    lines = jnp.concatenate(lines, axis=0)
    high = jnp.floor(lines * (1.0 / 256.0))
    digits = jnp.concatenate([high, lines - high * 256.0], axis=0).astype(BF16)
    for k in range(heads * slices):
        send_ref[k, HALF:, :] = digits


def own_sums(codes, values, heads, entries):
    width = values.shape[1] // heads
    slices = entries // HALF
    whole = lambda i: (0, 0, 0)
    return call(
        sum_kernel, "own_sums", (1,),
        [
            pl.BlockSpec(codes.shape, lambda i: (0, 0)),
            pl.BlockSpec(values.shape, lambda i: (0, 0)),
        ],
        [
            ((heads * slices, ROWS, TILE), BF16, pl.BlockSpec((heads * slices, ROWS, TILE), whole)),
            ((heads, entries, width), F32, pl.BlockSpec((heads, entries, width), whole)),
            ((heads, 1, entries), F32, pl.BlockSpec((heads, 1, entries), whole)),
        ],

    )(codes, values)


def prefix_kernel(me_ref, in_ref, first_ref, out_ref, count_ref):
    running = jnp.zeros(out_ref.shape[1:], F32)
    lines = (ROWS - HALF) // 2
    number = jnp.zeros((lines, TILE), F32)
    for d in range(in_ref.shape[0]):
        out_ref[d] = running.astype(BF16)
        running = running + in_ref[d, :HALF, :].astype(F32)
        digits = in_ref[d, HALF:, :].astype(F32)
        digits = digits[:lines] * 256.0 + digits[lines:]
        number = number + jnp.where(d < me_ref[0], digits, 0.0)
    heads = first_ref.shape[0]
    per = lines // heads
    for h in range(heads):
        for i in range(per):
            line = number[h * per + i : h * per + i + 1]
            columns = slice(i * TILE, (i + 1) * TILE)
            count_ref[0, h, :, columns] = line
            count_ref[1, h, :, columns] = line + first_ref[h, :, columns]


def prefix_scan(me, pieces, first):
    count = pieces.shape[0]
    heads, _, entries = first.shape
    whole = lambda i, *_: (0, 0, 0)
    shape = (2, heads, 1, entries)
    return call(
        prefix_kernel, "prefix_scan", (1,),
        [IN_VMEM, pl.BlockSpec(first.shape, whole)],
        [
            ((count, HALF, TILE), BF16, pl.BlockSpec((count, HALF, TILE), whole)),
            (shape, F32, pl.BlockSpec(shape, lambda i, *_: (0, 0, 0, 0))),
        ],
        prefetch=1
    )(me, pieces, first)


def suffix_kernel(in_ref, out_ref):
    running = jnp.zeros((HALF, TILE), F32)
    total = jnp.zeros((HALF, TILE), F32)
    for d in reversed(range(in_ref.shape[0])):
        out_ref[d, :HALF, :] = running.astype(BF16)
        running = running + in_ref[d, :HALF, :].astype(F32)
        total = total + in_ref[d, HALF:, :].astype(F32)
    low = total.astype(BF16)
    for d in range(in_ref.shape[0]):
        out_ref[d, HALF:, :] = low


def suffix_scan(pieces):
    spec = pl.BlockSpec(pieces.shape, lambda i: (0, 0, 0))
    return call(
        suffix_kernel, "suffix_scan", (1,), [IN_VMEM], [(pieces.shape, BF16, spec)], size=2 << 20
    )(pieces)[0]


def count_columns(number):
    tiles = [
        jnp.broadcast_to(number[:, i * TILE : (i + 1) * TILE], (TILE, TILE)).T
        for i in range(number.shape[1] // TILE)
    ]
    return jnp.concatenate(tiles, axis=0)


def forward_kernel(codes_ref, query_ref, book_ref, count_ref,
                   low_ref, keys_ref, book_t_ref, rows_k, counts, scores):
    entries, width = book_ref.shape[1:]
    head = pl.program_id(0)
    entry_tiles = entries // TILE
    factor = width ** -0.5 * math.log2(math.e)
    causal = lax.broadcasted_iota(jnp.int32, (TILE, TILE), 1) >= lax.broadcasted_iota(
        jnp.int32, (TILE, TILE), 0
    )
    parts = BLOCK // PART
    blocks = low_ref.shape[0]

    codes_row = row_at(codes_ref, head)
    book_t_ref[0] = book_ref[0].astype(F32).T.astype(BF16)

    def prepare(b):
        keys_t = dot(
            book_t_ref[0], onehot_rows(codes_row[:, b * BLOCK : (b + 1) * BLOCK], entries)
        )
        keys_ref[b, 0] = keys_t.astype(BF16)
        rows_k[b, :entries, :] = book_ref[0]
        rows_k[b, entries:, :] = keys_t.T.astype(BF16)
        counts[b] = count_columns(count_ref[b, 0])

    def multiply(b, n):
        used = entries + PART * (n + 1)
        at = b * BLOCK + n * PART
        scores[b, n, :used, :] = dot_nt(rows_k[b, :used, :], query_ref[at : at + PART, :])

    def soften(b, n):
        used = entries + PART * (n + 1)
        for j in range(PART // TILE):
            columns = slice(j * TILE, (j + 1) * TILE)
            target = slice(n * PART + j * TILE, n * PART + (j + 1) * TILE)
            pieces = range(entry_tiles + 2 * n + j + 1)
            top = jnp.full((8, TILE), -jnp.inf, F32)
            for i in pieces:
                rows = slice(i * TILE, (i + 1) * TILE)
                piece = scores[b, n, rows, columns]
                if i < entry_tiles:
                    piece = jnp.where(counts[b, rows, :] > 0.0, piece, -jnp.inf)
                    scores[b, n, rows, columns] = piece
                elif i == pieces[-1]:
                    piece = jnp.where(causal, piece, -jnp.inf)
                    scores[b, n, rows, columns] = piece
                top = jnp.maximum(top, fold_max(piece))
            top = jnp.max(top, axis=0, keepdims=True)
            total = jnp.zeros((8, TILE), F32)
            for i in pieces:
                rows = slice(i * TILE, (i + 1) * TILE)
                piece = jnp.exp2((scores[b, n, rows, columns] - top) * factor)
                scores[b, n, rows, columns] = piece
                if i < entry_tiles:
                    piece = piece * counts[b, rows, :]
                total = total + fold(piece)
            inverse = 1.0 / jnp.sum(total, axis=0, keepdims=True)
            for i in pieces:
                rows = slice(i * TILE, (i + 1) * TILE)
                low_ref[b, 0, rows, target] = (scores[b, n, rows, columns] * inverse).astype(BF16)
            if j == 0:
                low_ref[b, 0, used - TILE : used, target] = jnp.zeros((TILE, TILE), BF16)

    order = [(b, n) for b in range(blocks) for n in range(parts)]
    for b in range(blocks):
        prepare(b)
    multiply(*order[0])
    for k, item in enumerate(order):
        if k + 1 < len(order):
            multiply(*order[k + 1])
        soften(*item)


def forward(codes, queries, book, counts):
    heads, entries, width = book.shape
    tokens = queries.shape[0]
    blocks = tokens // BLOCK
    both = entries + BLOCK
    by_head = lambda h: (h, 0, 0)
    in_blocks = lambda h: (0, h, 0, 0)
    return call(
        forward_kernel, "forward", (heads,),
        [
            pl.BlockSpec(codes.shape, lambda h: (0, 0)),
            pl.BlockSpec((tokens, width), lambda h: (0, h)),
            pl.BlockSpec((1, entries, width), by_head),
            pl.BlockSpec((blocks, 1, 1, entries), in_blocks),
        ],
        [
            ((blocks, heads, both, BLOCK), BF16, pl.BlockSpec((blocks, 1, both, BLOCK), in_blocks)),
            ((blocks, heads, width, BLOCK), BF16, pl.BlockSpec((blocks, 1, width, BLOCK), in_blocks)),
            ((heads, width, entries), BF16, pl.BlockSpec((1, width, entries), by_head)),
        ],
        [
            pltpu.VMEM((blocks, both, width), BF16),
            pltpu.VMEM((blocks, entries, TILE), F32),
            pltpu.VMEM((blocks, 2, both, PART), F32),
        ],

    )(codes, queries, book, counts)


def backward_kernel(me_ref, core_ref, own_ref, left_ref, right_ref, far0_ref, far1_ref, weight_ref,
                    codes_ref, query_ref, value_ref, probs_ref, keys_ref, book_t_ref,
                    prefix_ref, count_ref, first_ref,
                    grad_query_ref, local_ref, part_ref, give_ref, keep_ref,
                    dout, hot, rows_v, counts, grads, score_grad, key_grad, wide_t):
    width, entries = book_t_ref.shape[1:]
    entry_tiles = entries // TILE
    parts = BLOCK // PART
    blocks = probs_ref.shape[0]
    scale = width ** -0.5
    step = pl.program_id(0)
    head = lax.rem(step + 2 - 2 * core_ref[0], 4)

    def chunk(offset):
        columns = own_ref.shape[1]
        at = lax.rem(me_ref[0] + offset, 4) * columns
        return weight_ref[:, pl.ds(pl.multiple_of(at, columns), columns)]

    codes_row = row_at(codes_ref, head)

    def prepare(b):
        hot[b] = onehot_rows(codes_row[:, b * BLOCK : (b + 1) * BLOCK], entries)
        wide_t[b, :, :entries] = book_t_ref[0]
        wide_t[b, :, entries:] = keys_ref[b, 0]
        slices = entries // HALF
        sums = prefix_ref[pl.ds(head * slices, slices)].reshape(entries, width)
        if b > 0:
            sums = (sums.astype(F32) + first_ref[0]).astype(BF16)
        rows_v[b, :entries, :] = sums
        rows_v[b, entries:, :] = value_ref[b * BLOCK : (b + 1) * BLOCK, :]
        counts[b] = count_columns(count_ref[b, 0])

    def multiply(b, n):
        used = entries + PART * (n + 1)
        at = b * BLOCK + n * PART
        grads[b, n, :used, :] = dot_nt(rows_v[b, :used, :], dout[head, at : at + PART, :])

    def combine(b, n):
        used = entries + PART * (n + 1)
        for j in range(PART // TILE):
            columns = slice(j * TILE, (j + 1) * TILE)
            source = slice(n * PART + j * TILE, n * PART + (j + 1) * TILE)
            pieces = range(entry_tiles + 2 * n + j + 1)
            delta = jnp.zeros((8, TILE), F32)
            for i in pieces:
                rows = slice(i * TILE, (i + 1) * TILE)
                delta = delta + fold(
                    probs_ref[b, 0, rows, source].astype(F32) * grads[b, n, rows, columns]
                )
            delta = jnp.sum(delta, axis=0, keepdims=True)
            for i in pieces:
                rows = slice(i * TILE, (i + 1) * TILE)
                shift = delta
                if i < entry_tiles:
                    shift = delta * counts[b, rows, :]
                piece = grads[b, n, rows, columns] - shift
                piece = probs_ref[b, 0, rows, source].astype(F32) * piece
                score_grad[b, n, rows, columns] = piece.astype(BF16)
            if j == 0:
                score_grad[b, n, used - TILE : used, columns] = jnp.zeros((TILE, TILE), BF16)

    sums_k = [[None] * parts for _ in range(blocks)]
    sums_v = [[None] * parts for _ in range(blocks)]

    def outputs(b, n):
        used = entries + PART * (n + 1)
        at = b * BLOCK + n * PART
        span = slice(at, at + PART)
        sums_v[b][n] = dot(probs_ref[b, 0, :used, n * PART : (n + 1) * PART], dout[head, span, :])
        sums_k[b][n] = dot(score_grad[b, n, :used, :], query_ref[span, :]) * scale
        grad_t = dot(wide_t[b, :, :used], score_grad[b, n, :used, :])
        grad_query_ref[span, :] = (grad_t * scale).T.astype(BF16)

    order = [(b, n) for b in range(blocks) for n in range(parts)]
    for b in range(blocks):
        prepare(b)

    @pl.when(step == 0)
    def _():
        count = own_ref.shape[0] // PART
        for n in range(count):
            span = slice(n * PART, (n + 1) * PART)
            total = dot_nt(own_ref[span, :], chunk(0)) + dot_nt(left_ref[span, :], chunk(3))
            total = total + dot_nt(right_ref[span, :], chunk(1))
            if n < count // 2:
                far = far0_ref[span, :]
            else:
                far = far1_ref[(n - count // 2) * PART : (n + 1 - count // 2) * PART, :]
            total = total + dot_nt(far, chunk(2))
            for h in range(dout.shape[0]):
                dout[h, span, :] = total[:, h * width : (h + 1) * width].astype(BF16)

    multiply(*order[0])
    code = None
    part = None
    middle = entries + PART
    for k, item in enumerate(order):
        if k + 1 < len(order):
            multiply(*order[k + 1])
        combine(*item)
        outputs(*item)
        b, n = item
        if n == parts - 1:
            first, last = sums_v[b]
            at = b * BLOCK
            local_ref[at : at + PART, :] = first[entries:] + last[entries:middle]
            local_ref[at + PART : at + BLOCK, :] = last[middle:]
            mine = first[:entries] + last[:entries]
            if b == blocks - 1:
                part_ref[0] = mine
            part = mine if b == 0 else part + mine
            first, last = sums_k[b]
            key_grad[b, :PART, :] = (first[entries:] + last[entries:middle]).astype(BF16)
            key_grad[b, PART:, :] = last[middle:].astype(BF16)
            mine = first[:entries] + last[:entries] + dot(hot[b], key_grad[b])
            code = mine if b == 0 else code + mine

    def write(ref, first):
        for k in range(entries // HALF):
            rows = slice(k * HALF, (k + 1) * HALF)
            at = first + k
            ref[at, :HALF, :] = part[rows].astype(BF16)
            ref[at, HALF:, :] = code[rows].astype(BF16)

    @pl.when(step < 2)
    def _():
        write(give_ref, lax.rem(step, 2) * (entries // HALF))

    @pl.when(step >= 2)
    def _():
        write(keep_ref, 0)


def backward(me, core, pieces, weight, codes, queries, values, probs, keys, book_t, prefix, counts,
             first):
    heads, width, entries = book_t.shape
    tokens = queries.shape[0]
    blocks = tokens // BLOCK
    both = entries + BLOCK
    slices = entries // HALF
    at = lambda s, core: lax.rem(s + 2 - 2 * core[0], 4)
    by_head = lambda s, _, core: (at(s, core), 0, 0)
    in_blocks = lambda s, _, core: (0, at(s, core), 0, 0)
    rows_of = pl.BlockSpec((tokens, width), lambda s, _, core: (0, at(s, core)))
    shape = (slices, 2 * HALF, width)
    both_heads = (2 * slices, 2 * HALF, width)
    per_head = pl.BlockSpec((1, entries, width), by_head)

    anywhere = pl.BlockSpec(memory_space=pl.ANY)
    whole = lambda s, *_: (0, 0)
    in_specs = [pl.BlockSpec(pieces[0].shape, whole)] + [IN_VMEM] * (len(pieces) - 1)
    in_specs.append(pl.BlockSpec(weight.shape, whole))
    in_specs += [
        pl.BlockSpec(codes.shape, lambda h, *_: (0, 0)),
        rows_of,
        rows_of,
        pl.BlockSpec((blocks, 1, both, BLOCK), in_blocks),
        pl.BlockSpec((blocks, 1, width, BLOCK), in_blocks),
        pl.BlockSpec((1, width, entries), by_head),
        IN_VMEM,
        pl.BlockSpec((blocks, 1, 1, entries), in_blocks),
        per_head,
    ]
    outs = [
        (queries.shape, BF16, rows_of),
        (queries.shape, F32, rows_of),
        ((heads, entries, width), F32, per_head),
        (both_heads, BF16, IN_VMEM),
        (both_heads, BF16, pl.BlockSpec(shape, lambda s, *_: (jnp.maximum(s - 2, 0), 0, 0))),
    ]
    return call(
        backward_kernel, "backward", (heads,), in_specs, outs,
        [
            pltpu.VMEM((heads, tokens, width), BF16),
            pltpu.VMEM((blocks, entries, BLOCK), BF16),
            pltpu.VMEM((blocks, both, width), BF16),
            pltpu.VMEM((blocks, entries, TILE), F32),
            pltpu.VMEM((blocks, 2, both, PART), F32),
            pltpu.VMEM((blocks, 2, both, PART), BF16),
            pltpu.VMEM((blocks, BLOCK, width), BF16),
            pltpu.VMEM((blocks, width, both), BF16),
        ],
        prefetch=2, flops=20 << 30, size=24 << 20,
    )(me, core, *pieces, weight, codes, queries, values, probs, keys, book_t, prefix, counts,
      first)


def finish_kernel(own, refs):
    me_ref, codes_ref, local_ref, later_ref = refs[:4]
    if own:
        kept_ref, part_ref = refs[4:6]
    else:
        part_ref = refs[4]
    out_ref, book_ref = refs[-2:]
    entries, width = part_ref.shape[1:]
    step = pl.program_id(0)
    head = 2 * me_ref[0] + step if own else 2 - 2 * me_ref[0] + step
    codes_row = row_at(codes_ref, head)
    mine = pl.ds(step * (entries // HALF), entries // HALF)
    later = later_ref[mine, :HALF, :].astype(F32)
    if own:
        later = later + jnp.where(me_ref[0] == 0, kept_ref[mine, :HALF, :].astype(F32), 0.0)
    later = later.reshape(entries, width)
    book_ref[0] = later_ref[mine, HALF:, :].reshape(entries, width).astype(F32)
    tokens = local_ref.shape[0]
    tables = [later.astype(BF16)] * (tokens // BLOCK)
    tables[0] = (later + part_ref[0]).astype(BF16)
    levels = lax.broadcasted_iota(jnp.int32, (TILE, TILE), 1)
    for i in range(tokens // TILE):
        rows = slice(i * TILE, (i + 1) * TILE)
        column = jnp.broadcast_to(codes_row[:, rows], (TILE, TILE)).T
        hot = jnp.concatenate(
            [
                jnp.where(levels + k * TILE == column, 1.0, 0.0).astype(BF16)
                for k in range(entries // TILE)
            ],
            axis=1,
        )
        out_ref[rows, :] = (local_ref[rows, :] + dot(hot, tables[i * TILE // BLOCK])).astype(BF16)


def finish(own, core, codes, local, later, part, extra):
    heads, entries, width = part.shape
    tokens = local.shape[0]
    at = lambda s, core: (2 * core[0] if own else 2 - 2 * core[0]) + s
    by_head = lambda s, core: (at(s, core), 0, 0)
    rows_of = pl.BlockSpec((tokens, width), lambda s, core: (0, at(s, core)))
    per_head = pl.BlockSpec((1, entries, width), by_head)
    in_specs = [pl.BlockSpec(codes.shape, lambda s, *_: (0, 0)), rows_of, IN_VMEM]
    if own:
        in_specs += [IN_VMEM, per_head]
        args = (*extra, part)
    else:
        in_specs += [per_head] + [pl.BlockSpec(memory_space=pl.ANY)] * 2
        args = (part, *extra)
    return call(
        lambda *refs: finish_kernel(own, refs), "finish_own" if own else "finish_other", (2,),
        in_specs,
        [(local.shape, BF16, rows_of), (part.shape, F32, per_head)],
        aliases=None if own else {5: 0, 6: 1}, prefetch=1, flops=1 << 30, size=8 << 20,
    )(core, codes, local, later, *args)


def ring_pieces(array):
    count = lax.axis_size("head")
    up = [(i, (i + 1) % count) for i in range(count)]
    down = [(i, (i - 1) % count) for i in range(count)]
    left = lax.ppermute(array, "head", up)
    right = lax.ppermute(array, "head", down)
    half = array.shape[0] // 2
    far = lax.ppermute(left[:half], "head", up), lax.ppermute(right[half:], "head", down)
    return array, left, right, *far


def per_device(queries, values, codes, codebook, out_weight, grad_out):
    heads, entries, width = codebook.shape
    exchange = functools.partial(
        lax.all_to_all, axis_name=("chip", "core"), split_axis=0, concat_axis=0, tiled=True
    )
    between_chips = functools.partial(
        lax.all_to_all, axis_name="chip", split_axis=0, concat_axis=0, tiled=True
    )
    other_core = functools.partial(lax.ppermute, axis_name="core", perm=[(0, 1), (1, 0)])
    core = lax.axis_index("core").astype(jnp.int32)
    me_seq = lax.axis_index(("chip", "core")).astype(jnp.int32).reshape(1)
    me = lax.axis_index("head").astype(jnp.int32).reshape(1)
    core_at = core.reshape(1)
    pieces = ring_pieces(grad_out)
    codes = codes.T
    send, first, first_count = own_sums(codes, values, heads, entries)
    prefix, counts = prefix_scan(me_seq, exchange(send), first_count)
    prefix = exchange(prefix)
    probs, keys, book_t = forward(codes, queries, codebook, counts)
    grad_query, local, part, give, keep = backward(
        me, core_at, pieces, out_weight, codes, queries, values, probs, keys, book_t, prefix, counts, first
    )
    got = other_core(give)
    chip = (keep.astype(F32) + got.astype(F32)).astype(BF16)
    later = between_chips(suffix_scan(between_chips(chip)))
    is_value = lax.broadcasted_iota(jnp.int32, later.shape, 1) < HALF
    mine = jnp.where(is_value & (core == 1), keep.astype(F32), 0.0)
    theirs = other_core((later.astype(F32) + mine).astype(BF16))
    results = finish(True, core_at, codes, local, later, part, (got,))
    grad_values, grad_book = finish(False, core_at, codes, local, theirs, part, results)
    return grad_query, grad_values, grad_book


def solution(mesh):
    finer = Mesh(mesh.devices.reshape(-1, 2, mesh.shape["head"]), ("chip", "core", "head"))
    rows = P(("chip", "core"), "head")
    return jax.shard_map(
        per_device,
        mesh=finer,
        in_specs=(rows, rows, rows, P("head", None, None), P("head", None), rows),
        out_specs=(rows, rows, P("head", None, None)),
        check_vma=False,
    )
```

```python
import functools
import math

import jax
import jax.numpy as jnp
from jax import lax
from jax.experimental import pallas as pl
from jax.experimental.pallas import tpu as pltpu
from jax.sharding import Mesh
from jax.sharding import PartitionSpec as P

BLOCK = 512
PART = 256
TILE = 128
HALF = 64
ROWS = 96
F32 = jnp.float32
BF16 = jnp.bfloat16
VMEM_LIMIT = 44 << 20
IN_VMEM = pl.BlockSpec(memory_space=pltpu.VMEM)


def dot(left, right):
    return lax.dot_general(left, right, (((1,), (0,)), ((), ())), preferred_element_type=F32)


def dot_nt(left, right):
    return lax.dot_general(left, right, (((1,), (1,)), ((), ())), preferred_element_type=F32)


def space_of(spec):
    return pltpu.VMEM if spec.memory_space == pltpu.VMEM else pltpu.HBM


def call(kernel, name, grid, in_specs, outs, scratch=(), aliases=None, prefetch=0, flops=0, size=0,
         limit=VMEM_LIMIT):
    run = pl.pallas_call(
        kernel,
        grid_spec=pltpu.PrefetchScalarGridSpec(
            num_scalar_prefetch=prefetch,
            grid=grid,
            in_specs=in_specs,
            out_specs=[spec for _, _, spec in outs],
            scratch_shapes=list(scratch),
        ),
        out_shape=[space_of(spec)(shape, dtype) for shape, dtype, spec in outs],
        input_output_aliases=aliases or {},
        compiler_params=pltpu.CompilerParams(
            dimension_semantics=("arbitrary",) * len(grid), vmem_limit_bytes=limit
        ),
        cost_estimate=pl.CostEstimate(flops=flops, bytes_accessed=size, transcendentals=0),
        name=name,
    )

    def placed(array, spec):
        return pltpu.with_memory_space_constraint(array, space_of(spec))

    def with_places(*args):
        arrays = [placed(a, spec) for a, spec in zip(args[prefetch:], in_specs)]
        return run(*args[:prefetch], *arrays)

    return with_places


def onehot_rows(codes_row, entries):
    entry = lax.broadcasted_iota(jnp.int32, (entries, codes_row.shape[1]), 0)
    return jnp.where(entry == codes_row, 1.0, 0.0).astype(BF16)


def row_at(ref, index):
    place = lax.broadcasted_iota(jnp.int32, ref.shape, 0)
    return jnp.sum(jnp.where(place == index, ref[...], 0), axis=0, keepdims=True)


def fold(array):
    rows, lanes = array.shape
    return jnp.sum(array.reshape(rows // 8, 8, lanes), axis=0)


def fold_max(array):
    rows, lanes = array.shape
    return jnp.max(array.reshape(rows // 8, 8, lanes), axis=0)


def sum_kernel(codes_ref, value_ref, send_ref, first_ref, first_count_ref):
    heads, entries, width = first_ref.shape
    slices = entries // HALF
    blocks = value_ref.shape[0] // BLOCK
    ones = jnp.ones((BLOCK, TILE), BF16)
    lines = []
    for h in range(heads):
        total = None
        for b in range(blocks):
            span = slice(b * BLOCK, (b + 1) * BLOCK)
            hot = onehot_rows(codes_ref[h : h + 1, span], entries)
            columns = value_ref[span, h * width : (h + 1) * width]
            part = dot(hot, jnp.concatenate([columns, ones], axis=1))
            if b == 0:
                first_ref[h] = part[:, :width]
                for i in range(entries // TILE):
                    rows = slice(i * TILE, (i + 1) * TILE)
                    first_count_ref[h, :, rows] = part[rows, width:].T[:1]
            total = part if b == 0 else total + part
        for k in range(slices):
            rows = slice(k * HALF, (k + 1) * HALF)
            send_ref[h * slices + k, :HALF, :] = total[rows, :width].astype(BF16)
        for i in range(entries // TILE):
            lines.append(total[i * TILE : (i + 1) * TILE, width:].T[:1])
    lines = jnp.concatenate(lines, axis=0)
    high = jnp.floor(lines * (1.0 / 256.0))
    digits = jnp.concatenate([high, lines - high * 256.0], axis=0).astype(BF16)
    for k in range(heads * slices):
        send_ref[k, HALF:, :] = digits


def own_sums(codes, values, heads, entries):
    width = values.shape[1] // heads
    slices = entries // HALF
    whole = lambda i: (0, 0, 0)
    return call(
        sum_kernel, "own_sums", (1,),
        [
            pl.BlockSpec(codes.shape, lambda i: (0, 0)),
            pl.BlockSpec(values.shape, lambda i: (0, 0)),
        ],
        [
            ((heads * slices, ROWS, TILE), BF16, pl.BlockSpec((heads * slices, ROWS, TILE), whole)),
            ((heads, entries, width), F32, pl.BlockSpec((heads, entries, width), whole)),
            ((heads, 1, entries), F32, pl.BlockSpec((heads, 1, entries), whole)),
        ],

    )(codes, values)


def prefix_kernel(me_ref, in_ref, first_ref, out_ref, count_ref):
    running = jnp.zeros(out_ref.shape[1:], F32)
    lines = (ROWS - HALF) // 2
    number = jnp.zeros((lines, TILE), F32)
    for d in range(in_ref.shape[0]):
        out_ref[d] = running.astype(BF16)
        running = running + in_ref[d, :HALF, :].astype(F32)
        digits = in_ref[d, HALF:, :].astype(F32)
        digits = digits[:lines] * 256.0 + digits[lines:]
        number = number + jnp.where(d < me_ref[0], digits, 0.0)
    heads = first_ref.shape[0]
    per = lines // heads
    for h in range(heads):
        for i in range(per):
            line = number[h * per + i : h * per + i + 1]
            columns = slice(i * TILE, (i + 1) * TILE)
            count_ref[0, h, :, columns] = line
            count_ref[1, h, :, columns] = line + first_ref[h, :, columns]


def prefix_scan(me, pieces, first):
    count = pieces.shape[0]
    heads, _, entries = first.shape
    whole = lambda i, *_: (0, 0, 0)
    shape = (2, heads, 1, entries)
    return call(
        prefix_kernel, "prefix_scan", (1,),
        [IN_VMEM, pl.BlockSpec(first.shape, whole)],
        [
            ((count, HALF, TILE), BF16, pl.BlockSpec((count, HALF, TILE), whole)),
            (shape, F32, pl.BlockSpec(shape, lambda i, *_: (0, 0, 0, 0))),
        ],
        prefetch=1
    )(me, pieces, first)


def suffix_kernel(in_ref, out_ref):
    running = jnp.zeros((HALF, TILE), F32)
    total = jnp.zeros((HALF, TILE), F32)
    for d in reversed(range(in_ref.shape[0])):
        out_ref[d, :HALF, :] = running.astype(BF16)
        running = running + in_ref[d, :HALF, :].astype(F32)
        total = total + in_ref[d, HALF:, :].astype(F32)
    low = total.astype(BF16)
    for d in range(in_ref.shape[0]):
        out_ref[d, HALF:, :] = low


def suffix_scan(pieces):
    spec = pl.BlockSpec(pieces.shape, lambda i: (0, 0, 0))
    return call(
        suffix_kernel, "suffix_scan", (1,), [IN_VMEM], [(pieces.shape, BF16, spec)], size=2 << 20
    )(pieces)[0]


def add_kernel(kept_ref, got_ref, out_ref):
    out_ref[...] = (kept_ref[...].astype(F32) + got_ref[...].astype(F32)).astype(BF16)


def chip_sums(kept, got):
    spec = pl.BlockSpec(kept.shape, lambda i: (0, 0, 0))
    return call(
        add_kernel, "chip_sums", (1,), [spec, IN_VMEM], [(kept.shape, BF16, IN_VMEM)], size=1 << 20
    )(kept, got)[0]


def count_columns(number):
    tiles = [
        jnp.broadcast_to(number[:, i * TILE : (i + 1) * TILE], (TILE, TILE)).T
        for i in range(number.shape[1] // TILE)
    ]
    return jnp.concatenate(tiles, axis=0)


def forward_kernel(codes_ref, query_ref, book_ref, count_ref,
                   low_ref, keys_ref, book_t_ref, rows_k, counts, scores):
    entries, width = book_ref.shape[1:]
    head = pl.program_id(0)
    entry_tiles = entries // TILE
    factor = width ** -0.5 * math.log2(math.e)
    causal = lax.broadcasted_iota(jnp.int32, (TILE, TILE), 1) >= lax.broadcasted_iota(
        jnp.int32, (TILE, TILE), 0
    )
    parts = BLOCK // PART
    blocks = low_ref.shape[0]

    codes_row = row_at(codes_ref, head)
    book_t_ref[0] = book_ref[0].astype(F32).T.astype(BF16)

    def prepare(b):
        keys_t = dot(
            book_t_ref[0], onehot_rows(codes_row[:, b * BLOCK : (b + 1) * BLOCK], entries)
        )
        keys_ref[b, 0] = keys_t.astype(BF16)
        rows_k[b, :entries, :] = book_ref[0]
        rows_k[b, entries:, :] = keys_t.T.astype(BF16)
        counts[b] = count_columns(count_ref[b, 0])

    def multiply(b, n):
        used = entries + PART * (n + 1)
        at = b * BLOCK + n * PART
        scores[b, n, :used, :] = dot_nt(rows_k[b, :used, :], query_ref[at : at + PART, :])

    def soften(b, n):
        used = entries + PART * (n + 1)
        for j in range(PART // TILE):
            columns = slice(j * TILE, (j + 1) * TILE)
            target = slice(n * PART + j * TILE, n * PART + (j + 1) * TILE)
            pieces = range(entry_tiles + 2 * n + j + 1)
            top = jnp.full((8, TILE), -jnp.inf, F32)
            for i in pieces:
                rows = slice(i * TILE, (i + 1) * TILE)
                piece = scores[b, n, rows, columns]
                if i < entry_tiles:
                    piece = jnp.where(counts[b, rows, :] > 0.0, piece, -jnp.inf)
                    scores[b, n, rows, columns] = piece
                elif i == pieces[-1]:
                    piece = jnp.where(causal, piece, -jnp.inf)
                    scores[b, n, rows, columns] = piece
                top = jnp.maximum(top, fold_max(piece))
            top = jnp.max(top, axis=0, keepdims=True)
            total = jnp.zeros((8, TILE), F32)
            for i in pieces:
                rows = slice(i * TILE, (i + 1) * TILE)
                piece = jnp.exp2((scores[b, n, rows, columns] - top) * factor)
                scores[b, n, rows, columns] = piece
                if i < entry_tiles:
                    piece = piece * counts[b, rows, :]
                total = total + fold(piece)
            inverse = 1.0 / jnp.sum(total, axis=0, keepdims=True)
            for i in pieces:
                rows = slice(i * TILE, (i + 1) * TILE)
                low_ref[b, 0, rows, target] = (scores[b, n, rows, columns] * inverse).astype(BF16)
            if j == 0:
                low_ref[b, 0, used - TILE : used, target] = jnp.zeros((TILE, TILE), BF16)

    order = [(b, n) for b in range(blocks) for n in range(parts)]
    for b in range(blocks):
        prepare(b)
    multiply(*order[0])
    for k, item in enumerate(order):
        if k + 1 < len(order):
            multiply(*order[k + 1])
        soften(*item)


def forward(codes, queries, book, counts):
    heads, entries, width = book.shape
    tokens = queries.shape[0]
    blocks = tokens // BLOCK
    both = entries + BLOCK
    by_head = lambda h: (h, 0, 0)
    in_blocks = lambda h: (0, h, 0, 0)
    return call(
        forward_kernel, "forward", (heads,),
        [
            pl.BlockSpec(codes.shape, lambda h: (0, 0)),
            pl.BlockSpec((tokens, width), lambda h: (0, h)),
            pl.BlockSpec((1, entries, width), by_head),
            pl.BlockSpec((blocks, 1, 1, entries), in_blocks),
        ],
        [
            ((blocks, heads, both, BLOCK), BF16, pl.BlockSpec((blocks, 1, both, BLOCK), in_blocks)),
            ((blocks, heads, width, BLOCK), BF16, pl.BlockSpec((blocks, 1, width, BLOCK), in_blocks)),
            ((heads, width, entries), BF16, pl.BlockSpec((1, width, entries), by_head)),
        ],
        [
            pltpu.VMEM((blocks, both, width), BF16),
            pltpu.VMEM((blocks, entries, TILE), F32),
            pltpu.VMEM((blocks, 2, both, PART), F32),
        ],

    )(codes, queries, book, counts)


def backward_kernel(me_ref, core_ref, own_ref, left_ref, right_ref, far0_ref, far1_ref, weight_ref,
                    codes_ref, query_ref, value_ref, probs_ref, keys_ref, book_t_ref,
                    prefix_ref, count_ref, first_ref,
                    grad_query_ref, local_ref, part_ref, give_ref, keep_ref,
                    dout, hot, rows_v, counts, grads, score_grad, key_grad, wide_t):
    width, entries = book_t_ref.shape[1:]
    entry_tiles = entries // TILE
    parts = BLOCK // PART
    blocks = probs_ref.shape[0]
    scale = width ** -0.5
    step = pl.program_id(0)
    head = lax.rem(step + 2 - 2 * core_ref[0], 4)

    def chunk(offset):
        columns = own_ref.shape[1]
        at = lax.rem(me_ref[0] + offset, 4) * columns
        return weight_ref[:, pl.ds(pl.multiple_of(at, columns), columns)]

    codes_row = row_at(codes_ref, head)

    def prepare(b):
        hot[b] = onehot_rows(codes_row[:, b * BLOCK : (b + 1) * BLOCK], entries)
        wide_t[b, :, :entries] = book_t_ref[0]
        wide_t[b, :, entries:] = keys_ref[b, 0]
        slices = entries // HALF
        sums = prefix_ref[pl.ds(head * slices, slices)].reshape(entries, width)
        if b > 0:
            sums = (sums.astype(F32) + first_ref[0]).astype(BF16)
        rows_v[b, :entries, :] = sums
        rows_v[b, entries:, :] = value_ref[b * BLOCK : (b + 1) * BLOCK, :]
        counts[b] = count_columns(count_ref[b, 0])

    def multiply(b, n):
        used = entries + PART * (n + 1)
        at = b * BLOCK + n * PART
        grads[b, n, :used, :] = dot_nt(rows_v[b, :used, :], dout[head, at : at + PART, :])

    def combine(b, n):
        used = entries + PART * (n + 1)
        for j in range(PART // TILE):
            columns = slice(j * TILE, (j + 1) * TILE)
            source = slice(n * PART + j * TILE, n * PART + (j + 1) * TILE)
            pieces = range(entry_tiles + 2 * n + j + 1)
            delta = jnp.zeros((8, TILE), F32)
            for i in pieces:
                rows = slice(i * TILE, (i + 1) * TILE)
                delta = delta + fold(
                    probs_ref[b, 0, rows, source].astype(F32) * grads[b, n, rows, columns]
                )
            delta = jnp.sum(delta, axis=0, keepdims=True)
            for i in pieces:
                rows = slice(i * TILE, (i + 1) * TILE)
                shift = delta
                if i < entry_tiles:
                    shift = delta * counts[b, rows, :]
                piece = grads[b, n, rows, columns] - shift
                piece = probs_ref[b, 0, rows, source].astype(F32) * piece
                score_grad[b, n, rows, columns] = piece.astype(BF16)
            if j == 0:
                score_grad[b, n, used - TILE : used, columns] = jnp.zeros((TILE, TILE), BF16)

    sums_k = [[None] * parts for _ in range(blocks)]
    sums_v = [[None] * parts for _ in range(blocks)]

    def outputs(b, n):
        used = entries + PART * (n + 1)
        at = b * BLOCK + n * PART
        span = slice(at, at + PART)
        sums_v[b][n] = dot(probs_ref[b, 0, :used, n * PART : (n + 1) * PART], dout[head, span, :])
        sums_k[b][n] = dot(score_grad[b, n, :used, :], query_ref[span, :]) * scale
        grad_t = dot(wide_t[b, :, :used], score_grad[b, n, :used, :])
        grad_query_ref[span, :] = (grad_t * scale).T.astype(BF16)

    order = [(b, n) for b in range(blocks) for n in range(parts)]
    for b in range(blocks):
        prepare(b)

    @pl.when(step == 0)
    def _():
        count = own_ref.shape[0] // PART
        for n in range(count):
            span = slice(n * PART, (n + 1) * PART)
            total = dot_nt(own_ref[span, :], chunk(0)) + dot_nt(left_ref[span, :], chunk(3))
            total = total + dot_nt(right_ref[span, :], chunk(1))
            if n < count // 2:
                far = far0_ref[span, :]
            else:
                far = far1_ref[(n - count // 2) * PART : (n + 1 - count // 2) * PART, :]
            total = total + dot_nt(far, chunk(2))
            for h in range(dout.shape[0]):
                dout[h, span, :] = total[:, h * width : (h + 1) * width].astype(BF16)

    multiply(*order[0])
    code = None
    part = None
    middle = entries + PART
    for k, item in enumerate(order):
        if k + 1 < len(order):
            multiply(*order[k + 1])
        combine(*item)
        outputs(*item)
        b, n = item
        if n == parts - 1:
            first, last = sums_v[b]
            at = b * BLOCK
            local_ref[at : at + PART, :] = first[entries:] + last[entries:middle]
            local_ref[at + PART : at + BLOCK, :] = last[middle:]
            mine = first[:entries] + last[:entries]
            if b == blocks - 1:
                part_ref[0] = mine
            part = mine if b == 0 else part + mine
            first, last = sums_k[b]
            key_grad[b, :PART, :] = (first[entries:] + last[entries:middle]).astype(BF16)
            key_grad[b, PART:, :] = last[middle:].astype(BF16)
            mine = first[:entries] + last[:entries] + dot(hot[b], key_grad[b])
            code = mine if b == 0 else code + mine

    def write(ref, first):
        for k in range(entries // HALF):
            rows = slice(k * HALF, (k + 1) * HALF)
            at = first + k
            ref[at, :HALF, :] = part[rows].astype(BF16)
            ref[at, HALF:, :] = code[rows].astype(BF16)

    @pl.when(step < 2)
    def _():
        write(give_ref, lax.rem(step, 2) * (entries // HALF))

    @pl.when(step >= 2)
    def _():
        write(keep_ref, 0)


def backward(me, core, pieces, weight, codes, queries, values, probs, keys, book_t, prefix, counts,
             first):
    heads, width, entries = book_t.shape
    tokens = queries.shape[0]
    blocks = tokens // BLOCK
    both = entries + BLOCK
    slices = entries // HALF
    at = lambda s, core: lax.rem(s + 2 - 2 * core[0], 4)
    by_head = lambda s, _, core: (at(s, core), 0, 0)
    in_blocks = lambda s, _, core: (0, at(s, core), 0, 0)
    rows_of = pl.BlockSpec((tokens, width), lambda s, _, core: (0, at(s, core)))
    shape = (slices, 2 * HALF, width)
    both_heads = (2 * slices, 2 * HALF, width)
    per_head = pl.BlockSpec((1, entries, width), by_head)

    anywhere = pl.BlockSpec(memory_space=pl.ANY)
    whole = lambda s, *_: (0, 0)
    in_specs = [pl.BlockSpec(pieces[0].shape, whole)] + [IN_VMEM] * (len(pieces) - 1)
    in_specs.append(pl.BlockSpec(weight.shape, whole))
    in_specs += [
        pl.BlockSpec(codes.shape, lambda h, *_: (0, 0)),
        rows_of,
        rows_of,
        pl.BlockSpec((blocks, 1, both, BLOCK), in_blocks),
        pl.BlockSpec((blocks, 1, width, BLOCK), in_blocks),
        pl.BlockSpec((1, width, entries), by_head),
        IN_VMEM,
        pl.BlockSpec((blocks, 1, 1, entries), in_blocks),
        per_head,
    ]
    outs = [
        (queries.shape, BF16, rows_of),
        (queries.shape, F32, rows_of),
        ((heads, entries, width), F32, per_head),
        (both_heads, BF16, IN_VMEM),
        (both_heads, BF16, pl.BlockSpec(shape, lambda s, *_: (jnp.maximum(s - 2, 0), 0, 0))),
    ]
    return call(
        backward_kernel, "backward", (heads,), in_specs, outs,
        [
            pltpu.VMEM((heads, tokens, width), BF16),
            pltpu.VMEM((blocks, entries, BLOCK), BF16),
            pltpu.VMEM((blocks, both, width), BF16),
            pltpu.VMEM((blocks, entries, TILE), F32),
            pltpu.VMEM((blocks, 2, both, PART), F32),
            pltpu.VMEM((blocks, 2, both, PART), BF16),
            pltpu.VMEM((blocks, BLOCK, width), BF16),
            pltpu.VMEM((blocks, width, both), BF16),
        ],
        prefetch=2, flops=20 << 30, size=24 << 20,
    )(me, core, *pieces, weight, codes, queries, values, probs, keys, book_t, prefix, counts,
      first)


def finish_kernel(own, refs):
    me_ref, codes_ref, local_ref, later_ref = refs[:4]
    if own:
        kept_ref, part_ref = refs[4:6]
    else:
        part_ref = refs[4]
    out_ref, book_ref = refs[-2:]
    entries, width = part_ref.shape[1:]
    step = pl.program_id(0)
    head = 2 * me_ref[0] + step if own else 2 - 2 * me_ref[0] + step
    codes_row = row_at(codes_ref, head)
    mine = pl.ds(step * (entries // HALF), entries // HALF)
    later = later_ref[mine, :HALF, :].astype(F32)
    if own:
        later = later + jnp.where(me_ref[0] == 0, kept_ref[mine, :HALF, :].astype(F32), 0.0)
    later = later.reshape(entries, width)
    book_ref[0] = later_ref[mine, HALF:, :].reshape(entries, width).astype(F32)
    tokens = local_ref.shape[0]
    tables = [later.astype(BF16)] * (tokens // BLOCK)
    tables[0] = (later + part_ref[0]).astype(BF16)
    levels = lax.broadcasted_iota(jnp.int32, (TILE, TILE), 1)
    for i in range(tokens // TILE):
        rows = slice(i * TILE, (i + 1) * TILE)
        column = jnp.broadcast_to(codes_row[:, rows], (TILE, TILE)).T
        hot = jnp.concatenate(
            [
                jnp.where(levels + k * TILE == column, 1.0, 0.0).astype(BF16)
                for k in range(entries // TILE)
            ],
            axis=1,
        )
        out_ref[rows, :] = (local_ref[rows, :] + dot(hot, tables[i * TILE // BLOCK])).astype(BF16)


def finish(own, core, codes, local, later, part, extra):
    heads, entries, width = part.shape
    tokens = local.shape[0]
    at = lambda s, core: (2 * core[0] if own else 2 - 2 * core[0]) + s
    by_head = lambda s, core: (at(s, core), 0, 0)
    rows_of = pl.BlockSpec((tokens, width), lambda s, core: (0, at(s, core)))
    per_head = pl.BlockSpec((1, entries, width), by_head)
    in_specs = [pl.BlockSpec(codes.shape, lambda s, *_: (0, 0)), rows_of, IN_VMEM]
    if own:
        in_specs += [IN_VMEM, per_head]
        args = (*extra, part)
    else:
        in_specs += [per_head] + [pl.BlockSpec(memory_space=pl.ANY)] * 2
        args = (part, *extra)
    return call(
        lambda *refs: finish_kernel(own, refs), "finish_own" if own else "finish_other", (2,),
        in_specs,
        [(local.shape, BF16, rows_of), (part.shape, F32, per_head)],
        aliases=None if own else {5: 0, 6: 1}, prefetch=1, flops=1 << 30, size=8 << 20,
    )(core, codes, local, later, *args)


def ring_pieces(array):
    count = lax.axis_size("head")
    up = [(i, (i + 1) % count) for i in range(count)]
    down = [(i, (i - 1) % count) for i in range(count)]
    left = lax.ppermute(array, "head", up)
    right = lax.ppermute(array, "head", down)
    half = array.shape[0] // 2
    far = lax.ppermute(left[:half], "head", up), lax.ppermute(right[half:], "head", down)
    return array, left, right, *far


def per_device(queries, values, codes, codebook, out_weight, grad_out):
    heads, entries, width = codebook.shape
    exchange = functools.partial(
        lax.all_to_all, axis_name=("chip", "core"), split_axis=0, concat_axis=0, tiled=True
    )
    between_chips = functools.partial(
        lax.all_to_all, axis_name="chip", split_axis=0, concat_axis=0, tiled=True
    )
    other_core = functools.partial(lax.ppermute, axis_name="core", perm=[(0, 1), (1, 0)])
    core = lax.axis_index("core").astype(jnp.int32)
    me_seq = lax.axis_index(("chip", "core")).astype(jnp.int32).reshape(1)
    me = lax.axis_index("head").astype(jnp.int32).reshape(1)
    core_at = core.reshape(1)
    pieces = ring_pieces(grad_out)
    codes = codes.T
    send, first, first_count = own_sums(codes, values, heads, entries)
    prefix, counts = prefix_scan(me_seq, exchange(send), first_count)
    prefix = exchange(prefix)
    probs, keys, book_t = forward(codes, queries, codebook, counts)
    grad_query, local, part, give, keep = backward(
        me, core_at, pieces, out_weight, codes, queries, values, probs, keys, book_t, prefix, counts, first
    )
    got = other_core(give)
    chip = chip_sums(keep, got)
    later = between_chips(suffix_scan(between_chips(chip)))
    is_value = lax.broadcasted_iota(jnp.int32, later.shape, 1) < HALF
    mine = jnp.where(is_value & (core == 1), keep.astype(F32), 0.0)
    theirs = other_core((later.astype(F32) + mine).astype(BF16))
    results = finish(True, core_at, codes, local, later, part, (got,))
    grad_values, grad_book = finish(False, core_at, codes, local, theirs, part, results)
    return grad_query, grad_values, grad_book


def solution(mesh):
    finer = Mesh(mesh.devices.reshape(-1, 2, mesh.shape["head"]), ("chip", "core", "head"))
    rows = P(("chip", "core"), "head")
    return jax.shard_map(
        per_device,
        mesh=finer,
        in_specs=(rows, rows, rows, P("head", None, None), P("head", None), rows),
        out_specs=(rows, rows, P("head", None, None)),
        check_vma=False,
    )
```

```python
import functools
import math

import jax
import jax.numpy as jnp
from jax import lax
from jax.experimental import pallas as pl
from jax.experimental.pallas import tpu as pltpu
from jax.sharding import Mesh
from jax.sharding import PartitionSpec as P

BLOCK = 512
PART = 256
TILE = 128
HALF = 64
ROWS = 96
F32 = jnp.float32
BF16 = jnp.bfloat16
VMEM_LIMIT = 44 << 20
IN_VMEM = pl.BlockSpec(memory_space=pltpu.VMEM)


def dot(left, right):
    return lax.dot_general(left, right, (((1,), (0,)), ((), ())), preferred_element_type=F32)


def dot_nt(left, right):
    return lax.dot_general(left, right, (((1,), (1,)), ((), ())), preferred_element_type=F32)


def space_of(spec):
    return pltpu.VMEM if spec.memory_space == pltpu.VMEM else pltpu.HBM


def call(kernel, name, grid, in_specs, outs, scratch=(), aliases=None, prefetch=0, flops=0, size=0,
         limit=VMEM_LIMIT):
    run = pl.pallas_call(
        kernel,
        grid_spec=pltpu.PrefetchScalarGridSpec(
            num_scalar_prefetch=prefetch,
            grid=grid,
            in_specs=in_specs,
            out_specs=[spec for _, _, spec in outs],
            scratch_shapes=list(scratch),
        ),
        out_shape=[space_of(spec)(shape, dtype) for shape, dtype, spec in outs],
        input_output_aliases=aliases or {},
        compiler_params=pltpu.CompilerParams(
            dimension_semantics=("arbitrary",) * len(grid), vmem_limit_bytes=limit
        ),
        cost_estimate=pl.CostEstimate(flops=flops, bytes_accessed=size, transcendentals=0),
        name=name,
    )

    def placed(array, spec):
        return pltpu.with_memory_space_constraint(array, space_of(spec))

    def with_places(*args):
        arrays = [placed(a, spec) for a, spec in zip(args[prefetch:], in_specs)]
        return run(*args[:prefetch], *arrays)

    return with_places


def onehot_rows(codes_row, entries):
    entry = lax.broadcasted_iota(jnp.int32, (entries, codes_row.shape[1]), 0)
    return jnp.where(entry == codes_row, 1.0, 0.0).astype(BF16)


def row_at(ref, index):
    place = lax.broadcasted_iota(jnp.int32, ref.shape, 0)
    return jnp.sum(jnp.where(place == index, ref[...], 0), axis=0, keepdims=True)


def fold(array):
    rows, lanes = array.shape
    return jnp.sum(array.reshape(rows // 8, 8, lanes), axis=0)


def fold_max(array):
    rows, lanes = array.shape
    return jnp.max(array.reshape(rows // 8, 8, lanes), axis=0)


def sum_kernel(codes_ref, value_ref, send_ref, first_ref, first_count_ref):
    heads, entries, width = first_ref.shape
    slices = entries // HALF
    blocks = value_ref.shape[0] // BLOCK
    ones = jnp.ones((BLOCK, TILE), BF16)
    lines = []
    for h in range(heads):
        total = None
        for b in range(blocks):
            span = slice(b * BLOCK, (b + 1) * BLOCK)
            hot = onehot_rows(codes_ref[h : h + 1, span], entries)
            columns = value_ref[span, h * width : (h + 1) * width]
            part = dot(hot, jnp.concatenate([columns, ones], axis=1))
            if b == 0:
                first_ref[h] = part[:, :width]
                for i in range(entries // TILE):
                    rows = slice(i * TILE, (i + 1) * TILE)
                    first_count_ref[h, :, rows] = part[rows, width:].T[:1]
            total = part if b == 0 else total + part
        for k in range(slices):
            rows = slice(k * HALF, (k + 1) * HALF)
            send_ref[h * slices + k, :HALF, :] = total[rows, :width].astype(BF16)
        for i in range(entries // TILE):
            lines.append(total[i * TILE : (i + 1) * TILE, width:].T[:1])
    lines = jnp.concatenate(lines, axis=0)
    high = jnp.floor(lines * (1.0 / 256.0))
    digits = jnp.concatenate([high, lines - high * 256.0], axis=0).astype(BF16)
    for k in range(heads * slices):
        send_ref[k, HALF:, :] = digits


def own_sums(codes, values, heads, entries):
    width = values.shape[1] // heads
    slices = entries // HALF
    whole = lambda i: (0, 0, 0)
    return call(
        sum_kernel, "own_sums", (1,),
        [
            pl.BlockSpec(codes.shape, lambda i: (0, 0)),
            pl.BlockSpec(values.shape, lambda i: (0, 0)),
        ],
        [
            ((heads * slices, ROWS, TILE), BF16, pl.BlockSpec((heads * slices, ROWS, TILE), whole)),
            ((heads, entries, width), F32, pl.BlockSpec((heads, entries, width), whole)),
            ((heads, 1, entries), F32, pl.BlockSpec((heads, 1, entries), whole)),
        ],

    )(codes, values)


def prefix_kernel(me_ref, in_ref, first_ref, out_ref, count_ref):
    running = jnp.zeros(out_ref.shape[1:], F32)
    lines = (ROWS - HALF) // 2
    number = jnp.zeros((lines, TILE), F32)
    for d in range(in_ref.shape[0]):
        out_ref[d] = running.astype(BF16)
        running = running + in_ref[d, :HALF, :].astype(F32)
        digits = in_ref[d, HALF:, :].astype(F32)
        digits = digits[:lines] * 256.0 + digits[lines:]
        number = number + jnp.where(d < me_ref[0], digits, 0.0)
    heads = first_ref.shape[0]
    per = lines // heads
    for h in range(heads):
        for i in range(per):
            line = number[h * per + i : h * per + i + 1]
            columns = slice(i * TILE, (i + 1) * TILE)
            count_ref[0, h, :, columns] = line
            count_ref[1, h, :, columns] = line + first_ref[h, :, columns]


def prefix_scan(me, pieces, first):
    count = pieces.shape[0]
    heads, _, entries = first.shape
    whole = lambda i, *_: (0, 0, 0)
    shape = (2, heads, 1, entries)
    return call(
        prefix_kernel, "prefix_scan", (1,),
        [IN_VMEM, pl.BlockSpec(first.shape, whole)],
        [
            ((count, HALF, TILE), BF16, pl.BlockSpec((count, HALF, TILE), whole)),
            (shape, F32, pl.BlockSpec(shape, lambda i, *_: (0, 0, 0, 0))),
        ],
        prefetch=1
    )(me, pieces, first)


def suffix_kernel(in_ref, out_ref):
    running = jnp.zeros((HALF, TILE), F32)
    total = jnp.zeros((HALF, TILE), F32)
    for d in reversed(range(in_ref.shape[0])):
        out_ref[d, :HALF, :] = running.astype(BF16)
        running = running + in_ref[d, :HALF, :].astype(F32)
        total = total + in_ref[d, HALF:, :].astype(F32)
    low = total.astype(BF16)
    for d in range(in_ref.shape[0]):
        out_ref[d, HALF:, :] = low


def suffix_scan(pieces):
    spec = pl.BlockSpec(pieces.shape, lambda i: (0, 0, 0))
    return call(
        suffix_kernel, "suffix_scan", (1,), [IN_VMEM], [(pieces.shape, BF16, spec)], size=2 << 20
    )(pieces)[0]


def count_columns(number):
    tiles = [
        jnp.broadcast_to(number[:, i * TILE : (i + 1) * TILE], (TILE, TILE)).T
        for i in range(number.shape[1] // TILE)
    ]
    return jnp.concatenate(tiles, axis=0)


def forward_kernel(codes_ref, query_ref, book_ref, count_ref,
                   low_ref, keys_ref, book_t_ref, rows_k, counts, scores):
    entries, width = book_ref.shape[1:]
    head = pl.program_id(0)
    entry_tiles = entries // TILE
    factor = width ** -0.5 * math.log2(math.e)
    causal = lax.broadcasted_iota(jnp.int32, (TILE, TILE), 1) >= lax.broadcasted_iota(
        jnp.int32, (TILE, TILE), 0
    )
    parts = BLOCK // PART
    blocks = low_ref.shape[0]

    codes_row = row_at(codes_ref, head)
    book_t_ref[0] = book_ref[0].astype(F32).T.astype(BF16)

    def prepare(b):
        keys_t = dot(
            book_t_ref[0], onehot_rows(codes_row[:, b * BLOCK : (b + 1) * BLOCK], entries)
        )
        keys_ref[b, 0] = keys_t.astype(BF16)
        rows_k[b, :entries, :] = book_ref[0]
        rows_k[b, entries:, :] = keys_t.T.astype(BF16)
        counts[b] = count_columns(count_ref[b, 0])

    def multiply(b, n):
        used = entries + PART * (n + 1)
        at = b * BLOCK + n * PART
        scores[b, n, :used, :] = dot_nt(rows_k[b, :used, :], query_ref[at : at + PART, :])

    def soften(b, n):
        used = entries + PART * (n + 1)
        for j in range(PART // TILE):
            columns = slice(j * TILE, (j + 1) * TILE)
            target = slice(n * PART + j * TILE, n * PART + (j + 1) * TILE)
            pieces = range(entry_tiles + 2 * n + j + 1)
            top = jnp.full((8, TILE), -jnp.inf, F32)
            for i in pieces:
                rows = slice(i * TILE, (i + 1) * TILE)
                piece = scores[b, n, rows, columns]
                if i < entry_tiles:
                    piece = jnp.where(counts[b, rows, :] > 0.0, piece, -jnp.inf)
                    scores[b, n, rows, columns] = piece
                elif i == pieces[-1]:
                    piece = jnp.where(causal, piece, -jnp.inf)
                    scores[b, n, rows, columns] = piece
                top = jnp.maximum(top, fold_max(piece))
            top = jnp.max(top, axis=0, keepdims=True)
            total = jnp.zeros((8, TILE), F32)
            for i in pieces:
                rows = slice(i * TILE, (i + 1) * TILE)
                piece = jnp.exp2((scores[b, n, rows, columns] - top) * factor)
                scores[b, n, rows, columns] = piece
                if i < entry_tiles:
                    piece = piece * counts[b, rows, :]
                total = total + fold(piece)
            inverse = 1.0 / jnp.sum(total, axis=0, keepdims=True)
            for i in pieces:
                rows = slice(i * TILE, (i + 1) * TILE)
                low_ref[b, 0, rows, target] = (scores[b, n, rows, columns] * inverse).astype(BF16)
            if j == 0:
                low_ref[b, 0, used - TILE : used, target] = jnp.zeros((TILE, TILE), BF16)

    order = [(b, n) for b in range(blocks) for n in range(parts)]
    for b in range(blocks):
        prepare(b)
    multiply(*order[0])
    for k, item in enumerate(order):
        if k + 1 < len(order):
            multiply(*order[k + 1])
        soften(*item)


def forward(codes, queries, book, counts):
    heads, entries, width = book.shape
    tokens = queries.shape[0]
    blocks = tokens // BLOCK
    both = entries + BLOCK
    by_head = lambda h: (h, 0, 0)
    in_blocks = lambda h: (0, h, 0, 0)
    return call(
        forward_kernel, "forward", (heads,),
        [
            pl.BlockSpec(codes.shape, lambda h: (0, 0)),
            pl.BlockSpec((tokens, width), lambda h: (0, h)),
            pl.BlockSpec((1, entries, width), by_head),
            pl.BlockSpec((blocks, 1, 1, entries), in_blocks),
        ],
        [
            ((blocks, heads, both, BLOCK), BF16, pl.BlockSpec((blocks, 1, both, BLOCK), in_blocks)),
            ((blocks, heads, width, BLOCK), BF16, pl.BlockSpec((blocks, 1, width, BLOCK), in_blocks)),
            ((heads, width, entries), BF16, pl.BlockSpec((1, width, entries), by_head)),
        ],
        [
            pltpu.VMEM((blocks, both, width), BF16),
            pltpu.VMEM((blocks, entries, TILE), F32),
            pltpu.VMEM((blocks, 2, both, PART), F32),
        ],

    )(codes, queries, book, counts)


def backward_kernel(me_ref, core_ref, own_ref, left_ref, right_ref, far0_ref, far1_ref, weight_ref,
                    codes_ref, query_ref, value_ref, probs_ref, keys_ref, book_t_ref,
                    prefix_ref, count_ref, first_ref,
                    grad_query_ref, local_ref, part_ref, give_ref, keep_ref,
                    dout, hot, rows_v, counts, grads, score_grad, key_grad, wide_t):
    width, entries = book_t_ref.shape[1:]
    entry_tiles = entries // TILE
    parts = BLOCK // PART
    blocks = probs_ref.shape[0]
    scale = width ** -0.5
    step = pl.program_id(0)
    head = lax.rem(step + 2 - 2 * core_ref[0], 4)

    def chunk(offset):
        columns = own_ref.shape[1]
        at = lax.rem(me_ref[0] + offset, 4) * columns
        return weight_ref[:, pl.ds(pl.multiple_of(at, columns), columns)]

    codes_row = row_at(codes_ref, head)

    def prepare(b):
        hot[b] = onehot_rows(codes_row[:, b * BLOCK : (b + 1) * BLOCK], entries)
        wide_t[b, :, :entries] = book_t_ref[0]
        wide_t[b, :, entries:] = keys_ref[b, 0]
        slices = entries // HALF
        sums = prefix_ref[pl.ds(head * slices, slices)].reshape(entries, width)
        if b > 0:
            sums = (sums.astype(F32) + first_ref[0]).astype(BF16)
        rows_v[b, :entries, :] = sums
        rows_v[b, entries:, :] = value_ref[b * BLOCK : (b + 1) * BLOCK, :]
        counts[b] = count_columns(count_ref[b, 0])

    def multiply(b, n):
        used = entries + PART * (n + 1)
        at = b * BLOCK + n * PART
        grads[b, n, :used, :] = dot_nt(rows_v[b, :used, :], dout[head, at : at + PART, :])

    def combine(b, n):
        used = entries + PART * (n + 1)
        for j in range(PART // TILE):
            columns = slice(j * TILE, (j + 1) * TILE)
            source = slice(n * PART + j * TILE, n * PART + (j + 1) * TILE)
            pieces = range(entry_tiles + 2 * n + j + 1)
            delta = jnp.zeros((8, TILE), F32)
            for i in pieces:
                rows = slice(i * TILE, (i + 1) * TILE)
                delta = delta + fold(
                    probs_ref[b, 0, rows, source].astype(F32) * grads[b, n, rows, columns]
                )
            delta = jnp.sum(delta, axis=0, keepdims=True)
            for i in pieces:
                rows = slice(i * TILE, (i + 1) * TILE)
                shift = delta
                if i < entry_tiles:
                    shift = delta * counts[b, rows, :]
                piece = grads[b, n, rows, columns] - shift
                piece = probs_ref[b, 0, rows, source].astype(F32) * piece
                score_grad[b, n, rows, columns] = piece.astype(BF16)
            if j == 0:
                score_grad[b, n, used - TILE : used, columns] = jnp.zeros((TILE, TILE), BF16)

    sums_k = [[None] * parts for _ in range(blocks)]
    sums_v = [[None] * parts for _ in range(blocks)]

    def outputs(b, n):
        used = entries + PART * (n + 1)
        at = b * BLOCK + n * PART
        span = slice(at, at + PART)
        sums_v[b][n] = dot(probs_ref[b, 0, :used, n * PART : (n + 1) * PART], dout[head, span, :])
        sums_k[b][n] = dot(score_grad[b, n, :used, :], query_ref[span, :]) * scale
        grad_t = dot(wide_t[b, :, :used], score_grad[b, n, :used, :])
        grad_query_ref[span, :] = (grad_t * scale).T.astype(BF16)

    order = [(b, n) for b in range(blocks) for n in range(parts)]
    for b in range(blocks):
        prepare(b)

    @pl.when(step == 0)
    def _():
        count = own_ref.shape[0] // PART
        for n in range(count):
            span = slice(n * PART, (n + 1) * PART)
            total = dot_nt(own_ref[span, :], chunk(0)) + dot_nt(left_ref[span, :], chunk(3))
            total = total + dot_nt(right_ref[span, :], chunk(1))
            if n < count // 2:
                far = far0_ref[span, :]
            else:
                far = far1_ref[(n - count // 2) * PART : (n + 1 - count // 2) * PART, :]
            total = total + dot_nt(far, chunk(2))
            for h in range(dout.shape[0]):
                dout[h, span, :] = total[:, h * width : (h + 1) * width].astype(BF16)

    multiply(*order[0])
    code = None
    part = None
    middle = entries + PART
    for k, item in enumerate(order):
        if k + 1 < len(order):
            multiply(*order[k + 1])
        combine(*item)
        outputs(*item)
        b, n = item
        if n == parts - 1:
            first, last = sums_v[b]
            at = b * BLOCK
            local_ref[at : at + PART, :] = first[entries:] + last[entries:middle]
            local_ref[at + PART : at + BLOCK, :] = last[middle:]
            mine = first[:entries] + last[:entries]
            if b == blocks - 1:
                part_ref[0] = mine
            part = mine if b == 0 else part + mine
            first, last = sums_k[b]
            key_grad[b, :PART, :] = (first[entries:] + last[entries:middle]).astype(BF16)
            key_grad[b, PART:, :] = last[middle:].astype(BF16)
            mine = first[:entries] + last[:entries] + dot(hot[b], key_grad[b])
            code = mine if b == 0 else code + mine

    def write(ref):
        for k in range(entries // HALF):
            rows = slice(k * HALF, (k + 1) * HALF)
            at = lax.rem(step, 2) * (entries // HALF) + k
            ref[at, :HALF, :] = part[rows].astype(BF16)
            ref[at, HALF:, :] = code[rows].astype(BF16)

    @pl.when(step < 2)
    def _():
        write(give_ref)

    @pl.when(step >= 2)
    def _():
        write(keep_ref)


def backward(me, core, pieces, weight, codes, queries, values, probs, keys, book_t, prefix, counts,
             first):
    heads, width, entries = book_t.shape
    tokens = queries.shape[0]
    blocks = tokens // BLOCK
    both = entries + BLOCK
    slices = entries // HALF
    at = lambda s, core: lax.rem(s + 2 - 2 * core[0], 4)
    by_head = lambda s, _, core: (at(s, core), 0, 0)
    in_blocks = lambda s, _, core: (0, at(s, core), 0, 0)
    rows_of = pl.BlockSpec((tokens, width), lambda s, _, core: (0, at(s, core)))
    both_heads = (2 * slices, 2 * HALF, width)
    per_head = pl.BlockSpec((1, entries, width), by_head)

    anywhere = pl.BlockSpec(memory_space=pl.ANY)
    whole = lambda s, *_: (0, 0)
    in_specs = [pl.BlockSpec(pieces[0].shape, whole), IN_VMEM, IN_VMEM]
    in_specs += [pl.BlockSpec(piece.shape, whole) for piece in pieces[3:]]
    in_specs.append(pl.BlockSpec(weight.shape, whole))
    in_specs += [
        pl.BlockSpec(codes.shape, lambda h, *_: (0, 0)),
        rows_of,
        rows_of,
        pl.BlockSpec((blocks, 1, both, BLOCK), in_blocks),
        pl.BlockSpec((blocks, 1, width, BLOCK), in_blocks),
        pl.BlockSpec((1, width, entries), by_head),
        IN_VMEM,
        pl.BlockSpec((blocks, 1, 1, entries), in_blocks),
        per_head,
    ]
    outs = [
        (queries.shape, BF16, rows_of),
        (queries.shape, F32, rows_of),
        ((heads, entries, width), F32, per_head),
        (both_heads, BF16, IN_VMEM),
        (both_heads, BF16, IN_VMEM),
    ]
    return call(
        backward_kernel, "backward", (heads,), in_specs, outs,
        [
            pltpu.VMEM((heads, tokens, width), BF16),
            pltpu.VMEM((blocks, entries, BLOCK), BF16),
            pltpu.VMEM((blocks, both, width), BF16),
            pltpu.VMEM((blocks, entries, TILE), F32),
            pltpu.VMEM((blocks, 2, both, PART), F32),
            pltpu.VMEM((blocks, 2, both, PART), BF16),
            pltpu.VMEM((blocks, BLOCK, width), BF16),
            pltpu.VMEM((blocks, width, both), BF16),
        ],
        prefetch=2, flops=20 << 30, size=24 << 20,
    )(me, core, *pieces, weight, codes, queries, values, probs, keys, book_t, prefix, counts,
      first)


def finish_kernel(own, refs):
    me_ref, codes_ref, local_ref, later_ref = refs[:4]
    if own:
        kept_ref, part_ref = refs[4:6]
    else:
        part_ref = refs[4]
    out_ref, book_ref = refs[-2:]
    entries, width = part_ref.shape[1:]
    step = pl.program_id(0)
    head = 2 * me_ref[0] + step if own else 2 - 2 * me_ref[0] + step
    codes_row = row_at(codes_ref, head)
    mine = pl.ds(step * (entries // HALF), entries // HALF)
    later = later_ref[mine, :HALF, :].astype(F32)
    if own:
        later = later + jnp.where(me_ref[0] == 0, kept_ref[mine, :HALF, :].astype(F32), 0.0)
    later = later.reshape(entries, width)
    book_ref[0] = later_ref[mine, HALF:, :].reshape(entries, width).astype(F32)
    tokens = local_ref.shape[0]
    tables = [later.astype(BF16)] * (tokens // BLOCK)
    tables[0] = (later + part_ref[0]).astype(BF16)
    levels = lax.broadcasted_iota(jnp.int32, (TILE, TILE), 1)
    for i in range(tokens // TILE):
        rows = slice(i * TILE, (i + 1) * TILE)
        column = jnp.broadcast_to(codes_row[:, rows], (TILE, TILE)).T
        hot = jnp.concatenate(
            [
                jnp.where(levels + k * TILE == column, 1.0, 0.0).astype(BF16)
                for k in range(entries // TILE)
            ],
            axis=1,
        )
        out_ref[rows, :] = (local_ref[rows, :] + dot(hot, tables[i * TILE // BLOCK])).astype(BF16)


def finish(own, core, codes, local, later, part, extra):
    heads, entries, width = part.shape
    tokens = local.shape[0]
    at = lambda s, core: (2 * core[0] if own else 2 - 2 * core[0]) + s
    by_head = lambda s, core: (at(s, core), 0, 0)
    rows_of = pl.BlockSpec((tokens, width), lambda s, core: (0, at(s, core)))
    per_head = pl.BlockSpec((1, entries, width), by_head)
    in_specs = [pl.BlockSpec(codes.shape, lambda s, *_: (0, 0)), rows_of, IN_VMEM]
    if own:
        in_specs += [IN_VMEM, per_head]
        args = (*extra, part)
    else:
        in_specs += [per_head] + [pl.BlockSpec(memory_space=pl.ANY)] * 2
        args = (part, *extra)
    return call(
        lambda *refs: finish_kernel(own, refs), "finish_own" if own else "finish_other", (2,),
        in_specs,
        [(local.shape, BF16, rows_of), (part.shape, F32, per_head)],
        aliases=None if own else {5: 0, 6: 1}, prefetch=1, flops=1 << 30, size=8 << 20,
    )(core, codes, local, later, *args)


def ring_pieces(array):
    count = lax.axis_size("head")
    up = [(i, (i + 1) % count) for i in range(count)]
    down = [(i, (i - 1) % count) for i in range(count)]
    left = lax.ppermute(array, "head", up)
    right = lax.ppermute(array, "head", down)
    half = array.shape[0] // 2
    far = lax.ppermute(left[:half], "head", up), lax.ppermute(right[half:], "head", down)
    return array, left, right, *far


def per_device(queries, values, codes, codebook, out_weight, grad_out):
    heads, entries, width = codebook.shape
    exchange = functools.partial(
        lax.all_to_all, axis_name=("chip", "core"), split_axis=0, concat_axis=0, tiled=True
    )
    between_chips = functools.partial(
        lax.all_to_all, axis_name="chip", split_axis=0, concat_axis=0, tiled=True
    )
    other_core = functools.partial(lax.ppermute, axis_name="core", perm=[(0, 1), (1, 0)])
    core = lax.axis_index("core").astype(jnp.int32)
    me_seq = lax.axis_index(("chip", "core")).astype(jnp.int32).reshape(1)
    me = lax.axis_index("head").astype(jnp.int32).reshape(1)
    core_at = core.reshape(1)
    pieces = ring_pieces(grad_out)
    codes = codes.T
    send, first, first_count = own_sums(codes, values, heads, entries)
    prefix, counts = prefix_scan(me_seq, exchange(send), first_count)
    prefix = exchange(prefix)
    probs, keys, book_t = forward(codes, queries, codebook, counts)
    grad_query, local, part, give, keep = backward(
        me, core_at, pieces, out_weight, codes, queries, values, probs, keys, book_t, prefix, counts, first
    )
    got = other_core(give)
    chip = (keep.astype(F32) + got.astype(F32)).astype(BF16)
    later = between_chips(suffix_scan(between_chips(chip)))
    is_value = lax.broadcasted_iota(jnp.int32, later.shape, 1) < HALF
    mine = jnp.where(is_value & (core == 1), keep.astype(F32), 0.0)
    theirs = other_core((later.astype(F32) + mine).astype(BF16))
    results = finish(True, core_at, codes, local, later, part, (got,))
    grad_values, grad_book = finish(False, core_at, codes, local, theirs, part, results)
    return grad_query, grad_values, grad_book


def solution(mesh):
    finer = Mesh(mesh.devices.reshape(-1, 2, mesh.shape["head"]), ("chip", "core", "head"))
    rows = P(("chip", "core"), "head")
    return jax.shard_map(
        per_device,
        mesh=finer,
        in_specs=(rows, rows, rows, P("head", None, None), P("head", None), rows),
        out_specs=(rows, rows, P("head", None, None)),
        check_vma=False,
    )
```
